32 devices in a mesh: band: 2 (over core), grid: 16 (over z, y, x).
Axes of the slice: x: 2, y: 2, z: 4, core: 2. Of those that a mesh axis runs over, the one named last changes fastest.
Arguments:
- coefficients: float32 [4, 2, 128, 128, 128], P('band', None, 'grid'), may hold values from -0.01171875 to 0.01171875
- potential: float32 [128, 128, 128], P('grid'), may hold values from -3 to 3
- external: float32 [128, 128, 128], P('grid'), may hold values from -6 to 6
- core_density: float32 [128, 128, 128], P('grid'), may hold values from 0.05 to 0.5
- rotations: float32 [2, 4, 2], P(None, 'band'), may hold values from -2 to 3
- mlp_in: float32 [3, 32], replicated, may hold values from -4 to 4
- mlp_out: float32 [32], replicated, may hold values from -0.4 to 0.4
Outputs:
- new_coefficients: float32 [4, 2, 128, 128, 128], P('band', None, 'grid')
- new_potential: float32 [128, 128, 128], P('grid')
The draws below stay inside these ranges and needn't reach their ends.
All inputs are finite; a program needn't handle non-finite values.
Results may differ from the reference program's by a relative error of at most 0.0003.
Values sent between devices are 32-bit elements; how exact they have to be, the bound alone decides.
A program may use at most 64 MiB of HBM per device.

```python
import math
import jax
import jax.numpy as jnp
from jax import lax

NX = 128
NY = 128
NZ = 128
BLOC = 2
ITERS = 2
NH = 32
BANDS = 4
N_BAND = 2


def draw_rotations(key, part):
    jitter = jax.random.truncated_normal(key, -3.0, 3.0, (ITERS, BANDS, BLOC), jnp.float32)
    band_rows = lax.iota(jnp.int32, BANDS) % BLOC
    diagonal = (band_rows[:, None] == lax.iota(jnp.int32, BLOC)[None, :]).astype(jnp.float32)
    return diagonal[None] + 0.5 * jitter / math.sqrt(BLOC)


def block_scale(key, extent, pieces, low, high):
    gain = 1.0
    for position, shards_of in pieces:
        steps = jax.random.uniform(jax.random.fold_in(jax.random.fold_in(key, 6), position), (shards_of,), jnp.float32, low / len(pieces), high / len(pieces))
        gain = gain * jnp.repeat(jnp.exp(steps), extent[position] // shards_of).reshape((-1,) + (1,) * (len(extent) - 1 - position))
    return gain


def gaussian(stream_key, dims, scale, reach, pieces=(), kind=jnp.bfloat16):
    loudness = block_scale(stream_key, dims, pieces, -0.22, 0.18) if pieces else 1.0
    result = jax.random.normal(stream_key, dims, jnp.float32) * scale * loudness
    return jnp.minimum(jnp.maximum(result, -reach), reach).astype(kind)


def setup_inputs(seed: int = 0) -> dict:
    splits = jax.random.split(jax.random.key(seed), 8)
    coefficients = gaussian(splits[0], (BANDS, 2, NX, NY, NZ), (NX * NY * NZ // 8) ** -0.5, 0.01171875, ((0, 2), (2, 16)), jnp.float32)
    potential = gaussian(splits[1], (NY, NX, NZ), 0.5, 3.0, ((0, 16),), jnp.float32)
    external = gaussian(splits[2], (NY, NX, NZ), 1.0, 6.0, ((0, 16),), jnp.float32)
    core_density = jnp.clip(jnp.exp(math.log(0.5) - 2.3025851 * jax.random.uniform(splits[3], (NY, NX, NZ), jnp.float32) ** block_scale(splits[3], (NY, NX, NZ), ((0, 16),), -0.2, 0.2)), 0.05, 0.5)
    rotations = draw_rotations(jax.random.fold_in(splits[7], 71), 0)
    mlp_in = gaussian(splits[5], (3, NH), 1.0, 4.0, (), jnp.float32)
    mlp_out = gaussian(splits[6], (NH,), 0.1, 0.4, (), jnp.float32)
    return dict(coefficients=coefficients, potential=potential, external=external, core_density=core_density, rotations=rotations, mlp_in=mlp_in, mlp_out=mlp_out)


step_size = 0.2
epsilon = 1e-06
spacing = 0.58
kinetic_scale = 0.5 * (2.0 * math.pi / spacing) ** 2
coulomb_scale = spacing * spacing / math.pi
gradient_scale = 2.0 * math.pi / spacing
reduced_scale = 2.0 * (3.0 * math.pi * math.pi) ** (1.0 / 3.0)
exchange_scale = (3.0 / math.pi) ** (1.0 / 3.0)

def frequencies(points, offset, length):
    places = offset + lax.iota(jnp.int32, length)
    return jnp.where(2 * places < points, places, places - points)

def without_nyquist(values, points):
    return jnp.where(2 * values == -points, 0, values)

def reciprocal_tables(offset, length):
    along_x = frequencies(NX, offset, length)
    along_y = frequencies(NY, 0, NY)
    raw_z = frequencies(NZ, 0, NZ)
    along_z = raw_z * (NX // NZ)
    squared = along_x[:, None, None] * along_x[:, None, None] + along_y[None, :, None] * along_y[None, :, None] + along_z[None, None, :] * along_z[None, None, :]
    cutoff = (16 * squared <= NX * NX).astype(jnp.float32)
    kinetic = kinetic_scale * squared.astype(jnp.float32) / (NX * NX)
    coulomb = jnp.where(squared > 0, coulomb_scale * (NX * NX) / jnp.maximum(squared, 1).astype(jnp.float32), 0.0).astype(jnp.float32)
    slope_x = gradient_scale * without_nyquist(along_x, NX).astype(jnp.float32) / NX
    slope_y = gradient_scale * without_nyquist(along_y, NY).astype(jnp.float32) / NX
    slope_z = gradient_scale * (without_nyquist(raw_z, NZ) * (NX // NZ)).astype(jnp.float32) / NX
    return (cutoff, kinetic, coulomb, slope_x[:, None, None], slope_y[None, :, None], slope_z[None, None, :])

def toward_position_grid(spectral_amplitude):
    wave = spectral_amplitude[:, 0] + 1j * spectral_amplitude[:, 1]
    position_grid_values = jnp.fft.ifftn(wave, axes=(1, 2, 3)) * (NX * NY * NZ)
    position_grid_values = jnp.transpose(position_grid_values, (0, 2, 1, 3))
    return jnp.stack([position_grid_values.real, position_grid_values.imag], 1)

def toward_spectral_amplitudes(position_grid_values):
    wave = position_grid_values[:, 0] + 1j * position_grid_values[:, 1]
    wave = jnp.transpose(wave, (0, 2, 1, 3))
    spectral_amplitude = jnp.fft.fftn(wave, axes=(1, 2, 3)) / (NX * NY * NZ)
    return jnp.stack([spectral_amplitude.real, spectral_amplitude.imag], 1)

def refine_group(spectral_amplitude, rotation, potential, cutoff, kinetic):
    highest = lax.Precision.HIGHEST
    current = cutoff * spectral_amplitude
    for iteration in range(ITERS):
        applied = cutoff * (kinetic * current + toward_spectral_amplitudes(toward_position_grid(current) * potential))
        intersection = lax.optimization_barrier(jnp.sum(current * current, axis=(1, 2, 3, 4)))
        energy = lax.optimization_barrier(jnp.sum(current * applied, axis=(1, 2, 3, 4)))
        factor = 1.0 + step_size * (energy / (intersection + epsilon))
        updated = factor[:, None, None, None, None] * current - step_size * applied
        updated = jnp.einsum('ij,jcxyz->icxyz', rotation[iteration], updated, precision=highest)
        length = lax.optimization_barrier(jnp.sum(updated * updated, axis=(1, 2, 3, 4)))
        current = updated / jnp.sqrt(length + epsilon)[:, None, None, None, None]
    real_space = toward_position_grid(current)
    partial_value = 2.0 / BANDS * lax.optimization_barrier(jnp.sum(real_space * real_space, axis=(0, 1)))
    return (current, partial_value)

def reference(coefficients, potential, external, core_density, rotations, mlp_in, mlp_out):
    highest = lax.Precision.HIGHEST
    cutoff, kinetic, coulomb, slope_x, slope_y, slope_z = reciprocal_tables(0, NX)
    groups = coefficients.reshape(N_BAND, BLOC, 2, NX, NY, NZ)
    turns = jnp.transpose(rotations.reshape(ITERS, N_BAND, BLOC, BLOC), (1, 0, 2, 3))

    def one_group(group_pair):
        return refine_group(group_pair[0], group_pair[1], potential, cutoff, kinetic)
    refined, partials = lax.map(one_group, (groups, turns))
    density = lax.optimization_barrier(jnp.sum(partials, axis=0)) + core_density
    spectrum = toward_spectral_amplitudes(jnp.stack([density, jnp.zeros_like(density)])[None])[0]
    spec_real = spectrum[0]
    spec_imag = spectrum[1]
    first_real = coulomb * spec_real - slope_x * spec_real
    first_imag = coulomb * spec_imag - slope_x * spec_imag
    second_real = -slope_y * spec_imag - slope_z * spec_real
    second_imag = slope_y * spec_real - slope_z * spec_imag
    fields = toward_position_grid(jnp.stack([jnp.stack([first_real, first_imag]), jnp.stack([second_real, second_imag])]))
    hartree = fields[0, 0]
    change_x = fields[0, 1]
    change_y = fields[1, 0]
    change_z = fields[1, 1]
    cube_root = jnp.cbrt(density)
    gradient = jnp.sqrt(change_x * change_x + change_y * change_y + change_z * change_z)
    reduced = gradient / (reduced_scale * density * cube_root)
    bounded = reduced / (1.0 + reduced)
    hidden = jnp.tanh(mlp_in[0][:, None, None, None] * cube_root + mlp_in[1][:, None, None, None] * bounded + mlp_in[2][:, None, None, None])
    enhance = 1.0 + jnp.einsum('k,kyxz->yxz', mlp_out, hidden, precision=highest)
    new_potential = external + hartree - exchange_scale * cube_root * enhance
    return (refined.reshape(BANDS, 2, NX, NY, NZ), new_potential)
```

```python
import functools
import math

import jax
import jax.numpy as jnp
import numpy as np
from jax import lax
from jax.experimental import pallas as pl
from jax.experimental.pallas import tpu as pltpu
from jax.sharding import PartitionSpec as P

MESH = pl.DeviceIdType.MESH
F32 = jnp.float32
BF16 = jnp.bfloat16
HIGHEST = lax.Precision.HIGHEST

step_size = 0.2
epsilon = 1e-06
spacing = 0.58
kinetic_scale = 0.5 * (2.0 * math.pi / spacing) ** 2
coulomb_scale = spacing * spacing / math.pi
gradient_scale = 2.0 * math.pi / spacing
reduced_scale = 2.0 * (3.0 * math.pi * math.pi) ** (1.0 / 3.0)
exchange_scale = (3.0 / math.pi) ** (1.0 / 3.0)
level_shift = 2.275


def halves(table):
    table = np.asarray(table, np.float32)
    high = table.astype(BF16)
    low = (table - high.astype(np.float32)).astype(BF16)
    return high, low


def table_for_left(table):
    high, low = halves(table)
    return np.concatenate([high, high, low], 1)


def table_for_right(table):
    high, low = halves(table)
    return np.concatenate([high, high, low], 0)


def split(value):
    high = value.astype(BF16)
    return high, (value - high.astype(F32)).astype(BF16)


def dot(a, b):
    return jnp.dot(a, b, preferred_element_type=F32)


def left(table, value):
    high, low = split(value)
    return dot(table, jnp.concatenate([high, low, high], 0))


def right(value, table):
    high, low = split(value)
    return dot(jnp.concatenate([high, low, high], 1), table)


def full_dot(a, b):
    return jnp.dot(a, b, preferred_element_type=F32, precision=HIGHEST)


def slot_planes(n, points):
    planes, slots = points // n, points // 2 // n
    found = []
    for device in range(n):
        quarter = device // (n // 4)
        owner = device + (0, -(n // 4), n // 4, 0)[quarter]
        start = owner * planes + (0, slots, slots, 0)[quarter]
        found += [start + i for i in range(slots)]
    return np.array(found)


def cell_order(count, share):
    return np.array([o * share + k for k in range(share) for o in range(count)])


def transform_tables(n, points, count, share):
    half = points // 2
    keep = np.arange(half)
    keep = np.where(keep < half // 2, keep, keep - half)
    cell = np.arange(points)

    def waves(freq):
        angle = 2.0 * np.pi * ((freq[:, None] * cell[None, :]) % points) / points
        return np.cos(angle), np.sin(angle)

    cos, sin = waves(keep)
    plane = slot_planes(n, points)
    cos_x, sin_x = waves(np.where(2 * plane < points, plane, plane - points))
    freq = np.where(2 * cell < points, cell, cell - points)
    slope = gradient_scale * np.where(2 * freq == -points, 0, freq) / points
    cos_all, sin_all = waves(cell)
    derivative = ((cos_all + 1j * sin_all) * slope[None, :] * 1j) @ (cos_all - 1j * sin_all) / points
    derivative = derivative.real
    basis = cos_all + sin_all
    order = cell_order(count, share)
    lefts = np.stack([
        table_for_left(t) for t in (
            np.concatenate([cos.T, sin.T], 1),
            np.concatenate([cos, sin], 0),
            np.concatenate([cos_x.T, sin_x.T], 1),
            np.concatenate([cos_x, sin_x], 0),
            basis[order],
            derivative[order][:, order],
            basis[:, order],
            derivative,
        )
    ])
    rights = np.concatenate([table_for_right(basis), table_for_right(derivative.T)], 1)
    z_out = table_for_right(np.block([[cos, sin], [-sin, cos]]))
    z_in = table_for_right(np.block([[cos.T, -sin.T], [sin.T, cos.T]]))
    plain = np.stack([basis, basis[:, order]]).astype(np.float32)
    return lefts, rights, z_out, z_in, plain


def kernel(
    n, peers, bands, points, iters, hidden,
    coefficients, potential_in, external_in, core_in, rotations, mlp_in, mlp_out,
    lefts, rights, z_out, z_in, plain,
    new_out, out,
    given, potential, external, core, raw, forward, vectors, mask, kinetic,
    sent, got, level_r, level_i, edge_r, edge_i, space_of, fixed_out, fixed_got,
    gram_tile, gram_got, fresh, returned, fixed_new, fixed_back,
    parts, coulomb, staged, arrived, slope_sent, slope_got, wave_sent, wave_got, change, network,
    load_sem, first_sem, fixed_sem, send_sem, recv_sem, gram_sem, last_sem, back_sem, dens_sem, field_sem, own_sem,
    share_sem,
):
    me = lax.axis_index("grid")
    band = lax.axis_index("band")
    half = points // 2
    reach = half // 2
    slots = half // n
    planes = points // n
    zone = n // 4
    home = n - zone
    edge = home * slots
    sub = math.gcd(peers, planes)
    share = planes // sub
    count = n * sub
    block = share * share
    seat = lax.rem(band, sub)
    team = band - seat
    rank = me * sub + seat
    holder = jnp.logical_or(me < zone, me >= home)
    partner = jnp.where(
        me < zone, me + zone, jnp.where(me < 2 * zone, me - zone, jnp.where(me < home, me + zone, me - zone))
    )

    def at(grid, other=None):
        return {"band": band if other is None else other, "grid": grid}

    def remote(source, target, send, recv, device):
        return pltpu.make_async_remote_copy(
            src_ref=source, dst_ref=target, send_sem=send, recv_sem=recv, device_id=device, device_id_type=MESH
        )

    def drained(ref, sem):
        pltpu.make_async_copy(ref, ref, sem).wait()

    loads = []
    for b in range(bands):
        for p in range(2):
            k = 2 * (2 * b + p)
            loads.append(pltpu.make_async_copy(
                coefficients.at[b, p, :, pl.ds(0, reach + 8)], given.at[b, p, :, pl.ds(0, reach + 8)], load_sem.at[k]
            ))
            loads.append(pltpu.make_async_copy(
                coefficients.at[b, p, :, pl.ds(points - reach, reach)],
                given.at[b, p, :, pl.ds(reach + 8, reach)],
                load_sem.at[k + 1],
            ))
    base = 4 * bands
    late = [
        pltpu.make_async_copy(potential_in, potential, load_sem.at[base]),
        pltpu.make_async_copy(external_in, external, load_sem.at[base + 1]),
        pltpu.make_async_copy(core_in, core, load_sem.at[base + 2]),
    ]
    for copy in loads + late:
        copy.start()

    barrier = pltpu.get_barrier_semaphore()

    @pl.loop(1, count)
    def _(i):
        other = lax.rem(rank + i, count)
        pl.semaphore_signal(barrier, inc=1, device_id=at(other // sub, team + lax.rem(other, sub)), device_id_type=MESH)

    for i in range(1, peers):
        other = lax.rem(band + i, peers)

        @pl.when(other - lax.rem(other, sub) != team)
        def _():
            pl.semaphore_signal(barrier, inc=1, device_id=at(me, other), device_id_type=MESH)

    lanes = lax.broadcasted_iota(jnp.int32, (1, points), 1)
    tile_lane = lax.broadcasted_iota(jnp.int32, (8, points), 1)
    tile_row = lax.broadcasted_iota(jnp.int32, (8, points), 0)
    sign = jnp.where(lanes < half, -1.0, 1.0).astype(F32)
    alone = jnp.where(lax.rem(lanes, half) == 0, 1.0, 0.0).astype(F32)

    def quarter_turn(k):
        k = lax.rem(k, 4)
        c = jnp.where(k == 0, 1.0, jnp.where(k == 2, -1.0, 0.0)).astype(F32)
        s = jnp.where(k == 1, 1.0, jnp.where(k == 3, -1.0, 0.0)).astype(F32)
        return c, s

    z_c, z_s = quarter_turn(lanes)
    y_c, y_s = quarter_turn(me * planes + lax.broadcasted_iota(jnp.int32, (planes, 1), 0))

    def turn(value):
        return pltpu.roll(value, half, 1) * sign

    def frequency(place):
        return jnp.where(2 * place < points, place, place - points)

    own_start = jnp.where(holder, me * planes, partner * planes + slots)
    row = lax.broadcasted_iota(jnp.int32, (half, points), 0)
    gy = jnp.where(row < reach, row, row - half)
    lane = lax.rem(lax.broadcasted_iota(jnp.int32, (half, points), 1), half)
    gz = jnp.where(lane < reach, lane, lane - half)
    flat = gy * gy + gz * gz
    for x in range(slots):
        gx = frequency(own_start + x)
        squared = flat + gx * gx
        if x == 0:
            spot = jnp.logical_and(jnp.logical_and(row == 0, lane < 4), me == home)
            squared = jnp.where(spot, reach * reach, squared)
        mask[x] = jnp.where(16 * squared <= points * points, 1.0, 0.0).astype(F32)
        kinetic[x] = kinetic_scale * squared.astype(F32) / (points * points)
    edge_r[...] = jnp.zeros_like(edge_r)
    edge_i[...] = jnp.zeros_like(edge_i)

    for copy in loads:
        copy.wait()

    def packed(b, x):
        found = []
        for p in range(2):
            found.append(jnp.concatenate([given[b, p, x, 0:reach], given[b, p, x, reach + 8 : half + 8]], 0))
        real, imag = found
        low = jnp.where(lanes < reach, real, pltpu.roll(real, half, 1))
        high = jnp.where(lanes < half + reach, pltpu.roll(imag, half, 1), imag)
        return jnp.where(lanes < half, low, high)

    @pl.when(holder)
    def _():
        for b in range(bands):
            for x in range(slots):
                forward[b, x] = packed(b, slots + x)
                raw[b, x] = packed(b, x)

    def lane_to(value, start, target):
        moved = pltpu.roll(value, (target - start) % points, 1)
        return jnp.where(jnp.logical_and(tile_lane == target, tile_row == 0), moved, 0.0)

    @pl.when(me == 0)
    def _():
        for b in range(bands):
            total = None
            for p in range(2):
                z_point = lane_to(given[b, p, 0, 0:8], reach, 2 + half * p)
                y_point = lane_to(given[b, p, 0, reach : reach + 8], 0, 3 + half * p)
                total = z_point + y_point if total is None else total + z_point + y_point
            fixed_out[b] = total

    @pl.when(me == zone)
    def _():
        for b in range(bands):
            fixed_out[b] = lane_to(given[b, 0, 0, 0:8], 0, 1) + lane_to(given[b, 1, 0, 0:8], 0, 1 + half)

    pl.semaphore_wait(barrier, count - 1 + peers - sub)

    def first(b):
        return remote(forward.at[b], raw.at[b], first_sem.at[0, b], first_sem.at[1, b], at(partner))

    def fixed(place):
        return remote(fixed_out, fixed_got.at[place], fixed_sem.at[0], fixed_sem.at[1 + place], at(home))

    @pl.when(holder)
    def _():
        for b in range(bands):
            first(b).start()

    @pl.when(me == 0)
    def _():
        fixed(0).start()

    @pl.when(me == zone)
    def _():
        fixed(1).start()

    def exchange(place):
        def copy(target):
            return remote(
                sent.at[place, target], got.at[place, me], send_sem.at[place], recv_sem.at[place], at(target)
            )

        @pl.loop(1, n)
        def _(i):
            copy(lax.rem(me + i, n)).start()

        pltpu.make_async_copy(sent.at[place, me], got.at[place, me], recv_sem.at[place]).start()

    def received(place):
        drained(got.at[place], recv_sem.at[place])

    def outward(value_of, place):
        stacked = []
        for x in range(slots):
            value = value_of(x)
            stacked.append(jnp.concatenate([value, turn(value)], 0))
        full = left(lefts[0], jnp.concatenate(stacked, 1))
        for x in range(slots):
            sent[place, :, x] = full[:, x * points : (x + 1) * points].reshape(n, planes, points)
        exchange(place)

    def space(place, action):
        levels = right(got[place].reshape(half * planes, points), z_out[...])
        level_r[...] = levels[:, :points]
        level_i[...] = levels[:, points:]
        special = got[place, home, 0]

        def lane_of(k):
            return jnp.broadcast_to(special[:, k : k + 1], (planes, points))

        minus_r, plus_r, z_r, y_r = [lane_of(k) for k in range(4)]
        minus_i, plus_i, z_i, y_i = [lane_of(half + k) for k in range(4)]
        level_r[edge * planes : (edge + 1) * planes, :] = minus_r + plus_r
        level_i[edge * planes : (edge + 1) * planes, :] = minus_i + plus_i
        level_r[0:planes, :] += z_r * z_c - z_i * z_s + y_r * y_c - y_i * y_s
        level_i[0:planes, :] += z_r * z_s + z_i * z_c + y_r * y_s + y_i * y_c
        edge_r[pl.ds(0, planes, stride=8), :] = 2.0 * plus_r
        edge_i[pl.ds(0, planes, stride=8), :] = 2.0 * plus_i

        def without(value, y, extra):
            tile = value[edge : edge + 8] - extra[y * 8 : y * 8 + 8, :]
            return jnp.concatenate([value[:edge], tile, value[edge + 8 :]], 0)

        for y in range(planes):
            real = level_r[pl.ds(y, half, stride=planes), :]
            imag = level_i[pl.ds(y, half, stride=planes), :]
            stacked = jnp.concatenate(
                [
                    jnp.concatenate([real, imag], 1),
                    jnp.concatenate([-without(imag, y, edge_i), without(real, y, edge_r)], 1),
                ],
                0,
            )
            action(y, left(lefts[2], stacked))

    def spectrum(index, place):
        def action(y, wave):
            space_of[index, y] = wave
            field = potential[y]
            product = wave * jnp.concatenate([field, field], 1)
            both = left(lefts[3], product)
            cos_r, cos_i = both[:half, :points], both[:half, points:]
            sin_r, sin_i = both[half:, :points], both[half:, points:]
            level_r[pl.ds(y, half, stride=planes), :] = cos_r + sin_i
            level_i[pl.ds(y, half, stride=planes), :] = cos_i - sin_r
            edge_r[8 * (planes + y) : 8 * (planes + y) + 8, :] = cos_r[edge : edge + 8] - sin_i[edge : edge + 8]
            edge_i[8 * (planes + y) : 8 * (planes + y) + 8, :] = cos_i[edge : edge + 8] + sin_r[edge : edge + 8]

        space(place, action)
        both = jnp.concatenate([level_r[...], level_i[...]], 1)
        sent[place + bands] = right(both, z_in[...]).reshape(n, slots, planes, points)

        def total(value):
            return jnp.sum(value, 1, keepdims=True)

        plus_r = edge_r[pl.ds(8 * planes, planes, stride=8), :]
        plus_i = edge_i[pl.ds(8 * planes, planes, stride=8), :]
        zero_r, zero_i = level_r[0:planes, :], level_i[0:planes, :]
        line_r, line_i = total(zero_r), total(zero_i)
        found = [
            total(plus_r), total(zero_r * z_c + zero_i * z_s), line_r * y_c + line_i * y_s,
            total(plus_i), total(zero_i * z_c - zero_r * z_s), line_i * y_c - line_r * y_s,
        ]
        special = sent[place + bands, home, 0] * alone
        for k, value in enumerate(found):
            special = jnp.where(lanes == (k + 1 if k < 3 else half + k - 2), value, special)
        sent[place + bands, home, 0] = special
        exchange(place + bands)

    def inward(place):
        columns = [got[place, :, x].reshape(points, points) for x in range(slots)]
        both = left(lefts[1], jnp.concatenate(columns, 1))
        found = []
        for x in range(slots):
            part = both[:, x * points : (x + 1) * points]
            found.append(part[:half] - turn(part[half:]))
        return found

    grams = {}

    def measure(p):
        for q in range(p + 1):
            u = vectors[p // bands, p % bands].reshape(slots * half, points)
            v = vectors[q // bands, q % bands].reshape(slots * half, points)
            grams[q, p] = jnp.sum(u * v, 0, keepdims=True)

    for b in range(bands):
        @pl.when(jnp.logical_not(holder))
        def _():
            first(b).wait_recv()

        if b == 0:
            @pl.when(me == home)
            def _():
                fixed(0).wait_recv()
                fixed(1).wait_recv()
                for c in range(bands):
                    fixed_got[0, c] = fixed_got[0, c] + fixed_got[1, c]

        @pl.when(me == home)
        def _():
            clean = jnp.where(tile_row == 0, alone, 1.0)
            raw[b, 0, 0:8, :] = raw[b, 0, 0:8, :] * clean * mask[0, 0:8, :] + fixed_got[0, b]

        vectors[0, b] = raw[b] * mask[...]
        outward(lambda x: vectors[0, b, x], b)

    late[0].wait()
    size = (iters + 1) * bands
    for b in range(bands):
        measure(b)
    for t in range(iters):
        for b in range(bands):
            received(2 * t * bands + b)
            spectrum(t * bands + b, 2 * t * bands + b)
        for b in range(bands):
            place = (2 * t + 1) * bands + b
            received(place)
            found = inward(place)
            for x in range(slots):
                vectors[t + 1, b, x] = mask[x] * (
                    kinetic[x] * vectors[t, b, x] + found[x] * (1.0 / points**3)
                )
            last = (t + 1) * bands + b == size - 1
            if last:
                measure(size - 1)
                tile = jnp.zeros((1, points), F32)
                keys = sorted(grams)
                for k, key in enumerate(keys):
                    tile = jnp.where(lanes == k, jnp.sum(grams[key], 1, keepdims=True), tile)
                gram_tile[...] = tile

                def gram_copy(target):
                    return remote(gram_tile, gram_got.at[me], gram_sem.at[0], gram_sem.at[1], at(target))

                @pl.loop(1, n)
                def _(i):
                    gram_copy(lax.rem(me + i, n)).start()

                pltpu.make_async_copy(gram_tile, gram_got.at[me], gram_sem.at[1]).start()
            outward(lambda x: vectors[t + 1, b, x], (2 * t + 2) * bands + b)
            if not last:
                measure((t + 1) * bands + b)

    drained(gram_got, gram_sem.at[1])
    sums = jnp.sum(gram_got[...], 0)
    gram = {}
    for k, (p, q) in enumerate(keys):
        gram[p, q] = gram[q, p] = sums[:, k : k + 1]

    def product(u, v):
        total = None
        for p, a in enumerate(u):
            inner = None
            for q, c in enumerate(v):
                if a is not None and c is not None:
                    term = c * gram[p, q]
                    inner = term if inner is None else inner + term
            if inner is not None:
                total = a * inner if total is None else total + a * inner
        return total

    def combine(terms):
        result = []
        for p in range(size):
            value = None
            for scale, u in terms:
                if u[p] is not None:
                    value = scale * u[p] if value is None else value + scale * u[p]
            result.append(value)
        return result

    one = jnp.ones((1, 1), F32)
    current = [[one if p == b else None for p in range(size)] for b in range(bands)]
    for t in range(iters):
        moved = []
        for b in range(bands):
            pushed = [None] * bands + current[b][: size - bands]
            factor = 1.0 + step_size * (product(current[b], pushed) / (product(current[b], current[b]) + epsilon))
            moved.append(combine([(factor, current[b]), (-step_size, pushed)]))
        following = []
        for b in range(bands):
            rotated = combine([(rotations[t, b, c], moved[c]) for c in range(bands)])
            scale = lax.rsqrt(jnp.maximum(product(rotated, rotated), 0.0) + epsilon)
            following.append([None if value is None else scale * value for value in rotated])
        current = following

    for b in range(bands):
        for x in range(slots):
            fresh[b, x] = sum(current[b][p] * vectors[p // bands, p % bands, x] for p in range(size))

    place = 2 * iters * bands
    for b in range(bands - 1):
        received(place + b)

        def keep(y, wave):
            space_of[iters * bands + b, y] = wave

        space(place + b, keep)

    for y in range(planes):
        for b in range(bands):
            known = [space_of[p, y] for p in range(size - 1)]
            mixed = [sum(current[b][p] * known[p] for p in range(size - 1)) for b in range(bands)]
        for b in range(bands):
            space_of[b, y] = mixed[b]

    def density_copy(i, y):
        target = lax.rem(band + i, peers)
        return remote(
            parts.at[band, y], parts.at[band, y], dens_sem.at[0, i - 1, y], dens_sem.at[1, i - 1, y], at(me, target)
        )

    received(place + bands - 1)

    def density(y, wave):
        total = None
        for b in range(bands):
            value = space_of[b, y] + current[b][size - 1] * wave
            square = value * value
            square = square[:, :points] + square[:, points:]
            total = square if total is None else total + square
        parts[band, y] = total * (2.0 / (bands * peers))
        for i in range(1, peers):
            @pl.when(lax.rem(lax.rem(band + i, peers), sub) == y // share)
            def _():
                density_copy(i, y).start()

    space(place + bands - 1, density)

    late[2].wait()
    late[1].wait()
    for i in range(1, peers):
        for y in range(planes):
            @pl.when(lax.rem(lax.rem(band + i, peers), sub) == y // share)
            def _():
                density_copy(i, y).wait_send()

            @pl.when(seat == y // share)
            def _():
                density_copy(i, y).wait_recv()

    first_plane = seat * share
    whole = []
    for k in range(share):
        total = core[first_plane + k]
        for other in range(peers):
            total = total + parts[other, first_plane + k]
        whole.append(total)
    varying = [value - level_shift for value in whole]

    def field_exchange(stage, source, target):
        def copy(other):
            return remote(
                source.at[pl.ds(other * block, block)],
                target.at[pl.ds(rank * block, block)],
                field_sem.at[0, stage],
                field_sem.at[1, stage],
                at(other // sub, team + lax.rem(other, sub)),
            )

        @pl.loop(1, count)
        def _(i):
            copy(lax.rem(rank + i, count)).start()

        pltpu.make_async_copy(
            source.at[pl.ds(rank * block, block)], target.at[pl.ds(rank * block, block)], field_sem.at[1, stage]
        ).start()

    level = full_dot(plain[0], jnp.concatenate(varying, 1))
    level = jnp.concatenate([level[:, k * points : (k + 1) * points] for k in range(share)], 0)
    level = full_dot(level, plain[0])
    for k in range(share):
        staged[pl.ds(k, points, stride=share), :] = level[k * points : (k + 1) * points]
    field_exchange(0, staged, arrived)

    def last(b):
        return remote(fresh.at[b], returned.at[b], last_sem.at[0, b], last_sem.at[1, b], at(partner))

    def back(target, sem):
        return remote(fixed_new, fixed_back, back_sem.at[sem], back_sem.at[2], at(target))

    @pl.when(jnp.logical_not(holder))
    def _():
        for b in range(bands):
            last(b).start()

    @pl.when(me == home)
    def _():
        for b in range(bands):
            fixed_new[b] = fresh[b, 0, 0:8, :]
        back(0, 0).start()
        back(zone, 1).start()

    columns = jnp.concatenate(varying, 1)
    change_x = left(lefts[7], columns)
    change_z = right(jnp.concatenate(varying, 0), rights[:, points:])
    for k in range(share):
        cx = change_x[:, k * points : (k + 1) * points]
        cz = change_z[k * points : (k + 1) * points]
        change[k] = cx * cx + cz * cz
    row = lax.broadcasted_iota(jnp.int32, (points, points), 0)
    lane = lax.broadcasted_iota(jnp.int32, (points, points), 1)
    gy, gz = frequency(row), frequency(lane)
    flat = gy * gy + gz * gz
    for i in range(share):
        gx = frequency(rank * share + i)
        squared = flat + gx * gx
        coulomb[:, i * points : (i + 1) * points] = jnp.where(
            squared > 0, (coulomb_scale / points) / jnp.maximum(squared, 1).astype(F32), 0.0
        )

    def gathered(ref, along):
        found = []
        for m in range(share):
            pieces = [
                ref[pl.ds(k * share + m if along else m * share + k, count, stride=block), :] for k in range(share)
            ]
            found.append(jnp.concatenate(pieces, 0))
        return found

    def scattered(ref, value):
        for i in range(share):
            for k in range(share):
                ref[pl.ds(i * share + k, count, stride=block), :] = value[
                    k * count : (k + 1) * count, i * points : (i + 1) * points
                ]

    drained(arrived, field_sem.at[1, 0])
    columns = jnp.concatenate(gathered(arrived, False), 1)
    scattered(slope_sent, left(lefts[5], columns))
    field_exchange(1, slope_sent, slope_got)
    scattered(wave_sent, left(lefts[4], coulomb[...] * full_dot(plain[1], columns)))
    field_exchange(2, wave_sent, wave_got)

    def to_cells(ref):
        value = left(lefts[6], jnp.concatenate(gathered(ref, True), 1))
        value = jnp.concatenate([value[:, k * points : (k + 1) * points] for k in range(share)], 0)
        return right(value, rights[:, :points])

    drained(slope_got, field_sem.at[1, 1])
    change_y = to_cells(slope_got) * (1.0 / (points * points))
    for k in range(share):
        cy = change_y[k * points : (k + 1) * points]
        gradient = jnp.sqrt(change[k] + cy * cy)
        dens = core[first_plane + k]
        for other in range(peers):
            dens = dens + parts[other, first_plane + k]
        root = jnp.exp(jnp.log(dens) * (1.0 / 3.0))
        root = root - (root * root * root - dens) / (3.0 * root * root)
        reduced = gradient / (reduced_scale * dens * root)
        bounded = reduced / (1.0 + reduced)

        def unit(h, total):
            return total + mlp_out[h] * jnp.tanh(mlp_in[0, h] * root + mlp_in[1, h] * bounded + mlp_in[2, h])

        enhance = lax.fori_loop(0, hidden, unit, jnp.ones_like(root), unroll=4)
        network[k] = external[first_plane + k] - exchange_scale * root * enhance

    drained(wave_got, field_sem.at[1, 2])
    hartree = to_cells(wave_got)

    def shared(i, seat_of, k):
        piece = out.at[seat_of * share + k]
        return remote(
            piece, piece, share_sem.at[0, i - 1, k], share_sem.at[1, i - 1, k], at(me, team + lax.rem(seat + i, sub))
        )

    for k in range(share):
        out[first_plane + k] = network[k] + hartree[k * points : (k + 1) * points]
        for i in range(1, sub):
            shared(i, seat, k).start()

    @pl.when(holder)
    def _():
        for b in range(bands):
            last(b).wait_recv()
        for b in range(bands):
            for x in range(planes):
                value = fresh[b, x] if x < slots else returned[b, x - slots]
                if x == 0:
                    clean = jnp.where(jnp.logical_and(tile_row == 0, me == home), alone, 1.0)
                    value = jnp.concatenate([value[:8] * clean, value[8:]], 0)
                swapped = pltpu.roll(value, half, 1)
                real = jnp.where(lanes < reach, value, jnp.where(lanes >= points - reach, swapped, 0.0))
                imag = jnp.where(lanes < reach, swapped, jnp.where(lanes >= points - reach, value, 0.0))
                for p, found in enumerate((real, imag)):
                    new_out[b, p, x, 0:reach] = found[:reach]
                    new_out[b, p, x, reach : reach + 8] = jnp.zeros((8, points), F32)
                    new_out[b, p, x, reach + 8 : half + 8] = found[reach:]

    @pl.when(jnp.logical_not(holder))
    def _():
        new_out[...] = jnp.zeros_like(new_out)

    @pl.when(me == 0)
    def _():
        back(0, 0).wait_recv()
        for b in range(bands):
            for p in range(2):
                z_point = lane_to(fixed_back[b], 2 + half * p, reach)
                new_out[b, p, 0, 0:8] = new_out[b, p, 0, 0:8] + z_point
                new_out[b, p, 0, reach : reach + 8] = lane_to(fixed_back[b], 3 + half * p, 0)

    @pl.when(me == zone)
    def _():
        back(0, 0).wait_recv()
        for b in range(bands):
            for p in range(2):
                new_out[b, p, 0, 0:8] = lane_to(fixed_back[b], 1 + half * p, 0)

    @pl.when(holder)
    def _():
        for b in range(bands):
            first(b).wait_send()

    @pl.when(jnp.logical_not(holder))
    def _():
        for b in range(bands):
            last(b).wait_send()

    @pl.when(me == 0)
    def _():
        fixed(0).wait_send()

    @pl.when(me == zone)
    def _():
        fixed(1).wait_send()

    @pl.when(me == home)
    def _():
        back(0, 0).wait_send()
        back(zone, 1).wait_send()

    for k in range((2 * iters + 1) * bands):
        drained(sent.at[k, pl.ds(0, n - 1)], send_sem.at[k])
    drained(gram_got.at[pl.ds(0, n - 1)], gram_sem.at[0])
    for stage, ref in enumerate((staged, slope_sent, wave_sent)):
        drained(ref.at[pl.ds(0, (count - 1) * block)], field_sem.at[0, stage])
    for i in range(1, sub):
        for k in range(share):
            shared(i, seat, k).wait_send()
            shared(i, lax.rem(seat + sub - i, sub), k).wait_recv()


def body(coefficients, potential, external, core_density, rotations, mlp_in, mlp_out):
    n, peers = lax.axis_size("grid"), lax.axis_size("band")
    bands, _, planes, points, _ = coefficients.shape
    iters = rotations.shape[0]
    half = points // 2
    slots = half // n
    sub = math.gcd(peers, planes)
    share = planes // sub
    count = n * sub
    rows = count * share * share
    stages = (2 * iters + 1) * bands
    size = (iters + 1) * bands
    tables = transform_tables(n, points, count, share)
    any_space = pl.BlockSpec(memory_space=pl.ANY)
    vmem = pl.BlockSpec(memory_space=pltpu.VMEM)
    smem = pl.BlockSpec(memory_space=pltpu.SMEM)
    dma = pltpu.SemaphoreType.DMA

    def store(*shape):
        return pltpu.VMEM(shape, F32)

    new, new_potential = pl.pallas_call(
        functools.partial(kernel, n, peers, bands, points, iters, mlp_out.shape[0]),
        out_shape=(
            jax.ShapeDtypeStruct((bands, 2, planes, half + 8, points), F32),
            jax.ShapeDtypeStruct((planes, points, points), F32),
        ),
        in_specs=[any_space] * 4 + [smem] * 3 + [vmem] * len(tables),
        out_specs=(vmem, vmem),
        scratch_shapes=[
            store(bands, 2, planes, half + 8, points),
            store(planes, points, points),
            store(planes, points, points),
            store(planes, points, points),
            store(bands, slots, half, points),
            store(bands, slots, half, points),
            store(iters + 1, bands, slots, half, points),
            store(slots, half, points),
            store(slots, half, points),
            store(stages, n, slots, planes, points),
            store(stages, n, slots, planes, points),
            store(half * planes, points),
            store(half * planes, points),
            store(16 * planes, points),
            store(16 * planes, points),
            store(size, planes, points, 2 * points),
            store(bands, 8, points),
            store(2, bands, 8, points),
            store(1, points),
            store(n, 1, points),
            store(bands, slots, half, points),
            store(bands, slots, half, points),
            store(bands, 8, points),
            store(bands, 8, points),
            store(peers, planes, points, points),
            store(points, share * points),
            store(rows, points),
            store(rows, points),
            store(rows, points),
            store(rows, points),
            store(rows, points),
            store(rows, points),
            store(share, points, points),
            store(share, points, points),
            dma((4 * bands + 3,)),
            dma((2, bands)),
            dma((3,)),
            dma((stages,)),
            dma((stages,)),
            dma((2,)),
            dma((2, bands)),
            dma((3,)),
            dma((2, max(peers - 1, 1), planes)),
            dma((2, 3)),
            dma((1,)),
            dma((2, max(sub - 1, 1), share)),
        ],
        compiler_params=pltpu.CompilerParams(
            collective_id=0, has_side_effects=True, vmem_limit_bytes=60 * 2**20
        ),
    )(coefficients, potential, external, core_density, rotations, mlp_in, mlp_out, *tables)

    reach = half // 2
    low = lax.slice_in_dim(new, 0, reach + 8, axis=3)
    high = lax.slice_in_dim(new, reach + 8, half + 8, axis=3)
    zeros = jnp.zeros((bands, 2, planes, points - half - 8, points), F32)
    return jnp.concatenate([low, zeros, high], 3), new_potential


def solution(mesh):
    in_specs = (
        P("band", None, "grid", None, None),
        P("grid", None, None),
        P("grid", None, None),
        P("grid", None, None),
        P(None, "band", None),
        P(),
        P(),
    )
    out_specs = (P("band", None, "grid", None, None), P("grid", None, None))
    return jax.shard_map(body, mesh=mesh, in_specs=in_specs, out_specs=out_specs, check_vma=False)
```

```python
import functools
import math

import jax
import jax.numpy as jnp
import numpy as np
from jax import lax
from jax.experimental import pallas as pl
from jax.experimental.pallas import tpu as pltpu
from jax.sharding import PartitionSpec as P

MESH = pl.DeviceIdType.MESH
F32 = jnp.float32
BF16 = jnp.bfloat16
HIGHEST = lax.Precision.HIGHEST

step_size = 0.2
epsilon = 1e-06
spacing = 0.58
kinetic_scale = 0.5 * (2.0 * math.pi / spacing) ** 2
coulomb_scale = spacing * spacing / math.pi
gradient_scale = 2.0 * math.pi / spacing
reduced_scale = 2.0 * (3.0 * math.pi * math.pi) ** (1.0 / 3.0)
exchange_scale = (3.0 / math.pi) ** (1.0 / 3.0)
level_shift = 2.275


def halves(table):
    table = np.asarray(table, np.float32)
    high = table.astype(BF16)
    low = (table - high.astype(np.float32)).astype(BF16)
    return high, low


def table_for_left(table):
    high, low = halves(table)
    return np.concatenate([high, high, low], 1)


def table_for_right(table):
    high, low = halves(table)
    return np.concatenate([high, high, low], 0)


def split(value):
    high = value.astype(BF16)
    return high, (value - high.astype(F32)).astype(BF16)


def dot(a, b):
    return jnp.dot(a, b, preferred_element_type=F32)


def left(table, value):
    high, low = split(value)
    return dot(table, jnp.concatenate([high, low, high], 0))


def right(value, table):
    high, low = split(value)
    return dot(jnp.concatenate([high, low, high], 1), table)


def full_dot(a, b):
    return jnp.dot(a, b, preferred_element_type=F32, precision=HIGHEST)


def slot_planes(n, points):
    planes, slots = points // n, points // 2 // n
    found = []
    for device in range(n):
        quarter = device // (n // 4)
        owner = device + (0, -(n // 4), n // 4, 0)[quarter]
        start = owner * planes + (0, slots, slots, 0)[quarter]
        found += [start + i for i in range(slots)]
    return np.array(found)


def cell_order(count, share):
    return np.array([o * share + k for k in range(share) for o in range(count)])


def transform_tables(n, points, count, share):
    half = points // 2
    keep = np.arange(half)
    keep = np.where(keep < half // 2, keep, keep - half)
    cell = np.arange(points)

    def waves(freq):
        angle = 2.0 * np.pi * ((freq[:, None] * cell[None, :]) % points) / points
        return np.cos(angle), np.sin(angle)

    cos, sin = waves(keep)
    plane = slot_planes(n, points)
    cos_x, sin_x = waves(np.where(2 * plane < points, plane, plane - points))
    freq = np.where(2 * cell < points, cell, cell - points)
    slope = gradient_scale * np.where(2 * freq == -points, 0, freq) / points
    cos_all, sin_all = waves(cell)
    derivative = ((cos_all + 1j * sin_all) * slope[None, :] * 1j) @ (cos_all - 1j * sin_all) / points
    derivative = derivative.real
    basis = cos_all + sin_all
    order = cell_order(count, share)
    lefts = np.stack([
        table_for_left(t) for t in (
            np.concatenate([cos.T, sin.T], 1),
            np.concatenate([cos, sin], 0),
            np.concatenate([cos_x.T, sin_x.T], 1),
            np.concatenate([cos_x, sin_x], 0),
            basis[order],
            derivative[order][:, order],
            basis[:, order],
            derivative,
            basis,
        )
    ])
    rights = np.concatenate([table_for_right(basis), table_for_right(derivative.T)], 1)
    z_out = table_for_right(np.block([[cos, sin], [-sin, cos]]))
    z_in = table_for_right(np.block([[cos.T, -sin.T], [sin.T, cos.T]]))
    plain = basis[:, order][None].astype(np.float32)
    return lefts, rights, z_out, z_in, plain


def kernel(
    n, peers, bands, points, iters, hidden,
    coefficients, potential_in, external_in, core_in, rotations, mlp_in, mlp_out,
    lefts_in, rights_in, z_out_in, z_in_in, plain_in,
    low_out, high_out, out,
    tables_l, tables_r, table_out, table_in, table_plain, given, potential, external, core, raw, forward, vectors, mask, kinetic,
    sent, got, level_r, level_i, edge_r, edge_i, space_of, fixed_out, fixed_got,
    gram_tile, gram_got, fresh, returned, fixed_new, fixed_back,
    parts, coulomb, staged, arrived, slope_sent, slope_got, wave_sent, wave_got, change, network,
    load_sem, first_sem, fixed_sem, send_sem, recv_sem, gram_sem, last_sem, back_sem, dens_sem, field_sem, own_sem,
    share_sem,
):
    me = lax.axis_index("grid")
    band = lax.axis_index("band")
    half = points // 2
    reach = half // 2
    slots = half // n
    planes = points // n
    zone = n // 4
    home = n - zone
    edge = home * slots
    sub = math.gcd(peers, planes)
    share = planes // sub
    count = n * sub
    block = share * share
    seat = lax.rem(band, sub)
    team = band - seat
    rank = me * sub + seat
    holder = jnp.logical_or(me < zone, me >= home)
    partner = jnp.where(
        me < zone, me + zone, jnp.where(me < 2 * zone, me - zone, jnp.where(me < home, me + zone, me - zone))
    )

    def at(grid, other=None):
        return {"band": band if other is None else other, "grid": grid}

    def remote(source, target, send, recv, device):
        return pltpu.make_async_remote_copy(
            src_ref=source, dst_ref=target, send_sem=send, recv_sem=recv, device_id=device, device_id_type=MESH
        )

    def drained(ref, sem):
        pltpu.make_async_copy(ref, ref, sem).wait()

    loads = []
    for b in range(bands):
        for p in range(2):
            k = 2 * (2 * b + p)
            loads.append(pltpu.make_async_copy(
                coefficients.at[b, p, :, pl.ds(0, reach + 8)], given.at[b, p, :, pl.ds(0, reach + 8)], load_sem.at[k]
            ))
            loads.append(pltpu.make_async_copy(
                coefficients.at[b, p, :, pl.ds(points - reach, reach)],
                given.at[b, p, :, pl.ds(reach + 8, reach)],
                load_sem.at[k + 1],
            ))
    base = 4 * bands
    tables = [
        pltpu.make_async_copy(source, target, load_sem.at[base + 3 + k])
        for k, (source, target) in enumerate((
            (lefts_in, tables_l), (z_out_in, table_out), (z_in_in, table_in), (rights_in, tables_r), (plain_in, table_plain)
        ))
    ]
    late = [
        pltpu.make_async_copy(potential_in, potential, load_sem.at[base]),
        pltpu.make_async_copy(external_in, external, load_sem.at[base + 1]),
        pltpu.make_async_copy(core_in, core, load_sem.at[base + 2]),
    ]
    needed = jnp.logical_or(holder, me == zone)

    @pl.when(needed)
    def _():
        for copy in loads:
            copy.start()

    for copy in tables + late:
        copy.start()

    barrier = pltpu.get_barrier_semaphore()

    @pl.loop(1, n)
    def _(i):
        for k in range(sub):
            pl.semaphore_signal(barrier, inc=1, device_id=at(lax.rem(me + i, n), team + k), device_id_type=MESH)

    for k in range(1, sub):
        pl.semaphore_signal(barrier, inc=1, device_id=at(me, team + lax.rem(seat + k, sub)), device_id_type=MESH)

    for i in range(1, peers):
        other = lax.rem(band + i, peers)

        @pl.when(other - lax.rem(other, sub) != team)
        def _():
            pl.semaphore_signal(barrier, inc=1, device_id=at(me, other), device_id_type=MESH)

    lanes = lax.broadcasted_iota(jnp.int32, (1, points), 1)
    tile_lane = lax.broadcasted_iota(jnp.int32, (8, points), 1)
    tile_row = lax.broadcasted_iota(jnp.int32, (8, points), 0)
    sign = jnp.where(lanes < half, -1.0, 1.0).astype(F32)
    alone = jnp.where(lax.rem(lanes, half) == 0, 1.0, 0.0).astype(F32)

    def quarter_turn(k):
        k = lax.rem(k, 4)
        c = jnp.where(k == 0, 1.0, jnp.where(k == 2, -1.0, 0.0)).astype(F32)
        s = jnp.where(k == 1, 1.0, jnp.where(k == 3, -1.0, 0.0)).astype(F32)
        return c, s

    z_c, z_s = quarter_turn(lanes)
    y_c, y_s = quarter_turn(me * planes + lax.broadcasted_iota(jnp.int32, (planes, 1), 0))

    def turn(value):
        return pltpu.roll(value, half, 1) * sign

    def frequency(place):
        return jnp.where(2 * place < points, place, place - points)

    own_start = jnp.where(holder, me * planes, partner * planes + slots)
    row = lax.broadcasted_iota(jnp.int32, (half, points), 0)
    gy = jnp.where(row < reach, row, row - half)
    lane = lax.rem(lax.broadcasted_iota(jnp.int32, (half, points), 1), half)
    gz = jnp.where(lane < reach, lane, lane - half)
    flat = gy * gy + gz * gz
    for x in range(slots):
        gx = frequency(own_start + x)
        squared = flat + gx * gx
        if x == 0:
            spot = jnp.logical_and(jnp.logical_and(row == 0, lane < 4), me == home)
            squared = jnp.where(spot, reach * reach, squared)
        mask[x] = jnp.where(16 * squared <= points * points, 1.0, 0.0).astype(F32)
        kinetic[x] = kinetic_scale * squared.astype(F32) / (points * points)
    edge_r[...] = jnp.zeros_like(edge_r)
    edge_i[...] = jnp.zeros_like(edge_i)

    @pl.when(needed)
    def _():
        for copy in loads:
            copy.wait()

    def packed(b, x):
        found = []
        for p in range(2):
            found.append(jnp.concatenate([given[b, p, x, 0:reach], given[b, p, x, reach + 8 : half + 8]], 0))
        real, imag = found
        low = jnp.where(lanes < reach, real, pltpu.roll(real, half, 1))
        high = jnp.where(lanes < half + reach, pltpu.roll(imag, half, 1), imag)
        return jnp.where(lanes < half, low, high)

    @pl.when(holder)
    def _():
        for b in range(bands):
            for x in range(slots):
                forward[b, x] = packed(b, slots + x)
                raw[b, x] = packed(b, x)

    def lane_to(value, start, target):
        moved = pltpu.roll(value, (target - start) % points, 1)
        return jnp.where(jnp.logical_and(tile_lane == target, tile_row == 0), moved, 0.0)

    @pl.when(me == 0)
    def _():
        for b in range(bands):
            total = None
            for p in range(2):
                z_point = lane_to(given[b, p, 0, 0:8], reach, 2 + half * p)
                y_point = lane_to(given[b, p, 0, reach : reach + 8], 0, 3 + half * p)
                total = z_point + y_point if total is None else total + z_point + y_point
            fixed_out[b] = total

    @pl.when(me == zone)
    def _():
        for b in range(bands):
            fixed_out[b] = lane_to(given[b, 0, 0, 0:8], 0, 1) + lane_to(given[b, 1, 0, 0:8], 0, 1 + half)

    pl.semaphore_wait(barrier, count - 1 + peers - sub)

    def first(b):
        return remote(forward.at[b], raw.at[b], first_sem.at[0, b], first_sem.at[1, b], at(partner))

    def fixed(place):
        return remote(fixed_out, fixed_got.at[place], fixed_sem.at[0], fixed_sem.at[1 + place], at(home))

    @pl.when(me == 0)
    def _():
        fixed(0).start()

    @pl.when(me == zone)
    def _():
        fixed(1).start()

    def exchange(place):
        def copy(target):
            return remote(
                sent.at[place, target], got.at[place, me], send_sem.at[place], recv_sem.at[place], at(target)
            )

        @pl.loop(1, n)
        def _(i):
            copy(lax.rem(me + i, n)).start()

        pltpu.make_async_copy(sent.at[place, me], got.at[place, me], recv_sem.at[place]).start()

    def received(place):
        drained(got.at[place], recv_sem.at[place])

    def outward(value_of, place):
        stacked = []
        for x in range(slots):
            value = value_of(x)
            stacked.append(jnp.concatenate([value, turn(value)], 0))
        full = left(tables_l[0], jnp.concatenate(stacked, 1))
        for x in range(slots):
            sent[place, :, x] = full[:, x * points : (x + 1) * points].reshape(n, planes, points)
        exchange(place)

    def space(place, action, order=range(planes)):
        levels = right(got[place].reshape(half * planes, points), table_out[...])
        level_r[...] = levels[:, :points]
        level_i[...] = levels[:, points:]
        special = got[place, home, 0]

        def lane_of(k):
            return jnp.broadcast_to(special[:, k : k + 1], (planes, points))

        minus_r, plus_r, z_r, y_r = [lane_of(k) for k in range(4)]
        minus_i, plus_i, z_i, y_i = [lane_of(half + k) for k in range(4)]
        level_r[edge * planes : (edge + 1) * planes, :] = minus_r + plus_r
        level_i[edge * planes : (edge + 1) * planes, :] = minus_i + plus_i
        level_r[0:planes, :] += z_r * z_c - z_i * z_s + y_r * y_c - y_i * y_s
        level_i[0:planes, :] += z_r * z_s + z_i * z_c + y_r * y_s + y_i * y_c
        edge_r[pl.ds(0, planes, stride=8), :] = 2.0 * plus_r
        edge_i[pl.ds(0, planes, stride=8), :] = 2.0 * plus_i

        def without(value, y, extra):
            tile = value[edge : edge + 8] - extra[pl.ds(pl.multiple_of(y * 8, 8), 8), :]
            return jnp.concatenate([value[:edge], tile, value[edge + 8 :]], 0)

        for y in order:
            real = level_r[pl.ds(y, half, stride=planes), :]
            imag = level_i[pl.ds(y, half, stride=planes), :]
            stacked = jnp.concatenate(
                [
                    jnp.concatenate([real, imag], 1),
                    jnp.concatenate([-without(imag, y, edge_i), without(real, y, edge_r)], 1),
                ],
                0,
            )
            action(y, left(tables_l[2], stacked))

    def spectrum(index, place):
        def action(y, wave):
            space_of[index, y] = wave
            field = potential[y]
            product = wave * jnp.concatenate([field, field], 1)
            both = left(tables_l[3], product)
            cos_r, cos_i = both[:half, :points], both[:half, points:]
            sin_r, sin_i = both[half:, :points], both[half:, points:]
            level_r[pl.ds(y, half, stride=planes), :] = cos_r + sin_i
            level_i[pl.ds(y, half, stride=planes), :] = cos_i - sin_r
            edge_r[8 * (planes + y) : 8 * (planes + y) + 8, :] = cos_r[edge : edge + 8] - sin_i[edge : edge + 8]
            edge_i[8 * (planes + y) : 8 * (planes + y) + 8, :] = cos_i[edge : edge + 8] + sin_r[edge : edge + 8]

        space(place, action)
        both = jnp.concatenate([level_r[...], level_i[...]], 1)
        sent[place + bands] = right(both, table_in[...]).reshape(n, slots, planes, points)

        def total(value):
            return jnp.sum(value, 1, keepdims=True)

        plus_r = edge_r[pl.ds(8 * planes, planes, stride=8), :]
        plus_i = edge_i[pl.ds(8 * planes, planes, stride=8), :]
        zero_r, zero_i = level_r[0:planes, :], level_i[0:planes, :]
        line_r, line_i = total(zero_r), total(zero_i)
        found = [
            total(plus_r), total(zero_r * z_c + zero_i * z_s), line_r * y_c + line_i * y_s,
            total(plus_i), total(zero_i * z_c - zero_r * z_s), line_i * y_c - line_r * y_s,
        ]
        special = sent[place + bands, home, 0] * alone
        for k, value in enumerate(found):
            special = jnp.where(lanes == (k + 1 if k < 3 else half + k - 2), value, special)
        sent[place + bands, home, 0] = special
        exchange(place + bands)

    def inward(place):
        columns = [got[place, :, x].reshape(points, points) for x in range(slots)]
        both = left(tables_l[1], jnp.concatenate(columns, 1))
        found = []
        for x in range(slots):
            part = both[:, x * points : (x + 1) * points]
            found.append(part[:half] - turn(part[half:]))
        return found

    grams = {}

    def measure(p):
        for q in range(p + 1):
            u = vectors[p // bands, p % bands].reshape(slots * half, points)
            v = vectors[q // bands, q % bands].reshape(slots * half, points)
            grams[q, p] = jnp.sum(u * v, 0, keepdims=True)

    tables[0].wait()
    for b in range(bands):
        @pl.when(holder)
        def _():
            first(b).start()

        @pl.when(jnp.logical_not(holder))
        def _():
            first(b).wait_recv()

        if b == 0:
            @pl.when(me == home)
            def _():
                fixed(0).wait_recv()
                fixed(1).wait_recv()
                for c in range(bands):
                    fixed_got[0, c] = fixed_got[0, c] + fixed_got[1, c]

        @pl.when(me == home)
        def _():
            clean = jnp.where(tile_row == 0, alone, 1.0)
            raw[b, 0, 0:8, :] = raw[b, 0, 0:8, :] * clean * mask[0, 0:8, :] + fixed_got[0, b]

        vectors[0, b] = raw[b] * mask[...]
        outward(lambda x: vectors[0, b, x], b)

    late[0].wait()
    tables[1].wait()
    tables[2].wait()
    size = (iters + 1) * bands
    for b in range(bands):
        measure(b)
    for t in range(iters):
        for b in range(bands):
            received(2 * t * bands + b)
            spectrum(t * bands + b, 2 * t * bands + b)
        for b in range(bands):
            place = (2 * t + 1) * bands + b
            received(place)
            found = inward(place)
            for x in range(slots):
                vectors[t + 1, b, x] = mask[x] * (
                    kinetic[x] * vectors[t, b, x] + found[x] * (1.0 / points**3)
                )
            last = (t + 1) * bands + b == size - 1
            if last:
                measure(size - 1)
                tile = jnp.zeros((1, points), F32)
                keys = sorted(grams)
                for k, key in enumerate(keys):
                    tile = jnp.where(lanes == k, jnp.sum(grams[key], 1, keepdims=True), tile)
                gram_tile[...] = tile

                def gram_copy(target):
                    return remote(gram_tile, gram_got.at[me], gram_sem.at[0], gram_sem.at[1], at(target))

                @pl.loop(1, n)
                def _(i):
                    gram_copy(lax.rem(me + i, n)).start()

                pltpu.make_async_copy(gram_tile, gram_got.at[me], gram_sem.at[1]).start()
            outward(lambda x: vectors[t + 1, b, x], (2 * t + 2) * bands + b)
            if not last:
                measure((t + 1) * bands + b)

    drained(gram_got, gram_sem.at[1])
    sums = jnp.sum(gram_got[...], 0)
    gram = {}
    for k, (p, q) in enumerate(keys):
        gram[p, q] = gram[q, p] = sums[:, k : k + 1]

    def product(u, v):
        total = None
        for p, a in enumerate(u):
            inner = None
            for q, c in enumerate(v):
                if a is not None and c is not None:
                    term = c * gram[p, q]
                    inner = term if inner is None else inner + term
            if inner is not None:
                total = a * inner if total is None else total + a * inner
        return total

    def combine(terms):
        result = []
        for p in range(size):
            value = None
            for scale, u in terms:
                if u[p] is not None:
                    value = scale * u[p] if value is None else value + scale * u[p]
            result.append(value)
        return result

    one = jnp.ones((1, 1), F32)
    current = [[one if p == b else None for p in range(size)] for b in range(bands)]
    for t in range(iters):
        moved = []
        for b in range(bands):
            pushed = [None] * bands + current[b][: size - bands]
            factor = 1.0 + step_size * (product(current[b], pushed) / (product(current[b], current[b]) + epsilon))
            moved.append(combine([(factor, current[b]), (-step_size, pushed)]))
        following = []
        for b in range(bands):
            rotated = combine([(rotations[t, b, c], moved[c]) for c in range(bands)])
            scale = lax.rsqrt(jnp.maximum(product(rotated, rotated), 0.0) + epsilon)
            following.append([None if value is None else scale * value for value in rotated])
        current = following

    for b in range(bands):
        for x in range(slots):
            fresh[b, x] = sum(current[b][p] * vectors[p // bands, p % bands, x] for p in range(size))

    place = 2 * iters * bands
    for b in range(bands - 1):
        received(place + b)

        def keep(y, wave):
            space_of[iters * bands + b, y] = wave

        space(place + b, keep)

    for y in range(planes):
        for b in range(bands):
            known = [space_of[p, y] for p in range(size - 1)]
            mixed = [sum(current[b][p] * known[p] for p in range(size - 1)) for b in range(bands)]
        for b in range(bands):
            space_of[b, y] = mixed[b]

    def density_copy(i, y):
        target = lax.rem(band + i, peers)
        return remote(
            parts.at[band, y], parts.at[band, y], dens_sem.at[0, i - 1, y], dens_sem.at[1, i - 1, y], at(me, target)
        )

    received(place + bands - 1)

    def density(y, wave):
        total = None
        for b in range(bands):
            value = space_of[b, y] + current[b][size - 1] * wave
            square = value * value
            square = square[:, :points] + square[:, points:]
            total = square if total is None else total + square
        parts[band, y] = total * (2.0 / (bands * peers))
        for i in range(1, peers):
            @pl.when(lax.rem(lax.rem(band + i, peers), sub) == lax.div(y, share))
            def _():
                density_copy(i, y).start()

    turns = [lax.rem(seat + 1 + m // share, sub) * share + m % share for m in range(planes)]
    space(place + bands - 1, density, turns)

    late[2].wait()
    late[1].wait()
    tables[3].wait()
    tables[4].wait()
    for i in range(1, peers):
        for y in range(planes):
            @pl.when(lax.rem(lax.rem(band + i, peers), sub) == y // share)
            def _():
                density_copy(i, y).wait_send()

            @pl.when(seat == y // share)
            def _():
                density_copy(i, y).wait_recv()

    first_plane = seat * share
    whole = []
    for k in range(share):
        total = core[first_plane + k]
        for other in range(peers):
            total = total + parts[other, first_plane + k]
        whole.append(total)
    varying = [value - level_shift for value in whole]

    pieces = 2 if share % 2 == 0 else 1
    piece = block // pieces
    width = share // pieces

    def field_exchange(stage, part, source, target):
        k = stage * pieces + part

        def copy(other, seat_of):
            return remote(
                source.at[pl.ds((other * sub + seat_of) * block + part * piece, piece)],
                target.at[pl.ds(rank * block + part * piece, piece)],
                field_sem.at[0, k],
                field_sem.at[1, k],
                at(other, team + seat_of),
            )

        @pl.loop(1, n)
        def _(i):
            for seat_of in range(sub):
                copy(lax.rem(me + i, n), seat_of).start()

        for i in range(1, sub):
            copy(me, lax.rem(seat + i, sub)).start()

        own = pl.ds(rank * block + part * piece, piece)
        pltpu.make_async_copy(source.at[own], target.at[own], field_sem.at[1, k]).start()

    def field_drained(stage, part, ref):
        drained(ref.at[pl.ds(0, count * piece)], field_sem.at[1, stage * pieces + part])

    level = left(tables_l[8], jnp.concatenate(varying, 1))
    level = jnp.concatenate([level[:, k * points : (k + 1) * points] for k in range(share)], 0)
    level = right(level, tables_r[:, :points])
    for k in range(share):
        staged[pl.ds(k, points, stride=share), :] = level[k * points : (k + 1) * points]
    for part in range(pieces):
        field_exchange(0, part, staged, arrived)

    def last(b):
        return remote(fresh.at[b], returned.at[b], last_sem.at[0, b], last_sem.at[1, b], at(partner))

    def back(target, sem):
        return remote(fixed_new, fixed_back, back_sem.at[sem], back_sem.at[2], at(target))

    @pl.when(jnp.logical_not(holder))
    def _():
        for b in range(bands):
            last(b).start()

    @pl.when(me == home)
    def _():
        for b in range(bands):
            fixed_new[b] = fresh[b, 0, 0:8, :]
        back(0, 0).start()
        back(zone, 1).start()

    columns = jnp.concatenate(varying, 1)
    change_x = left(tables_l[7], columns)
    change_z = right(jnp.concatenate(varying, 0), tables_r[:, points:])
    for k in range(share):
        cx = change_x[:, k * points : (k + 1) * points]
        cz = change_z[k * points : (k + 1) * points]
        change[k] = cx * cx + cz * cz
    row = lax.broadcasted_iota(jnp.int32, (points, points), 0)
    lane = lax.broadcasted_iota(jnp.int32, (points, points), 1)
    gy, gz = frequency(row), frequency(lane)
    flat = gy * gy + gz * gz
    for i in range(share):
        gx = frequency(rank * share + i)
        squared = flat + gx * gx
        coulomb[:, i * points : (i + 1) * points] = jnp.where(
            squared > 0, (coulomb_scale / points) / jnp.maximum(squared, 1).astype(F32), 0.0
        )

    def column(ref, i):
        return jnp.concatenate([ref[pl.ds(i * share + k, count, stride=block), :] for k in range(share)], 0)

    def plane_of(ref, k):
        return jnp.concatenate([ref[pl.ds(i * share + k, count, stride=block), :] for i in range(share)], 0)

    def scattered(ref, part, value):
        for j in range(width):
            for k in range(share):
                ref[pl.ds((part * width + j) * share + k, count, stride=block), :] = value[
                    k * count : (k + 1) * count, j * points : (j + 1) * points
                ]

    columns = []
    for part in range(pieces):
        field_drained(0, part, arrived)
        columns.append(jnp.concatenate([column(arrived, part * width + j) for j in range(width)], 1))
        scattered(slope_sent, part, left(tables_l[5], columns[part]))
        field_exchange(1, part, slope_sent, slope_got)
    for part in range(pieces):
        weight = coulomb[:, part * width * points : (part + 1) * width * points]
        scattered(wave_sent, part, left(tables_l[4], weight * full_dot(table_plain[0], columns[part])))
        field_exchange(2, part, wave_sent, wave_got)

    def to_cells(ref):
        value = left(tables_l[6], jnp.concatenate([plane_of(ref, k) for k in range(share)], 1))
        value = jnp.concatenate([value[:, k * points : (k + 1) * points] for k in range(share)], 0)
        return right(value, tables_r[:, :points])

    for part in range(pieces):
        field_drained(1, part, slope_got)
    change_y = to_cells(slope_got) * (1.0 / (points * points))
    for k in range(share):
        cy = change_y[k * points : (k + 1) * points]
        gradient = jnp.sqrt(change[k] + cy * cy)
        dens = core[first_plane + k]
        for other in range(peers):
            dens = dens + parts[other, first_plane + k]
        root = jnp.exp(jnp.log(dens) * (1.0 / 3.0))
        root = root - (root * root * root - dens) / (3.0 * root * root)
        reduced = gradient / (reduced_scale * dens * root)
        bounded = reduced / (1.0 + reduced)

        def unit(h, total):
            return total + mlp_out[h] * jnp.tanh(mlp_in[0, h] * root + mlp_in[1, h] * bounded + mlp_in[2, h])

        enhance = lax.fori_loop(0, hidden, unit, jnp.ones_like(root), unroll=4)
        network[k] = external[first_plane + k] - exchange_scale * root * enhance

    @pl.when(holder)
    def _():
        for b in range(bands):
            last(b).wait_recv()
        for b in range(bands):
            for x in range(planes):
                value = fresh[b, x] if x < slots else returned[b, x - slots]
                if x == 0:
                    clean = jnp.where(jnp.logical_and(tile_row == 0, me == home), alone, 1.0)
                    value = jnp.concatenate([value[:8] * clean, value[8:]], 0)
                swapped = pltpu.roll(value, half, 1)
                real = jnp.where(lanes < reach, value, jnp.where(lanes >= points - reach, swapped, 0.0))
                imag = jnp.where(lanes < reach, swapped, jnp.where(lanes >= points - reach, value, 0.0))
                for p, found in enumerate((real, imag)):
                    low_out[b, p, x, 0:reach] = found[:reach]
                    low_out[b, p, x, reach : reach + 8] = jnp.zeros((8, points), F32)
                    high_out[b, p, x] = found[reach:]

    @pl.when(jnp.logical_not(holder))
    def _():
        low_out[...] = jnp.zeros_like(low_out)
        high_out[...] = jnp.zeros_like(high_out)

    @pl.when(me == 0)
    def _():
        back(0, 0).wait_recv()
        for b in range(bands):
            for p in range(2):
                z_point = lane_to(fixed_back[b], 2 + half * p, reach)
                low_out[b, p, 0, 0:8] = low_out[b, p, 0, 0:8] + z_point
                low_out[b, p, 0, reach : reach + 8] = lane_to(fixed_back[b], 3 + half * p, 0)

    @pl.when(me == zone)
    def _():
        back(0, 0).wait_recv()
        for b in range(bands):
            for p in range(2):
                low_out[b, p, 0, 0:8] = lane_to(fixed_back[b], 1 + half * p, 0)

    for part in range(pieces):
        field_drained(2, part, wave_got)
    hartree = to_cells(wave_got)

    def shared(i, seat_of, k):
        plane = out.at[seat_of * share + k]
        return remote(
            plane, plane, share_sem.at[0, i - 1, k], share_sem.at[1, i - 1, k], at(me, team + lax.rem(seat + i, sub))
        )

    for k in range(share):
        out[first_plane + k] = network[k] + hartree[k * points : (k + 1) * points]
        for i in range(1, sub):
            shared(i, seat, k).start()

    @pl.when(holder)
    def _():
        for b in range(bands):
            first(b).wait_send()

    @pl.when(jnp.logical_not(holder))
    def _():
        for b in range(bands):
            last(b).wait_send()

    @pl.when(me == 0)
    def _():
        fixed(0).wait_send()

    @pl.when(me == zone)
    def _():
        fixed(1).wait_send()

    @pl.when(me == home)
    def _():
        back(0, 0).wait_send()
        back(zone, 1).wait_send()

    for k in range((2 * iters + 1) * bands):
        drained(sent.at[k, pl.ds(0, n - 1)], send_sem.at[k])
    drained(gram_got.at[pl.ds(0, n - 1)], gram_sem.at[0])
    for stage, ref in enumerate((staged, slope_sent, wave_sent)):
        for part in range(pieces):
            drained(ref.at[pl.ds(0, (count - 1) * piece)], field_sem.at[0, stage * pieces + part])
    for i in range(1, sub):
        for k in range(share):
            shared(i, seat, k).wait_send()
            shared(i, lax.rem(seat + sub - i, sub), k).wait_recv()


def spread(bands, low, high, field, new, out, low_here, high_here, field_here, zeros, in_sem, out_sem):
    edge, width = low.shape[3], zeros.shape[2]
    arrivals = []
    for b in range(bands):
        arrivals.append(pltpu.make_async_copy(low.at[b], low_here.at[b], in_sem.at[2 * b]))
        arrivals.append(pltpu.make_async_copy(high.at[b], high_here.at[b], in_sem.at[2 * b + 1]))
    arrivals.append(pltpu.make_async_copy(field, field_here, in_sem.at[2 * bands]))
    for copy in arrivals:
        copy.start()
    zeros[...] = jnp.zeros_like(zeros)
    leaving = []
    for b in range(bands):
        leaving.append(pltpu.make_async_copy(zeros, new.at[b, :, :, pl.ds(edge, width)], out_sem.at[3 * b]))
        leaving[-1].start()
    for k, copy in enumerate(arrivals):
        copy.wait()
        b = k // 2
        if b == bands:
            place, source = out, field_here
        elif k % 2 == 0:
            place, source = new.at[b, :, :, pl.ds(0, edge)], low_here.at[b]
        else:
            place, source = new.at[b, :, :, pl.ds(edge + width, high.shape[3])], high_here.at[b]
        leaving.append(pltpu.make_async_copy(source, place, out_sem.at[3 * b + 1 + k % 2 if b < bands else 3 * bands]))
        leaving[-1].start()
    for copy in leaving:
        copy.wait()


def body(coefficients, potential, external, core_density, rotations, mlp_in, mlp_out):
    n, peers = lax.axis_size("grid"), lax.axis_size("band")
    bands, _, planes, points, _ = coefficients.shape
    iters = rotations.shape[0]
    half = points // 2
    slots = half // n
    sub = math.gcd(peers, planes)
    share = planes // sub
    count = n * sub
    rows = count * share * share
    stages = (2 * iters + 1) * bands
    size = (iters + 1) * bands
    lefts, rights, z_out, z_in, plain = transform_tables(n, points, count, share)
    tables = (lefts, rights, z_out, z_in, plain)
    any_space = pl.BlockSpec(memory_space=pl.ANY)
    vmem = pl.BlockSpec(memory_space=pltpu.VMEM)
    smem = pl.BlockSpec(memory_space=pltpu.SMEM)
    dma = pltpu.SemaphoreType.DMA

    def store(*shape):
        return pltpu.VMEM(shape, F32)

    low, high, new_potential = pl.pallas_call(
        functools.partial(kernel, n, peers, bands, points, iters, mlp_out.shape[0]),
        out_shape=(
            jax.ShapeDtypeStruct((bands, 2, planes, half // 2 + 8, points), F32),
            jax.ShapeDtypeStruct((bands, 2, planes, half // 2, points), F32),
            jax.ShapeDtypeStruct((planes, points, points), F32),
        ),
        in_specs=[any_space] * 4 + [smem] * 3 + [any_space] * len(tables),
        out_specs=(vmem, vmem, vmem),
        scratch_shapes=[pltpu.VMEM(t.shape, t.dtype) for t in tables] + [
            store(bands, 2, planes, half + 8, points),
            store(planes, points, points),
            store(planes, points, points),
            store(planes, points, points),
            store(bands, slots, half, points),
            store(bands, slots, half, points),
            store(iters + 1, bands, slots, half, points),
            store(slots, half, points),
            store(slots, half, points),
            store(stages, n, slots, planes, points),
            store(stages, n, slots, planes, points),
            store(half * planes, points),
            store(half * planes, points),
            store(16 * planes, points),
            store(16 * planes, points),
            store(size, planes, points, 2 * points),
            store(bands, 8, points),
            store(2, bands, 8, points),
            store(1, points),
            store(n, 1, points),
            store(bands, slots, half, points),
            store(bands, slots, half, points),
            store(bands, 8, points),
            store(bands, 8, points),
            store(peers, planes, points, points),
            store(points, share * points),
            store(rows, points),
            store(rows, points),
            store(rows, points),
            store(rows, points),
            store(rows, points),
            store(rows, points),
            store(share, points, points),
            store(share, points, points),
            dma((4 * bands + 3 + len(tables),)),
            dma((2, bands)),
            dma((3,)),
            dma((stages,)),
            dma((stages,)),
            dma((2,)),
            dma((2, bands)),
            dma((3,)),
            dma((2, max(peers - 1, 1), planes)),
            dma((2, 6)),
            dma((1,)),
            dma((2, max(sub - 1, 1), share)),
        ],
        compiler_params=pltpu.CompilerParams(
            collective_id=0, has_side_effects=True, vmem_limit_bytes=60 * 2**20
        ),
    )(coefficients, potential, external, core_density, rotations, mlp_in, mlp_out, *tables)

    return pl.pallas_call(
        functools.partial(spread, bands),
        out_shape=(
            jax.ShapeDtypeStruct((bands, 2, planes, points, points), F32),
            jax.ShapeDtypeStruct((planes, points, points), F32),
        ),
        in_specs=[any_space] * 3,
        out_specs=(any_space, any_space),
        scratch_shapes=[
            pltpu.VMEM(low.shape, F32),
            pltpu.VMEM(high.shape, F32),
            pltpu.VMEM(new_potential.shape, F32),
            store(2, planes, points - half - 8, points),
            dma((2 * bands + 1,)),
            dma((3 * bands + 1,)),
        ],
        compiler_params=pltpu.CompilerParams(vmem_limit_bytes=60 * 2**20),
    )(low, high, new_potential)


def solution(mesh):
    in_specs = (
        P("band", None, "grid", None, None),
        P("grid", None, None),
        P("grid", None, None),
        P("grid", None, None),
        P(None, "band", None),
        P(),
        P(),
    )
    out_specs = (P("band", None, "grid", None, None), P("grid", None, None))
    return jax.shard_map(body, mesh=mesh, in_specs=in_specs, out_specs=out_specs, check_vma=False)
```

```python
import functools
import math

import jax
import jax.numpy as jnp
import numpy as np
from jax import lax
from jax.experimental import pallas as pl
from jax.experimental.pallas import tpu as pltpu
from jax.sharding import PartitionSpec as P

MESH = pl.DeviceIdType.MESH
F32 = jnp.float32
BF16 = jnp.bfloat16
HIGHEST = lax.Precision.HIGHEST

step_size = 0.2
epsilon = 1e-06
spacing = 0.58
kinetic_scale = 0.5 * (2.0 * math.pi / spacing) ** 2
coulomb_scale = spacing * spacing / math.pi
gradient_scale = 2.0 * math.pi / spacing
reduced_scale = 2.0 * (3.0 * math.pi * math.pi) ** (1.0 / 3.0)
exchange_scale = (3.0 / math.pi) ** (1.0 / 3.0)
level_shift = 2.275


def halves(table):
    table = np.asarray(table, np.float32)
    high = table.astype(BF16)
    low = (table - high.astype(np.float32)).astype(BF16)
    return high, low


def table_for_left(table):
    high, low = halves(table)
    return np.concatenate([high, high, low], 1)


def table_for_right(table):
    high, low = halves(table)
    return np.concatenate([high, high, low], 0)


def split(value):
    high = value.astype(BF16)
    return high, (value - high.astype(F32)).astype(BF16)


def dot(a, b):
    return jnp.dot(a, b, preferred_element_type=F32)


def left(table, value):
    high, low = split(value)
    return dot(table, jnp.concatenate([high, low, high], 0))


def right(value, table):
    high, low = split(value)
    return dot(jnp.concatenate([high, low, high], 1), table)


def full_dot(a, b):
    return jnp.dot(a, b, preferred_element_type=F32, precision=HIGHEST)


class Plan:
    def __init__(self, n, points):
        planes, slots, reach, zone = points // n, points // 2 // n, points // 4, n // 4
        self.points, self.reach, self.planes, self.slots = points, reach, planes, slots
        kept = list(range(reach)) + list(range(points - reach, points))
        edge = points - reach
        holders = list(range(zone)) + list(range(n - zone, n))
        pairs = self.pairs(kept, edge) if slots > 1 else {}
        owned = self.shared_rows(n, pairs, kept, holders) if len(pairs) == n // 2 else None
        if owned is None:
            owned = [None] * n
            for h in holders:
                other = h + zone if h < zone else h - zone
                owned[h] = [(h * planes + i, None) for i in range(slots)]
                owned[other] = [(h * planes + slots + i, None) for i in range(slots)]
        self.owned = owned
        self.base = min(len(rows) for rows in owned)
        self.extra = [d for d in range(n) if len(owned[d]) > self.base]
        if len(self.extra) == n:
            self.base, self.extra = slots, []
        spare = [d * slots + i for d in range(n) for i in range(len(owned[d]), slots)]
        self.mixed, self.order, self.sends = [], [0] * (n * slots), {h: [] for h in holders}
        self.narrow = set()
        for d in range(n):
            for i, (wide, narrow) in enumerate(owned[d]):
                place = d * slots + i
                self.order[place] = wide
                self.sends[wide // planes].append((wide % planes, d, i, 0))
                if narrow is not None:
                    self.narrow.add(narrow)
                    self.sends[narrow // planes].append((narrow % planes, d, i, 1))
                    self.mixed.append((place, spare[len(self.mixed)], wide))
                    self.order[self.mixed[-1][1]] = narrow
                if edge in (wide, narrow):
                    self.home, self.home_slot, self.home_part = d, i, 0 if edge == wide else 1
        self.edge, self.zero = self.order.index(edge), self.order.index(0)

    def freq(self, plane):
        return plane if 2 * plane < self.points else plane - self.points

    def width(self, plane):
        return math.isqrt(self.reach**2 - self.freq(plane) ** 2)

    def pairs(self, kept, edge):
        found, used = {}, {edge}
        for side in (1, -1):
            group = [p for p in kept if (self.freq(p) >= 0) == (side > 0) and p != edge]
            for narrow in sorted(group, key=self.width):
                if narrow in used or 2 * self.width(narrow) >= self.reach - 1:
                    continue
                limit = self.reach - 1 - self.width(narrow)
                fits = [p for p in group if p not in used and p != narrow and self.width(p) <= limit]
                fits = [p for p in fits if self.width(p) > self.width(narrow)]
                if fits:
                    wide = max(fits, key=lambda p: (self.width(p), abs(self.freq(p))))
                    found[wide] = narrow
                    used |= {wide, narrow}
        for wide in sorted(kept, reverse=True):
            mirror = (self.points - wide) % self.points
            if wide not in used and mirror not in used and wide > mirror and mirror in kept:
                if 2 * self.width(wide) < self.reach:
                    found[wide] = mirror
                    used |= {wide, mirror}
        close = [p for p in kept if p not in used and p // self.planes == edge // self.planes]
        close = [p for p in close if self.width(p) <= self.reach - 4]
        if close:
            found[max(close, key=self.width)] = edge
        return found

    def shared_rows(self, n, pairs, kept, holders):
        zone, slots, planes = n // 4, self.slots, self.planes
        taken = set(pairs.values())
        owned = [[] for _ in range(n)]
        for group in (holders[:zone], holders[zone:]):
            waiting = []
            others = []
            for h in group:
                other = h + zone if h < zone else h - zone
                others.append(other)
                rows = [(p, pairs.get(p)) for p in range(h * planes, (h + 1) * planes) if p not in taken]
                rows.sort(key=lambda row: row[1] is None)
                owned[h] = rows[:slots]
                owned[other] = rows[slots : 2 * slots - 1]
                waiting += rows[2 * slots - 1 :]
                if len(owned[h]) < slots:
                    return None
            for other in others:
                while len(owned[other]) < slots - 1 and waiting:
                    owned[other].append(waiting.pop(0))
            if waiting or any(len(owned[other]) != slots - 1 for other in others):
                return None
        return owned


def cell_order(count, share):
    return np.array([o * share + k for k in range(share) for o in range(count)])


def transform_tables(n, points, count, share):
    half = points // 2
    keep = np.arange(half)
    keep = np.where(keep < half // 2, keep, keep - half)
    cell = np.arange(points)

    def waves(freq):
        angle = 2.0 * np.pi * ((freq[:, None] * cell[None, :]) % points) / points
        return np.cos(angle), np.sin(angle)

    cos, sin = waves(keep)
    plane = np.array(Plan(n, points).order)
    cos_x, sin_x = waves(np.where(2 * plane < points, plane, plane - points))
    freq = np.where(2 * cell < points, cell, cell - points)
    slope = gradient_scale * np.where(2 * freq == -points, 0, freq) / points
    cos_all, sin_all = waves(cell)
    derivative = ((cos_all + 1j * sin_all) * slope[None, :] * 1j) @ (cos_all - 1j * sin_all) / points
    derivative = derivative.real
    basis = cos_all + sin_all
    order = cell_order(count, share)
    lefts = np.stack([
        table_for_left(t) for t in (
            np.concatenate([cos.T, sin.T], 1),
            np.concatenate([cos, sin], 0),
            np.concatenate([cos_x.T, sin_x.T], 1),
            np.concatenate([cos_x, sin_x], 0),
            basis[order],
            derivative[order][:, order],
            basis[:, order],
            derivative,
            basis,
        )
    ])
    rights = np.concatenate([table_for_right(basis), table_for_right(derivative.T)], 1)
    z_out = table_for_right(np.block([[cos, sin], [-sin, cos]]))
    z_in = table_for_right(np.block([[cos.T, -sin.T], [sin.T, cos.T]]))
    plain = basis[:, order][None].astype(np.float32)
    return lefts, rights, z_out, z_in, plain


def kernel(
    n, peers, bands, points, iters, hidden,
    coefficients, potential_in, external_in, core_in, rotations_in, mlp_first_in, mlp_second_in,
    lefts_in, rights_in, z_out_in, z_in_in, plain_in,
    low_out, high_out, out,
    low_here, high_here, rotations, mlp_in, mlp_out,
    tables_l, tables_r, table_out, table_in, table_plain, given, potential, external, core, raw, forward, vectors, mask, kinetic,
    sent, got, level_r, level_i, edge_r, edge_i, space_of, fixed_out, fixed_got,
    gram_tile, gram_got, fresh, returned, fixed_new, fixed_back,
    parts, coulomb, staged, arrived, slope_sent, slope_got, wave_sent, wave_got, change, network,
    load_sem, first_send, first_recv, fixed_sem, send_sem, recv_sem, gram_sem, last_send, last_recv, back_sem, dens_sem, field_sem, out_sem,
    share_sem,
):
    me = lax.axis_index("grid")
    band = lax.axis_index("band")
    half = points // 2
    reach = half // 2
    slots = half // n
    planes = points // n
    zone = n // 4
    plan = Plan(n, points)
    base_rows, extra = plan.base, plan.extra
    home, edge = plan.home, plan.edge
    edge_tile, edge_row = edge // 8 * 8, edge % 8
    zero = plan.zero * planes
    sub = math.gcd(peers, planes)
    share = planes // sub
    count = n * sub
    block = share * share
    seat = lax.rem(band, sub)
    team = band - seat
    rank = me * sub + seat
    holder = jnp.logical_or(me < zone, me >= n - zone)

    def one_of(devices):
        found = me == -1
        for d in devices:
            found = jnp.logical_or(found, me == d)
        return found

    def pick(values):
        found = jnp.int32(values[0])
        for d in range(1, n):
            if values[d] != values[0]:
                found = jnp.where(me == d, values[d], found)
        return found

    def at(grid, other=None):
        return {"band": band if other is None else other, "grid": grid}

    def remote(source, target, send, recv, device):
        return pltpu.make_async_remote_copy(
            src_ref=source, dst_ref=target, send_sem=send, recv_sem=recv, device_id=device, device_id_type=MESH
        )

    def drained(ref, sem):
        pltpu.make_async_copy(ref, ref, sem).wait()

    barrier = pltpu.get_barrier_semaphore()

    @pl.loop(1, n)
    def _(i):
        for k in range(sub):
            pl.semaphore_signal(barrier, inc=1, device_id=at(lax.rem(me + i, n), team + k), device_id_type=MESH)

    for k in range(1, sub):
        pl.semaphore_signal(barrier, inc=1, device_id=at(me, team + lax.rem(seat + k, sub)), device_id_type=MESH)

    for i in range(1, peers):
        other = lax.rem(band + i, peers)

        @pl.when(other - lax.rem(other, sub) != team)
        def _():
            pl.semaphore_signal(barrier, inc=1, device_id=at(me, other), device_id_type=MESH)

    loads = []
    for b in range(bands):
        for p in range(2):
            k = 2 * (2 * b + p)
            loads.append(pltpu.make_async_copy(
                coefficients.at[b, p, :, pl.ds(0, reach + 8)], given.at[b, p, :, pl.ds(0, reach + 8)], load_sem.at[k]
            ))
            loads.append(pltpu.make_async_copy(
                coefficients.at[b, p, :, pl.ds(points - reach, reach)],
                given.at[b, p, :, pl.ds(reach + 8, reach)],
                load_sem.at[k + 1],
            ))
    base = 4 * bands
    tables = [
        pltpu.make_async_copy(source, target, load_sem.at[base + 3 + k])
        for k, (source, target) in enumerate((
            (lefts_in, tables_l), (z_out_in, table_out), (z_in_in, table_in), (rights_in, tables_r), (plain_in, table_plain)
        ))
    ]
    late = [
        pltpu.make_async_copy(potential_in, potential, load_sem.at[base]),
        pltpu.make_async_copy(external_in, external, load_sem.at[base + 1]),
        pltpu.make_async_copy(core_in, core, load_sem.at[base + 2]),
        pltpu.make_async_copy(rotations_in, rotations, load_sem.at[base + 3 + len(tables)]),
        pltpu.make_async_copy(mlp_first_in, mlp_in, load_sem.at[base + 4 + len(tables)]),
        pltpu.make_async_copy(mlp_second_in, mlp_out, load_sem.at[base + 5 + len(tables)]),
    ]
    needed = jnp.logical_or(holder, me == zone)

    @pl.when(needed)
    def _():
        for copy in loads:
            copy.start()

    for copy in tables + late:
        copy.start()

    lanes = lax.broadcasted_iota(jnp.int32, (1, points), 1)
    tile_lane = lax.broadcasted_iota(jnp.int32, (8, points), 1)
    tile_row = lax.broadcasted_iota(jnp.int32, (8, points), 0)
    sign = jnp.where(lanes < half, -1.0, 1.0).astype(F32)
    alone = jnp.where(lax.rem(lanes, half) == 0, 1.0, 0.0).astype(F32)

    def quarter_turn(k):
        k = lax.rem(k, 4)
        c = jnp.where(k == 0, 1.0, jnp.where(k == 2, -1.0, 0.0)).astype(F32)
        s = jnp.where(k == 1, 1.0, jnp.where(k == 3, -1.0, 0.0)).astype(F32)
        return c, s

    z_c, z_s = quarter_turn(lanes)
    y_c, y_s = quarter_turn(me * planes + lax.broadcasted_iota(jnp.int32, (planes, 1), 0))

    def turn(value):
        return pltpu.roll(value, half, 1) * sign

    def frequency(place):
        return jnp.where(2 * place < points, place, place - points)

    row = lax.broadcasted_iota(jnp.int32, (half, points), 0)
    gy = jnp.where(row < reach, row, row - half)
    lane = lax.rem(lanes, half)
    lane_far = lax.rem(lane + reach, half)

    def centred(value):
        return jnp.where(value < reach, value, value - half)

    def swap(value):
        return jnp.where(lane < reach, pltpu.roll(value, points - reach, 1), pltpu.roll(value, reach, 1))

    gz, gz_far = centred(lane), centred(lane_far)
    flat, flat_far = gy * gy + gz * gz, gy * gy + gz_far * gz_far
    outer = []
    for x in range(slots):
        rows = [plan.owned[d][x] if x < len(plan.owned[d]) else (None, None) for d in range(n)]
        gx = pick([points if wide is None else plan.freq(wide) for wide, _ in rows])
        gx_far = pick([points if narrow is None else plan.freq(narrow) for _, narrow in rows])
        outer.append(gx * gx + gz * gz > reach * reach)
        squared = jnp.where(outer[x], flat_far + gx_far * gx_far, flat + gx * gx)
        if x == plan.home_slot:
            spot = jnp.logical_and(row == 0, me == home)
            where = jnp.logical_and(outer[x], lane_far < 4) if plan.home_part else lane < 4
            squared = jnp.where(jnp.logical_and(spot, where), reach * reach, squared)
        mask[x] = jnp.where(16 * squared <= points * points, 1.0, 0.0).astype(F32)
        kinetic[x] = kinetic_scale * squared.astype(F32) / (points * points)
    edge_r[...] = jnp.zeros_like(edge_r)
    edge_i[...] = jnp.zeros_like(edge_i)

    @pl.when(needed)
    def _():
        for copy in loads:
            copy.wait()

    def packed(b, x):
        found = []
        for p in range(2):
            found.append(jnp.concatenate([given[b, p, x, 0:reach], given[b, p, x, reach + 8 : half + 8]], 0))
        real, imag = found
        low = jnp.where(lanes < reach, real, pltpu.roll(real, half, 1))
        high = jnp.where(lanes < half + reach, pltpu.roll(imag, half, 1), imag)
        return jnp.where(lanes < half, low, high)

    @pl.when(holder)
    def _():
        for b in range(bands):
            for x in range(planes):
                forward[b, x] = packed(b, x)

    if extra:
        @pl.when(jnp.logical_not(one_of(extra)))
        def _():
            for b in range(bands):
                raw[0, b, base_rows] = jnp.zeros((half, points), F32)

    def lane_to(value, start, target):
        moved = pltpu.roll(value, (target - start) % points, 1)
        return jnp.where(jnp.logical_and(tile_lane == target, tile_row == 0), moved, 0.0)

    @pl.when(me == 0)
    def _():
        for b in range(bands):
            total = None
            for p in range(2):
                z_point = lane_to(given[b, p, 0, 0:8], reach, 2 + half * p)
                y_point = lane_to(given[b, p, 0, reach : reach + 8], 0, 3 + half * p)
                total = z_point + y_point if total is None else total + z_point + y_point
            fixed_out[b] = total

    @pl.when(me == zone)
    def _():
        for b in range(bands):
            fixed_out[b] = lane_to(given[b, 0, 0, 0:8], 0, 1) + lane_to(given[b, 1, 0, 0:8], 0, 1 + half)

    pl.semaphore_wait(barrier, count - 1 + peers - sub)

    def first(b, h, entry):
        x, d, i, part = entry
        target, sem = raw.at[part, b, i], first_recv.at[part, b, i]
        if d == h:
            return pltpu.make_async_copy(forward.at[b, x], target, sem)
        return remote(forward.at[b, x], target, first_send.at[b, x], sem, at(d))

    def distribute(b):
        for h, entries in plan.sends.items():
            @pl.when(me == h)
            def _():
                for entry in sorted(entries, key=lambda e: e[1] == h):
                    first(b, h, entry).start()

    def gather(b):
        for x in range(slots):
            for part in range(2):
                devices = [
                    d for d in range(n) if x < len(plan.owned[d]) and plan.owned[d][x][part] is not None
                ]
                if len(devices) == n:
                    drained(raw.at[part, b, x], first_recv.at[part, b, x])
                elif devices:
                    @pl.when(one_of(devices))
                    def _():
                        drained(raw.at[part, b, x], first_recv.at[part, b, x])

    def merge(b):
        for x in range(slots):
            devices = [d for d in range(n) if x < len(plan.owned[d]) and plan.owned[d][x][1] is not None]
            if devices:
                @pl.when(one_of(devices))
                def _():
                    raw[0, b, x] = jnp.where(outer[x], swap(raw[1, b, x]), raw[0, b, x])

    def fixed(place):
        return remote(fixed_out, fixed_got.at[place], fixed_sem.at[0], fixed_sem.at[1 + place], at(home))

    @pl.when(me == 0)
    def _():
        fixed(0).start()

    @pl.when(me == zone)
    def _():
        fixed(1).start()

    def part_copy(place, target, part):
        rows = pl.ds(0, base_rows) if part == 0 else pl.ds(base_rows, 1)
        return remote(
            sent.at[place, target, rows], got.at[place, me, rows],
            send_sem.at[part, place], recv_sem.at[part, place], at(target),
        )

    def own_copy(place, part):
        rows = pl.ds(0, base_rows) if part == 0 else pl.ds(base_rows, 1)
        return pltpu.make_async_copy(sent.at[place, me, rows], got.at[place, me, rows], recv_sem.at[part, place])

    def is_extra(device):
        return jnp.logical_or(device < zone, device >= n - zone)

    if extra:
        assert extra == list(range(zone)) + list(range(n - zone, n))

    def exchange(place, to_cells):
        @pl.loop(1, n)
        def _(i):
            target = lax.rem(me + i, n)
            part_copy(place, target, 0).start()
            if extra:
                @pl.when(is_extra(me if to_cells else target))
                def _():
                    part_copy(place, target, 1).start()

        own_copy(place, 0).start()
        if extra:
            @pl.when(is_extra(me))
            def _():
                own_copy(place, 1).start()

    def received(place, to_cells):
        drained(got.at[place, pl.ds(0, n), pl.ds(0, base_rows)], recv_sem.at[0, place])
        if extra and to_cells:
            drained(got.at[place, pl.ds(0, len(extra)), base_rows], recv_sem.at[1, place])
        elif extra:
            @pl.when(is_extra(me))
            def _():
                drained(got.at[place, pl.ds(0, n), base_rows], recv_sem.at[1, place])

    def all_sent(place, to_cells):
        drained(sent.at[place, pl.ds(0, n - 1), pl.ds(0, base_rows)], send_sem.at[0, place])
        if extra and to_cells:
            @pl.when(is_extra(me))
            def _():
                drained(sent.at[place, pl.ds(0, n - 1), base_rows], send_sem.at[1, place])
        elif extra:
            @pl.when(is_extra(me))
            def _():
                drained(sent.at[place, pl.ds(0, len(extra) - 1), base_rows], send_sem.at[1, place])

            @pl.when(jnp.logical_not(is_extra(me)))
            def _():
                drained(sent.at[place, pl.ds(0, len(extra)), base_rows], send_sem.at[1, place])

    def outward(value_of, place):
        stacked = []
        for x in range(slots):
            value = value_of(x)
            stacked.append(jnp.concatenate([value, turn(value)], 0))
        full = left(tables_l[0], jnp.concatenate(stacked, 1))
        for x in range(slots):
            sent[place, :, x] = full[:, x * points : (x + 1) * points].reshape(n, planes, points)
        exchange(place, True)

    def space(place, action, order=range(planes)):
        for wide, narrow, plane in plan.mixed:
            value = got[place, wide // slots, wide % slots]
            far = gz * gz + plan.freq(plane) ** 2 > reach * reach
            got[place, narrow // slots, narrow % slots] = swap(jnp.where(far, value, 0.0))
            got[place, wide // slots, wide % slots] = jnp.where(far, 0.0, value)
        levels = right(got[place].reshape(half * planes, points), table_out[...])
        level_r[...] = levels[:, :points]
        level_i[...] = levels[:, points:]
        special = got[place, edge // slots, edge % slots]

        def lane_of(k):
            return jnp.broadcast_to(special[:, k : k + 1], (planes, points))

        minus_r, plus_r, z_r, y_r = [lane_of(k) for k in range(4)]
        minus_i, plus_i, z_i, y_i = [lane_of(half + k) for k in range(4)]
        level_r[edge * planes : (edge + 1) * planes, :] = minus_r + plus_r
        level_i[edge * planes : (edge + 1) * planes, :] = minus_i + plus_i
        level_r[zero : zero + planes, :] += z_r * z_c - z_i * z_s + y_r * y_c - y_i * y_s
        level_i[zero : zero + planes, :] += z_r * z_s + z_i * z_c + y_r * y_s + y_i * y_c
        edge_r[pl.ds(edge_row, planes, stride=8), :] = 2.0 * plus_r
        edge_i[pl.ds(edge_row, planes, stride=8), :] = 2.0 * plus_i

        def without(value, y, extra):
            tile = value[edge_tile : edge_tile + 8] - extra[pl.ds(pl.multiple_of(y * 8, 8), 8), :]
            return jnp.concatenate([value[:edge_tile], tile, value[edge_tile + 8 :]], 0)

        for y in order:
            real = level_r[pl.ds(y, half, stride=planes), :]
            imag = level_i[pl.ds(y, half, stride=planes), :]
            stacked = jnp.concatenate(
                [
                    jnp.concatenate([real, imag], 1),
                    jnp.concatenate([-without(imag, y, edge_i), without(real, y, edge_r)], 1),
                ],
                0,
            )
            action(y, left(tables_l[2], stacked))

    def spectrum(index, place):
        def action(y, wave):
            space_of[index, y] = wave
            field = potential[y]
            product = wave * jnp.concatenate([field, field], 1)
            both = left(tables_l[3], product)
            cos_r, cos_i = both[:half, :points], both[:half, points:]
            sin_r, sin_i = both[half:, :points], both[half:, points:]
            level_r[pl.ds(y, half, stride=planes), :] = cos_r + sin_i
            level_i[pl.ds(y, half, stride=planes), :] = cos_i - sin_r
            edge_r[8 * (planes + y) : 8 * (planes + y) + 8, :] = cos_r[edge_tile : edge_tile + 8] - sin_i[edge_tile : edge_tile + 8]
            edge_i[8 * (planes + y) : 8 * (planes + y) + 8, :] = cos_i[edge_tile : edge_tile + 8] + sin_r[edge_tile : edge_tile + 8]

        space(place, action)
        both = jnp.concatenate([level_r[...], level_i[...]], 1)
        sent[place + bands] = right(both, table_in[...]).reshape(n, slots, planes, points)

        def total(value):
            return jnp.sum(value, 1, keepdims=True)

        plus_r = edge_r[pl.ds(8 * planes + edge_row, planes, stride=8), :]
        plus_i = edge_i[pl.ds(8 * planes + edge_row, planes, stride=8), :]
        zero_r, zero_i = level_r[zero : zero + planes, :], level_i[zero : zero + planes, :]
        line_r, line_i = total(zero_r), total(zero_i)
        found = [
            total(plus_r), total(zero_r * z_c + zero_i * z_s), line_r * y_c + line_i * y_s,
            total(plus_i), total(zero_i * z_c - zero_r * z_s), line_i * y_c - line_r * y_s,
        ]
        special = sent[place + bands, edge // slots, edge % slots] * alone
        for k, value in enumerate(found):
            special = jnp.where(lanes == (k + 1 if k < 3 else half + k - 2), value, special)
        sent[place + bands, edge // slots, edge % slots] = special
        for wide, narrow, plane in plan.mixed:
            far = gz * gz + plan.freq(plane) ** 2 > reach * reach
            value = sent[place + bands, narrow // slots, narrow % slots]
            kept = sent[place + bands, wide // slots, wide % slots]
            sent[place + bands, wide // slots, wide % slots] = jnp.where(far, swap(value), kept)
        exchange(place + bands, False)

    def inward(place):
        columns = [got[place, :, x].reshape(points, points) for x in range(slots)]
        both = left(tables_l[1], jnp.concatenate(columns, 1))
        found = []
        for x in range(slots):
            part = both[:, x * points : (x + 1) * points]
            found.append(part[:half] - turn(part[half:]))
        return found

    grams = {}

    def measure(p):
        for q in range(p + 1):
            u = vectors[p // bands, p % bands].reshape(slots * half, points)
            v = vectors[q // bands, q % bands].reshape(slots * half, points)
            grams[q, p] = jnp.sum(u * v, 0, keepdims=True)

    tables[0].wait()
    for b in range(bands):
        distribute(b)
        gather(b)
        if b == 0:
            @pl.when(me == home)
            def _():
                fixed(0).wait_recv()
                fixed(1).wait_recv()
                for c in range(bands):
                    fixed_got[0, c] = fixed_got[0, c] + fixed_got[1, c]

        @pl.when(me == home)
        def _():
            clean = jnp.where(tile_row == 0, alone, 1.0)
            tile = raw[plan.home_part, b, plan.home_slot, 0:8, :]
            raw[plan.home_part, b, plan.home_slot, 0:8, :] = tile * clean + fixed_got[0, b]

        merge(b)
        vectors[0, b] = jnp.where(mask[...] > 0.0, raw[0, b], 0.0)
        outward(lambda x: vectors[0, b, x], b)

    late[0].wait()
    late[3].wait()
    tables[1].wait()
    tables[2].wait()
    size = (iters + 1) * bands
    for b in range(bands):
        measure(b)
    for t in range(iters):
        for b in range(bands):
            received(2 * t * bands + b, True)
            spectrum(t * bands + b, 2 * t * bands + b)
        for b in range(bands):
            place = (2 * t + 1) * bands + b
            received(place, False)
            found = inward(place)
            for x in range(slots):
                value = kinetic[x] * vectors[t, b, x] + found[x] * (1.0 / points**3)
                vectors[t + 1, b, x] = jnp.where(mask[x] > 0.0, value, 0.0)
            last = (t + 1) * bands + b == size - 1
            if last:
                measure(size - 1)
                tile = jnp.zeros((1, points), F32)
                keys = sorted(grams)
                for k, key in enumerate(keys):
                    tile = jnp.where(lanes == k, jnp.sum(grams[key], 1, keepdims=True), tile)
                gram_tile[...] = tile

                def gram_copy(target):
                    return remote(gram_tile, gram_got.at[me], gram_sem.at[0], gram_sem.at[1], at(target))

                @pl.loop(1, n)
                def _(i):
                    gram_copy(lax.rem(me + i, n)).start()

                pltpu.make_async_copy(gram_tile, gram_got.at[me], gram_sem.at[1]).start()
            outward(lambda x: vectors[t + 1, b, x], (2 * t + 2) * bands + b)
            if not last:
                measure((t + 1) * bands + b)

    drained(gram_got, gram_sem.at[1])
    sums = jnp.sum(gram_got[...], 0)
    gram = {}
    for k, (p, q) in enumerate(keys):
        gram[p, q] = gram[q, p] = sums[:, k : k + 1]

    def product(u, v):
        total = None
        for p, a in enumerate(u):
            inner = None
            for q, c in enumerate(v):
                if a is not None and c is not None:
                    term = c * gram[p, q]
                    inner = term if inner is None else inner + term
            if inner is not None:
                total = a * inner if total is None else total + a * inner
        return total

    def combine(terms):
        result = []
        for p in range(size):
            value = None
            for scale, u in terms:
                if u[p] is not None:
                    value = scale * u[p] if value is None else value + scale * u[p]
            result.append(value)
        return result

    one = jnp.ones((1, 1), F32)
    current = [[one if p == b else None for p in range(size)] for b in range(bands)]
    for t in range(iters):
        moved = []
        for b in range(bands):
            pushed = [None] * bands + current[b][: size - bands]
            factor = 1.0 + step_size * (product(current[b], pushed) / (product(current[b], current[b]) + epsilon))
            moved.append(combine([(factor, current[b]), (-step_size, pushed)]))
        following = []
        for b in range(bands):
            rotated = combine([(rotations[t, b, c], moved[c]) for c in range(bands)])
            scale = lax.rsqrt(jnp.maximum(product(rotated, rotated), 0.0) + epsilon)
            following.append([None if value is None else scale * value for value in rotated])
        current = following

    for b in range(bands):
        for x in range(slots):
            fresh[b, x] = sum(current[b][p] * vectors[p // bands, p % bands, x] for p in range(size))

    place = 2 * iters * bands
    for b in range(bands - 1):
        received(place + b, True)

        def keep(y, wave):
            space_of[iters * bands + b, y] = wave

        space(place + b, keep)

    for y in range(planes):
        for b in range(bands):
            known = [space_of[p, y] for p in range(size - 1)]
            mixed = [sum(current[b][p] * known[p] for p in range(size - 1)) for b in range(bands)]
        for b in range(bands):
            space_of[b, y] = mixed[b]

    def density_copy(i, y):
        target = lax.rem(band + i, peers)
        return remote(
            parts.at[band, y], parts.at[band, y], dens_sem.at[0, i - 1, y], dens_sem.at[1, i - 1, y], at(me, target)
        )

    received(place + bands - 1, True)

    def density(y, wave):
        total = None
        for b in range(bands):
            value = space_of[b, y] + current[b][size - 1] * wave
            square = value * value
            square = square[:, :points] + square[:, points:]
            total = square if total is None else total + square
        parts[band, y] = total * (2.0 / (bands * peers))
        for i in range(1, peers):
            @pl.when(lax.rem(lax.rem(band + i, peers), sub) == lax.div(y, share))
            def _():
                density_copy(i, y).start()

    turns = [lax.rem(seat + 1 + m // share, sub) * share + m % share for m in range(planes)]
    space(place + bands - 1, density, turns)

    late[2].wait()
    late[1].wait()
    late[4].wait()
    late[5].wait()
    tables[3].wait()
    tables[4].wait()
    for i in range(1, peers):
        for y in range(planes):
            @pl.when(lax.rem(lax.rem(band + i, peers), sub) == y // share)
            def _():
                density_copy(i, y).wait_send()

            @pl.when(seat == y // share)
            def _():
                density_copy(i, y).wait_recv()

    first_plane = seat * share
    whole = []
    for k in range(share):
        total = core[first_plane + k]
        for other in range(peers):
            total = total + parts[other, first_plane + k]
        whole.append(total)
    varying = [value - level_shift for value in whole]

    pieces = 2 if share % 2 == 0 else 1
    piece = block // pieces
    width = share // pieces

    def field_exchange(stage, part, source, target):
        k = stage * pieces + part

        def copy(other, seat_of):
            return remote(
                source.at[pl.ds((other * sub + seat_of) * block + part * piece, piece)],
                target.at[pl.ds(rank * block + part * piece, piece)],
                field_sem.at[0, k],
                field_sem.at[1, k],
                at(other, team + seat_of),
            )

        @pl.loop(1, n)
        def _(i):
            for seat_of in range(sub):
                copy(lax.rem(me + i, n), seat_of).start()

        for i in range(1, sub):
            copy(me, lax.rem(seat + i, sub)).start()

        own = pl.ds(rank * block + part * piece, piece)
        pltpu.make_async_copy(source.at[own], target.at[own], field_sem.at[1, k]).start()

    def field_drained(stage, part, ref):
        drained(ref.at[pl.ds(0, count * piece)], field_sem.at[1, stage * pieces + part])

    level = left(tables_l[8], jnp.concatenate(varying, 1))
    level = jnp.concatenate([level[:, k * points : (k + 1) * points] for k in range(share)], 0)
    level = right(level, tables_r[:, :points])
    for k in range(share):
        staged[pl.ds(k, points, stride=share), :] = level[k * points : (k + 1) * points]
    for part in range(pieces):
        field_exchange(0, part, staged, arrived)

    def returning(b, d, remote_only=False):
        found = []
        for i, planes_of in enumerate(plan.owned[d]):
            for part, plane in enumerate(planes_of):
                if plane is None:
                    continue
                h, x = plane // planes, plane % planes
                if h != d:
                    found.append(remote(
                        fresh.at[b, i], returned.at[b, x], last_send.at[b, i, part], last_recv.at[b, x], at(h)
                    ))
                elif not remote_only:
                    found.append(pltpu.make_async_copy(fresh.at[b, i], returned.at[b, x], last_recv.at[b, x]))
        return found

    def back(target, sem):
        return remote(fixed_new, fixed_back, back_sem.at[sem], back_sem.at[2], at(target))

    for d in range(n):
        @pl.when(me == d)
        def _():
            for b in range(bands):
                for copy in returning(b, d):
                    copy.start()

    @pl.when(me == home)
    def _():
        for b in range(bands):
            tile = fresh[b, plan.home_slot, 0:8, :]
            fixed_new[b] = swap(tile) if plan.home_part else tile
        back(0, 0).start()
        back(zone, 1).start()

    columns = jnp.concatenate(varying, 1)
    change_x = left(tables_l[7], columns)
    change_z = right(jnp.concatenate(varying, 0), tables_r[:, points:])
    for k in range(share):
        cx = change_x[:, k * points : (k + 1) * points]
        cz = change_z[k * points : (k + 1) * points]
        change[k] = cx * cx + cz * cz
    gy_all = frequency(lax.broadcasted_iota(jnp.int32, (points, points), 0))
    gz_all = frequency(lax.broadcasted_iota(jnp.int32, (points, points), 1))
    flat_all = gy_all * gy_all + gz_all * gz_all
    for i in range(share):
        gx = frequency(rank * share + i)
        squared = flat_all + gx * gx
        coulomb[:, i * points : (i + 1) * points] = jnp.where(
            squared > 0, (coulomb_scale / points) / jnp.maximum(squared, 1).astype(F32), 0.0
        )

    def column(ref, i):
        return jnp.concatenate([ref[pl.ds(i * share + k, count, stride=block), :] for k in range(share)], 0)

    def plane_of(ref, k):
        return jnp.concatenate([ref[pl.ds(i * share + k, count, stride=block), :] for i in range(share)], 0)

    def scattered(ref, part, value):
        for j in range(width):
            for k in range(share):
                ref[pl.ds((part * width + j) * share + k, count, stride=block), :] = value[
                    k * count : (k + 1) * count, j * points : (j + 1) * points
                ]

    columns = []
    for part in range(pieces):
        field_drained(0, part, arrived)
        columns.append(jnp.concatenate([column(arrived, part * width + j) for j in range(width)], 1))
        scattered(slope_sent, part, left(tables_l[5], columns[part]))
        field_exchange(1, part, slope_sent, slope_got)
    for part in range(pieces):
        weight = coulomb[:, part * width * points : (part + 1) * width * points]
        scattered(wave_sent, part, left(tables_l[4], weight * full_dot(table_plain[0], columns[part])))
        field_exchange(2, part, wave_sent, wave_got)

    def to_cells(ref):
        value = left(tables_l[6], jnp.concatenate([plane_of(ref, k) for k in range(share)], 1))
        value = jnp.concatenate([value[:, k * points : (k + 1) * points] for k in range(share)], 0)
        return right(value, tables_r[:, :points])

    @pl.when(holder)
    def _():
        for x in range(planes):
            narrow = [p // planes for p in sorted(plan.narrow) if p % planes == x]
            gx = frequency(me * planes + x)
            inside = 16 * (flat + gx * gx) <= points * points
            for b in range(bands):
                drained(returned.at[b, x], last_recv.at[b, x])
                value = returned[b, x]
                if narrow:
                    value = jnp.where(one_of(narrow), swap(value), value)
                value = jnp.where(inside, value, 0.0)
                swapped = pltpu.roll(value, half, 1)
                real = jnp.where(lanes < reach, value, jnp.where(lanes >= points - reach, swapped, 0.0))
                imag = jnp.where(lanes < reach, swapped, jnp.where(lanes >= points - reach, value, 0.0))
                for p, found in enumerate((real, imag)):
                    low_here[b, p, x, 0:reach] = found[:reach]
                    low_here[b, p, x, reach : reach + 8] = jnp.zeros((8, points), F32)
                    high_here[b, p, x] = found[reach:]

    @pl.when(jnp.logical_not(holder))
    def _():
        low_here[...] = jnp.zeros_like(low_here)
        high_here[...] = jnp.zeros_like(high_here)

    @pl.when(me == 0)
    def _():
        back(0, 0).wait_recv()
        for b in range(bands):
            for p in range(2):
                z_point = lane_to(fixed_back[b], 2 + half * p, reach)
                low_here[b, p, 0, 0:8] = low_here[b, p, 0, 0:8] + z_point
                low_here[b, p, 0, reach : reach + 8] = lane_to(fixed_back[b], 3 + half * p, 0)

    @pl.when(me == zone)
    def _():
        back(0, 0).wait_recv()
        for b in range(bands):
            for p in range(2):
                low_here[b, p, 0, 0:8] = lane_to(fixed_back[b], 1 + half * p, 0)

    leaving = [
        pltpu.make_async_copy(low_here, low_out, out_sem.at[0]),
        pltpu.make_async_copy(high_here, high_out, out_sem.at[1]),
    ]
    for copy in leaving:
        copy.start()

    for part in range(pieces):
        field_drained(1, part, slope_got)
    change_y = to_cells(slope_got) * (1.0 / (points * points))
    for k in range(share):
        cy = change_y[k * points : (k + 1) * points]
        gradient = jnp.sqrt(change[k] + cy * cy)
        dens = core[first_plane + k]
        for other in range(peers):
            dens = dens + parts[other, first_plane + k]
        root = jnp.exp(jnp.log(dens) * (1.0 / 3.0))
        root = root - (root * root * root - dens) / (3.0 * root * root)
        reduced = gradient / (reduced_scale * dens * root)
        bounded = reduced / (1.0 + reduced)

        for first_row in range(0, points, points // 2):
            r = root[first_row : first_row + points // 2]
            q = bounded[first_row : first_row + points // 2]

            def unit(h, total):
                return total + mlp_out[h] * jnp.tanh(mlp_in[0, h] * r + mlp_in[1, h] * q + mlp_in[2, h])

            enhance = lax.fori_loop(0, hidden, unit, jnp.ones_like(r), unroll=8)
            rows = pl.ds(first_row, points // 2)
            network[k, rows] = external[first_plane + k, rows] - exchange_scale * r * enhance

    for part in range(pieces):
        field_drained(2, part, wave_got)
    hartree = to_cells(wave_got)

    def shared(i, seat_of, k):
        return remote(
            network.at[k], out.at[seat_of * share + k],
            share_sem.at[0, i - 1, k], share_sem.at[1, i - 1, k], at(me, team + lax.rem(seat + i, sub)),
        )

    for k in range(share):
        network[k] = network[k] + hartree[k * points : (k + 1) * points]
        for i in range(1, sub):
            shared(i, seat, k).start()
        leaving.append(pltpu.make_async_copy(network.at[k], out.at[first_plane + k], out_sem.at[2 + k]))
        leaving[-1].start()

    for h, entries in plan.sends.items():
        @pl.when(me == h)
        def _():
            for b in range(bands):
                for entry in entries:
                    if entry[1] != h:
                        first(b, h, entry).wait_send()

    for d in range(n):
        @pl.when(me == d)
        def _():
            for b in range(bands):
                for copy in returning(b, d, True):
                    copy.wait_send()

    @pl.when(me == 0)
    def _():
        fixed(0).wait_send()

    @pl.when(me == zone)
    def _():
        fixed(1).wait_send()

    @pl.when(me == home)
    def _():
        back(0, 0).wait_send()
        back(zone, 1).wait_send()

    for k in range((2 * iters + 1) * bands):
        all_sent(k, k // bands % 2 == 0)
    drained(gram_got.at[pl.ds(0, n - 1)], gram_sem.at[0])
    for stage, ref in enumerate((staged, slope_sent, wave_sent)):
        for part in range(pieces):
            drained(ref.at[pl.ds(0, (count - 1) * piece)], field_sem.at[0, stage * pieces + part])
    for i in range(1, sub):
        for k in range(share):
            shared(i, seat, k).wait_send()
            shared(i, lax.rem(seat + sub - i, sub), k).wait_recv()
    for copy in leaving:
        copy.wait()


def spread(bands, low, high, field, new, out, low_here, high_here, field_here, zeros, in_sem, out_sem):
    edge, width = low.shape[3], zeros.shape[2]
    arrivals = []
    for b in range(bands):
        arrivals.append(pltpu.make_async_copy(low.at[b], low_here.at[b], in_sem.at[2 * b]))
        arrivals.append(pltpu.make_async_copy(high.at[b], high_here.at[b], in_sem.at[2 * b + 1]))
    arrivals.append(pltpu.make_async_copy(field, field_here, in_sem.at[2 * bands]))
    for copy in arrivals:
        copy.start()
    zeros[...] = jnp.zeros_like(zeros)
    leaving = []
    for b in range(bands):
        leaving.append(pltpu.make_async_copy(zeros, new.at[b, :, :, pl.ds(edge, width)], out_sem.at[3 * b]))
        leaving[-1].start()
    for k, copy in enumerate(arrivals):
        copy.wait()
        b = k // 2
        if b == bands:
            place, source = out, field_here
        elif k % 2 == 0:
            place, source = new.at[b, :, :, pl.ds(0, edge)], low_here.at[b]
        else:
            place, source = new.at[b, :, :, pl.ds(edge + width, high.shape[3])], high_here.at[b]
        leaving.append(pltpu.make_async_copy(source, place, out_sem.at[3 * b + 1 + k % 2 if b < bands else 3 * bands]))
        leaving[-1].start()
    for copy in leaving:
        copy.wait()


def body(coefficients, potential, external, core_density, rotations, mlp_in, mlp_out):
    n, peers = lax.axis_size("grid"), lax.axis_size("band")
    bands, _, planes, points, _ = coefficients.shape
    iters = rotations.shape[0]
    half = points // 2
    slots = half // n
    sub = math.gcd(peers, planes)
    share = planes // sub
    count = n * sub
    rows = count * share * share
    stages = (2 * iters + 1) * bands
    size = (iters + 1) * bands
    lefts, rights, z_out, z_in, plain = transform_tables(n, points, count, share)
    tables = (lefts, rights, z_out, z_in, plain)
    any_space = pl.BlockSpec(memory_space=pl.ANY)
    dma = pltpu.SemaphoreType.DMA

    def store(*shape):
        return pltpu.VMEM(shape, F32)

    low, high, new_potential = pl.pallas_call(
        functools.partial(kernel, n, peers, bands, points, iters, mlp_out.shape[0]),
        out_shape=(
            jax.ShapeDtypeStruct((bands, 2, planes, half // 2 + 8, points), F32),
            jax.ShapeDtypeStruct((bands, 2, planes, half // 2, points), F32),
            jax.ShapeDtypeStruct((planes, points, points), F32),
        ),
        in_specs=[any_space] * (7 + len(tables)),
        out_specs=(any_space, any_space, any_space),
        scratch_shapes=[
            store(bands, 2, planes, half // 2 + 8, points),
            store(bands, 2, planes, half // 2, points),
            pltpu.SMEM(rotations.shape, F32),
            pltpu.SMEM(mlp_in.shape, F32),
            pltpu.SMEM(mlp_out.shape, F32),
        ] + [pltpu.VMEM(t.shape, t.dtype) for t in tables] + [
            store(bands, 2, planes, half + 8, points),
            store(planes, points, points),
            store(planes, points, points),
            store(planes, points, points),
            store(2, bands, slots, half, points),
            store(bands, planes, half, points),
            store(iters + 1, bands, slots, half, points),
            store(slots, half, points),
            store(slots, half, points),
            store(stages, n, slots, planes, points),
            store(stages, n, slots, planes, points),
            store(half * planes, points),
            store(half * planes, points),
            store(16 * planes, points),
            store(16 * planes, points),
            store(size, planes, points, 2 * points),
            store(bands, 8, points),
            store(2, bands, 8, points),
            store(1, points),
            store(n, 1, points),
            store(bands, slots, half, points),
            store(bands, planes, half, points),
            store(bands, 8, points),
            store(bands, 8, points),
            store(peers, planes, points, points),
            store(points, share * points),
            store(rows, points),
            store(rows, points),
            store(rows, points),
            store(rows, points),
            store(rows, points),
            store(rows, points),
            store(share, points, points),
            store(share, points, points),
            dma((4 * bands + 6 + len(tables),)),
            dma((bands, planes)),
            dma((2, bands, slots)),
            dma((3,)),
            dma((2, stages)),
            dma((2, stages)),
            dma((2,)),
            dma((bands, slots, 2)),
            dma((bands, planes)),
            dma((3,)),
            dma((2, max(peers - 1, 1), planes)),
            dma((2, 6)),
            dma((2 + share,)),
            dma((2, max(sub - 1, 1), share)),
        ],
        compiler_params=pltpu.CompilerParams(
            collective_id=0, has_side_effects=True, vmem_limit_bytes=60 * 2**20
        ),
    )(coefficients, potential, external, core_density, rotations, mlp_in, mlp_out, *tables)

    return pl.pallas_call(
        functools.partial(spread, bands),
        out_shape=(
            jax.ShapeDtypeStruct((bands, 2, planes, points, points), F32),
            jax.ShapeDtypeStruct((planes, points, points), F32),
        ),
        in_specs=[any_space] * 3,
        out_specs=(any_space, any_space),
        scratch_shapes=[
            pltpu.VMEM(low.shape, F32),
            pltpu.VMEM(high.shape, F32),
            pltpu.VMEM(new_potential.shape, F32),
            store(2, planes, points - half - 8, points),
            dma((2 * bands + 1,)),
            dma((3 * bands + 1,)),
        ],
        compiler_params=pltpu.CompilerParams(vmem_limit_bytes=60 * 2**20),
    )(low, high, new_potential)


def solution(mesh):
    in_specs = (
        P("band", None, "grid", None, None),
        P("grid", None, None),
        P("grid", None, None),
        P("grid", None, None),
        P(None, "band", None),
        P(),
        P(),
    )
    out_specs = (P("band", None, "grid", None, None), P("grid", None, None))
    return jax.shard_map(body, mesh=mesh, in_specs=in_specs, out_specs=out_specs, check_vma=False)
```

```python
import functools
import math

import jax
import jax.numpy as jnp
import numpy as np
from jax import lax
from jax.experimental import pallas as pl
from jax.experimental.pallas import tpu as pltpu
from jax.sharding import PartitionSpec as P

MESH = pl.DeviceIdType.MESH
F32 = jnp.float32
BF16 = jnp.bfloat16
HIGHEST = lax.Precision.HIGHEST

step_size = 0.2
epsilon = 1e-06
spacing = 0.58
kinetic_scale = 0.5 * (2.0 * math.pi / spacing) ** 2
coulomb_scale = spacing * spacing / math.pi
gradient_scale = 2.0 * math.pi / spacing
reduced_scale = 2.0 * (3.0 * math.pi * math.pi) ** (1.0 / 3.0)
exchange_scale = (3.0 / math.pi) ** (1.0 / 3.0)
level_shift = 2.275


def halves(table):
    table = np.asarray(table, np.float32)
    high = table.astype(BF16)
    low = (table - high.astype(np.float32)).astype(BF16)
    return high, low


def table_for_left(table):
    high, low = halves(table)
    return np.concatenate([high, high, low], 1)


def table_for_right(table):
    high, low = halves(table)
    return np.concatenate([high, high, low], 0)


def split(value):
    high = value.astype(BF16)
    return high, (value - high.astype(F32)).astype(BF16)


def dot(a, b):
    return jnp.dot(a, b, preferred_element_type=F32)


def left(table, value):
    high, low = split(value)
    return dot(table, jnp.concatenate([high, low, high], 0))


def right(value, table):
    high, low = split(value)
    return dot(jnp.concatenate([high, low, high], 1), table)


def full_dot(a, b):
    return jnp.dot(a, b, preferred_element_type=F32, precision=HIGHEST)


class Plan:
    def __init__(self, n, points):
        planes, slots, reach, zone = points // n, points // 2 // n, points // 4, n // 4
        self.points, self.reach, self.planes, self.slots = points, reach, planes, slots
        kept = list(range(reach)) + list(range(points - reach, points))
        edge = points - reach
        holders = list(range(zone)) + list(range(n - zone, n))
        pairs = self.pairs(kept, edge) if slots > 1 else {}
        owned = self.shared_rows(n, pairs, kept, holders) if len(pairs) == n // 2 else None
        if owned is None:
            owned = [None] * n
            for h in holders:
                other = h + zone if h < zone else h - zone
                owned[h] = [(h * planes + i, None) for i in range(slots)]
                owned[other] = [(h * planes + slots + i, None) for i in range(slots)]
        self.owned = owned
        self.base = min(len(rows) for rows in owned)
        self.extra = [d for d in range(n) if len(owned[d]) > self.base]
        if len(self.extra) == n:
            self.base, self.extra = slots, []
        spare = [d * slots + i for d in range(n) for i in range(len(owned[d]), slots)]
        self.mixed, self.order, self.sends = [], [0] * (n * slots), {h: [] for h in holders}
        self.narrow = set()
        for d in range(n):
            for i, (wide, narrow) in enumerate(owned[d]):
                place = d * slots + i
                self.order[place] = wide
                self.sends[wide // planes].append((wide % planes, d, i, 0))
                if narrow is not None:
                    self.narrow.add(narrow)
                    self.sends[narrow // planes].append((narrow % planes, d, i, 1))
                    self.mixed.append((place, spare[len(self.mixed)], wide))
                    self.order[self.mixed[-1][1]] = narrow
                if edge in (wide, narrow):
                    self.home, self.home_slot, self.home_part = d, i, 0 if edge == wide else 1
        self.edge, self.zero = self.order.index(edge), self.order.index(0)

    def freq(self, plane):
        return plane if 2 * plane < self.points else plane - self.points

    def width(self, plane):
        return math.isqrt(self.reach**2 - self.freq(plane) ** 2)

    def pairs(self, kept, edge):
        found, used = {}, {edge}
        for side in (1, -1):
            group = [p for p in kept if (self.freq(p) >= 0) == (side > 0) and p != edge]
            for narrow in sorted(group, key=self.width):
                if narrow in used or 2 * self.width(narrow) >= self.reach - 1:
                    continue
                limit = self.reach - 1 - self.width(narrow)
                fits = [p for p in group if p not in used and p != narrow and self.width(p) <= limit]
                fits = [p for p in fits if self.width(p) > self.width(narrow)]
                if fits:
                    wide = max(fits, key=lambda p: (self.width(p), abs(self.freq(p))))
                    found[wide] = narrow
                    used |= {wide, narrow}
        for wide in sorted(kept, reverse=True):
            mirror = (self.points - wide) % self.points
            if wide not in used and mirror not in used and wide > mirror and mirror in kept:
                if 2 * self.width(wide) < self.reach:
                    found[wide] = mirror
                    used |= {wide, mirror}
        close = [p for p in kept if p not in used and p // self.planes == edge // self.planes]
        close = [p for p in close if self.width(p) <= self.reach - 4]
        if close:
            found[max(close, key=self.width)] = edge
        return found

    def shared_rows(self, n, pairs, kept, holders):
        zone, slots, planes = n // 4, self.slots, self.planes
        taken = set(pairs.values())
        owned = [[] for _ in range(n)]
        for group in (holders[:zone], holders[zone:]):
            waiting = []
            others = []
            for h in group:
                other = h + zone if h < zone else h - zone
                others.append(other)
                rows = [(p, pairs.get(p)) for p in range(h * planes, (h + 1) * planes) if p not in taken]
                rows.sort(key=lambda row: row[1] is None)
                owned[h] = rows[:slots]
                owned[other] = rows[slots : 2 * slots - 1]
                waiting += rows[2 * slots - 1 :]
                if len(owned[h]) < slots:
                    return None
            for other in others:
                while len(owned[other]) < slots - 1 and waiting:
                    owned[other].append(waiting.pop(0))
            if waiting or any(len(owned[other]) != slots - 1 for other in others):
                return None
        return owned


def cell_order(count, share):
    return np.array([o * share + k for k in range(share) for o in range(count)])


def transform_tables(n, points, count, share):
    half = points // 2
    keep = np.arange(half)
    keep = np.where(keep < half // 2, keep, keep - half)
    cell = np.arange(points)

    def waves(freq):
        angle = 2.0 * np.pi * ((freq[:, None] * cell[None, :]) % points) / points
        return np.cos(angle), np.sin(angle)

    cos, sin = waves(keep)
    plane = np.array(Plan(n, points).order)
    cos_x, sin_x = waves(np.where(2 * plane < points, plane, plane - points))
    freq = np.where(2 * cell < points, cell, cell - points)
    slope = gradient_scale * np.where(2 * freq == -points, 0, freq) / points
    cos_all, sin_all = waves(cell)
    derivative = ((cos_all + 1j * sin_all) * slope[None, :] * 1j) @ (cos_all - 1j * sin_all) / points
    derivative = derivative.real
    basis = cos_all + sin_all
    order = cell_order(count, share)
    lefts = np.stack([
        table_for_left(t) for t in (
            np.concatenate([cos.T, sin.T], 1),
            np.concatenate([cos, sin], 0),
            np.concatenate([cos_x.T, sin_x.T], 1),
            np.concatenate([cos_x, sin_x], 0),
            basis[order],
            derivative[order][:, order],
            basis[:, order],
            derivative,
            basis,
        )
    ])
    rights = np.concatenate([table_for_right(basis), table_for_right(derivative.T)], 1)
    z_out = table_for_right(np.block([[cos, sin], [-sin, cos]]))
    z_in = table_for_right(np.block([[cos.T, -sin.T], [sin.T, cos.T]]))
    plain = basis[:, order][None].astype(np.float32)
    return lefts, rights, z_out, z_in, plain


def kernel(
    n, peers, bands, points, iters, hidden,
    coefficients, potential_in, external_in, core_in, rotations_in, mlp_first_in, mlp_second_in,
    lefts_in, rights_in, z_out_in, z_in_in, plain_in,
    low_out, high_out, out,
    low_here, high_here, rotations, mlp_in, mlp_out,
    tables_l, tables_r, table_out, table_in, table_plain, given, potential, external, core, raw, forward, vectors, mask, kinetic,
    sent, got, level_r, level_i, edge_r, edge_i, space_of, fixed_out, fixed_got,
    gram_tile, gram_got, fresh, returned, fixed_new, fixed_back,
    parts, coulomb, staged, arrived, slope_sent, slope_got, wave_sent, wave_got, change, network,
    load_sem, first_send, first_recv, fixed_sem, send_sem, recv_sem, gram_sem, last_send, last_recv, back_sem, dens_sem, field_sem, out_sem,
    share_sem,
):
    me = lax.axis_index("grid")
    band = lax.axis_index("band")
    half = points // 2
    reach = half // 2
    slots = half // n
    planes = points // n
    zone = n // 4
    plan = Plan(n, points)
    base_rows, extra = plan.base, plan.extra
    home, edge = plan.home, plan.edge
    edge_tile, edge_row = edge // 8 * 8, edge % 8
    zero = plan.zero * planes
    sub = math.gcd(peers, planes)
    share = planes // sub
    count = n * sub
    block = share * share
    seat = lax.rem(band, sub)
    team = band - seat
    rank = me * sub + seat
    holder = jnp.logical_or(me < zone, me >= n - zone)

    def one_of(devices):
        found = me == -1
        for d in devices:
            found = jnp.logical_or(found, me == d)
        return found

    def pick(values):
        found = jnp.int32(values[0])
        for d in range(1, n):
            if values[d] != values[0]:
                found = jnp.where(me == d, values[d], found)
        return found

    def at(grid, other=None):
        return {"band": band if other is None else other, "grid": grid}

    def remote(source, target, send, recv, device):
        return pltpu.make_async_remote_copy(
            src_ref=source, dst_ref=target, send_sem=send, recv_sem=recv, device_id=device, device_id_type=MESH
        )

    def drained(ref, sem):
        pltpu.make_async_copy(ref, ref, sem).wait()

    barrier = pltpu.get_barrier_semaphore()

    @pl.loop(1, n)
    def _(i):
        for k in range(sub):
            pl.semaphore_signal(barrier, inc=1, device_id=at(lax.rem(me + i, n), team + k), device_id_type=MESH)

    for k in range(1, sub):
        pl.semaphore_signal(barrier, inc=1, device_id=at(me, team + lax.rem(seat + k, sub)), device_id_type=MESH)

    for i in range(1, peers):
        other = lax.rem(band + i, peers)

        @pl.when(other - lax.rem(other, sub) != team)
        def _():
            pl.semaphore_signal(barrier, inc=1, device_id=at(me, other), device_id_type=MESH)

    loads = []
    for b in range(bands):
        for p in range(2):
            k = 2 * (2 * b + p)
            loads.append(pltpu.make_async_copy(
                coefficients.at[b, p, :, pl.ds(0, reach + 8)], given.at[b, p, :, pl.ds(0, reach + 8)], load_sem.at[k]
            ))
            loads.append(pltpu.make_async_copy(
                coefficients.at[b, p, :, pl.ds(points - reach, reach)],
                given.at[b, p, :, pl.ds(reach + 8, reach)],
                load_sem.at[k + 1],
            ))
    base = 4 * bands
    tables = [
        pltpu.make_async_copy(source, target, load_sem.at[base + 3 + k])
        for k, (source, target) in enumerate((
            (lefts_in, tables_l), (z_out_in, table_out), (z_in_in, table_in), (rights_in, tables_r), (plain_in, table_plain)
        ))
    ]
    late = [
        pltpu.make_async_copy(potential_in, potential, load_sem.at[base]),
        pltpu.make_async_copy(external_in, external, load_sem.at[base + 1]),
        pltpu.make_async_copy(core_in, core, load_sem.at[base + 2]),
        pltpu.make_async_copy(rotations_in, rotations, load_sem.at[base + 3 + len(tables)]),
        pltpu.make_async_copy(mlp_first_in, mlp_in, load_sem.at[base + 4 + len(tables)]),
        pltpu.make_async_copy(mlp_second_in, mlp_out, load_sem.at[base + 5 + len(tables)]),
    ]
    needed = jnp.logical_or(holder, me == zone)

    @pl.when(needed)
    def _():
        for copy in loads:
            copy.start()

    for copy in tables + late:
        copy.start()

    lanes = lax.broadcasted_iota(jnp.int32, (1, points), 1)
    tile_lane = lax.broadcasted_iota(jnp.int32, (8, points), 1)
    tile_row = lax.broadcasted_iota(jnp.int32, (8, points), 0)
    sign = jnp.where(lanes < half, -1.0, 1.0).astype(F32)
    alone = jnp.where(lax.rem(lanes, half) == 0, 1.0, 0.0).astype(F32)

    def quarter_turn(k):
        k = lax.rem(k, 4)
        c = jnp.where(k == 0, 1.0, jnp.where(k == 2, -1.0, 0.0)).astype(F32)
        s = jnp.where(k == 1, 1.0, jnp.where(k == 3, -1.0, 0.0)).astype(F32)
        return c, s

    z_c, z_s = quarter_turn(lanes)
    y_c, y_s = quarter_turn(me * planes + lax.broadcasted_iota(jnp.int32, (planes, 1), 0))

    def turn(value):
        return pltpu.roll(value, half, 1) * sign

    def frequency(place):
        return jnp.where(2 * place < points, place, place - points)

    row = lax.broadcasted_iota(jnp.int32, (half, points), 0)
    gy = jnp.where(row < reach, row, row - half)
    lane = lax.rem(lanes, half)
    lane_far = lax.rem(lane + reach, half)

    def centred(value):
        return jnp.where(value < reach, value, value - half)

    def swap(value):
        return jnp.where(lane < reach, pltpu.roll(value, points - reach, 1), pltpu.roll(value, reach, 1))

    gz, gz_far = centred(lane), centred(lane_far)
    flat, flat_far = gy * gy + gz * gz, gy * gy + gz_far * gz_far
    outer = []
    for x in range(slots):
        rows = [plan.owned[d][x] if x < len(plan.owned[d]) else (None, None) for d in range(n)]
        gx = pick([points if wide is None else plan.freq(wide) for wide, _ in rows])
        gx_far = pick([points if narrow is None else plan.freq(narrow) for _, narrow in rows])
        outer.append(gx * gx + gz * gz > reach * reach)
        squared = jnp.where(outer[x], flat_far + gx_far * gx_far, flat + gx * gx)
        if x == plan.home_slot:
            spot = jnp.logical_and(row == 0, me == home)
            where = jnp.logical_and(outer[x], lane_far < 4) if plan.home_part else lane < 4
            squared = jnp.where(jnp.logical_and(spot, where), reach * reach, squared)
        mask[x] = jnp.where(16 * squared <= points * points, 1.0, 0.0).astype(F32)
        kinetic[x] = kinetic_scale * squared.astype(F32) / (points * points)
    edge_r[...] = jnp.zeros_like(edge_r)
    edge_i[...] = jnp.zeros_like(edge_i)

    @pl.when(needed)
    def _():
        for copy in loads:
            copy.wait()

    def packed(b, x):
        found = []
        for p in range(2):
            found.append(jnp.concatenate([given[b, p, x, 0:reach], given[b, p, x, reach + 8 : half + 8]], 0))
        real, imag = found
        low = jnp.where(lanes < reach, real, pltpu.roll(real, half, 1))
        high = jnp.where(lanes < half + reach, pltpu.roll(imag, half, 1), imag)
        return jnp.where(lanes < half, low, high)

    @pl.when(holder)
    def _():
        for b in range(bands):
            for x in range(planes):
                forward[b, x] = packed(b, x)

    if extra:
        @pl.when(jnp.logical_not(one_of(extra)))
        def _():
            for b in range(bands):
                raw[0, b, base_rows] = jnp.zeros((half, points), F32)

    def lane_to(value, start, target):
        moved = pltpu.roll(value, (target - start) % points, 1)
        return jnp.where(jnp.logical_and(tile_lane == target, tile_row == 0), moved, 0.0)

    @pl.when(me == 0)
    def _():
        for b in range(bands):
            total = None
            for p in range(2):
                z_point = lane_to(given[b, p, 0, 0:8], reach, 2 + half * p)
                y_point = lane_to(given[b, p, 0, reach : reach + 8], 0, 3 + half * p)
                total = z_point + y_point if total is None else total + z_point + y_point
            fixed_out[b] = total

    @pl.when(me == zone)
    def _():
        for b in range(bands):
            fixed_out[b] = lane_to(given[b, 0, 0, 0:8], 0, 1) + lane_to(given[b, 1, 0, 0:8], 0, 1 + half)

    pl.semaphore_wait(barrier, count - 1 + peers - sub)

    def first(b, h, entry):
        x, d, i, part = entry
        target, sem = raw.at[part, b, i], first_recv.at[part, b, i]
        if d == h:
            return pltpu.make_async_copy(forward.at[b, x], target, sem)
        return remote(forward.at[b, x], target, first_send.at[b, x], sem, at(d))

    def distribute(b):
        for h, entries in plan.sends.items():
            @pl.when(me == h)
            def _():
                for entry in sorted(entries, key=lambda e: e[1] == h):
                    first(b, h, entry).start()

    def gather(b):
        for x in range(slots):
            for part in range(2):
                devices = [
                    d for d in range(n) if x < len(plan.owned[d]) and plan.owned[d][x][part] is not None
                ]
                if len(devices) == n:
                    drained(raw.at[part, b, x], first_recv.at[part, b, x])
                elif devices:
                    @pl.when(one_of(devices))
                    def _():
                        drained(raw.at[part, b, x], first_recv.at[part, b, x])

    def merge(b):
        for x in range(slots):
            devices = [d for d in range(n) if x < len(plan.owned[d]) and plan.owned[d][x][1] is not None]
            if devices:
                @pl.when(one_of(devices))
                def _():
                    raw[0, b, x] = jnp.where(outer[x], swap(raw[1, b, x]), raw[0, b, x])

    def fixed(place):
        return remote(fixed_out, fixed_got.at[place], fixed_sem.at[0], fixed_sem.at[1 + place], at(home))

    @pl.when(me == 0)
    def _():
        fixed(0).start()

    @pl.when(me == zone)
    def _():
        fixed(1).start()

    def part_copy(place, target, part):
        rows = pl.ds(0, base_rows) if part == 0 else pl.ds(base_rows, 1)
        return remote(
            sent.at[place, target, rows], got.at[place, me, rows],
            send_sem.at[part, place], recv_sem.at[part, place], at(target),
        )

    def own_copy(place, part):
        rows = pl.ds(0, base_rows) if part == 0 else pl.ds(base_rows, 1)
        return pltpu.make_async_copy(sent.at[place, me, rows], got.at[place, me, rows], recv_sem.at[part, place])

    def is_extra(device):
        return jnp.logical_or(device < zone, device >= n - zone)

    if extra:
        assert extra == list(range(zone)) + list(range(n - zone, n))

    def exchange(place, to_cells):
        @pl.loop(1, n)
        def _(i):
            target = lax.rem(me + i, n)
            part_copy(place, target, 0).start()
            if extra:
                @pl.when(is_extra(me if to_cells else target))
                def _():
                    part_copy(place, target, 1).start()

        own_copy(place, 0).start()
        if extra:
            @pl.when(is_extra(me))
            def _():
                own_copy(place, 1).start()

    def received(place, to_cells):
        drained(got.at[place, pl.ds(0, n), pl.ds(0, base_rows)], recv_sem.at[0, place])
        if extra and to_cells:
            drained(got.at[place, pl.ds(0, len(extra)), base_rows], recv_sem.at[1, place])
        elif extra:
            @pl.when(is_extra(me))
            def _():
                drained(got.at[place, pl.ds(0, n), base_rows], recv_sem.at[1, place])

    def all_sent(place, to_cells):
        drained(sent.at[place, pl.ds(0, n - 1), pl.ds(0, base_rows)], send_sem.at[0, place])
        if extra and to_cells:
            @pl.when(is_extra(me))
            def _():
                drained(sent.at[place, pl.ds(0, n - 1), base_rows], send_sem.at[1, place])
        elif extra:
            @pl.when(is_extra(me))
            def _():
                drained(sent.at[place, pl.ds(0, len(extra) - 1), base_rows], send_sem.at[1, place])

            @pl.when(jnp.logical_not(is_extra(me)))
            def _():
                drained(sent.at[place, pl.ds(0, len(extra)), base_rows], send_sem.at[1, place])

    def outward(value_of, place):
        stacked = []
        for x in range(slots):
            value = value_of(x)
            stacked.append(jnp.concatenate([value, turn(value)], 0))
        full = left(tables_l[0], jnp.concatenate(stacked, 1))
        for x in range(slots):
            sent[place, :, x] = full[:, x * points : (x + 1) * points].reshape(n, planes, points)
        exchange(place, True)

    def space(place, action, order=range(planes)):
        for wide, narrow, plane in plan.mixed:
            value = got[place, wide // slots, wide % slots]
            far = gz * gz + plan.freq(plane) ** 2 > reach * reach
            got[place, narrow // slots, narrow % slots] = swap(jnp.where(far, value, 0.0))
            got[place, wide // slots, wide % slots] = jnp.where(far, 0.0, value)
        levels = right(got[place].reshape(half * planes, points), table_out[...])
        level_r[...] = levels[:, :points]
        level_i[...] = levels[:, points:]
        special = got[place, edge // slots, edge % slots]

        def lane_of(k):
            return jnp.broadcast_to(special[:, k : k + 1], (planes, points))

        minus_r, plus_r, z_r, y_r = [lane_of(k) for k in range(4)]
        minus_i, plus_i, z_i, y_i = [lane_of(half + k) for k in range(4)]
        level_r[edge * planes : (edge + 1) * planes, :] = minus_r + plus_r
        level_i[edge * planes : (edge + 1) * planes, :] = minus_i + plus_i
        level_r[zero : zero + planes, :] += z_r * z_c - z_i * z_s + y_r * y_c - y_i * y_s
        level_i[zero : zero + planes, :] += z_r * z_s + z_i * z_c + y_r * y_s + y_i * y_c
        edge_r[pl.ds(edge_row, planes, stride=8), :] = 2.0 * plus_r
        edge_i[pl.ds(edge_row, planes, stride=8), :] = 2.0 * plus_i

        def without(value, y, extra):
            tile = value[edge_tile : edge_tile + 8] - extra[pl.ds(pl.multiple_of(y * 8, 8), 8), :]
            return jnp.concatenate([value[:edge_tile], tile, value[edge_tile + 8 :]], 0)

        for y in order:
            real = level_r[pl.ds(y, half, stride=planes), :]
            imag = level_i[pl.ds(y, half, stride=planes), :]
            stacked = jnp.concatenate(
                [
                    jnp.concatenate([real, imag], 1),
                    jnp.concatenate([-without(imag, y, edge_i), without(real, y, edge_r)], 1),
                ],
                0,
            )
            action(y, left(tables_l[2], stacked))

    def spectrum(index, place):
        def action(y, wave):
            space_of[index, y] = wave
            field = potential[y]
            product = wave * jnp.concatenate([field, field], 1)
            both = left(tables_l[3], product)
            cos_r, cos_i = both[:half, :points], both[:half, points:]
            sin_r, sin_i = both[half:, :points], both[half:, points:]
            level_r[pl.ds(y, half, stride=planes), :] = cos_r + sin_i
            level_i[pl.ds(y, half, stride=planes), :] = cos_i - sin_r
            edge_r[8 * (planes + y) : 8 * (planes + y) + 8, :] = cos_r[edge_tile : edge_tile + 8] - sin_i[edge_tile : edge_tile + 8]
            edge_i[8 * (planes + y) : 8 * (planes + y) + 8, :] = cos_i[edge_tile : edge_tile + 8] + sin_r[edge_tile : edge_tile + 8]

        space(place, action)
        both = jnp.concatenate([level_r[...], level_i[...]], 1)
        sent[place + bands] = right(both, table_in[...]).reshape(n, slots, planes, points)

        def total(value):
            return jnp.sum(value, 1, keepdims=True)

        plus_r = edge_r[pl.ds(8 * planes + edge_row, planes, stride=8), :]
        plus_i = edge_i[pl.ds(8 * planes + edge_row, planes, stride=8), :]
        zero_r, zero_i = level_r[zero : zero + planes, :], level_i[zero : zero + planes, :]
        line_r, line_i = total(zero_r), total(zero_i)
        found = [
            total(plus_r), total(zero_r * z_c + zero_i * z_s), line_r * y_c + line_i * y_s,
            total(plus_i), total(zero_i * z_c - zero_r * z_s), line_i * y_c - line_r * y_s,
        ]
        special = sent[place + bands, edge // slots, edge % slots] * alone
        for k, value in enumerate(found):
            special = jnp.where(lanes == (k + 1 if k < 3 else half + k - 2), value, special)
        sent[place + bands, edge // slots, edge % slots] = special
        for wide, narrow, plane in plan.mixed:
            far = gz * gz + plan.freq(plane) ** 2 > reach * reach
            value = sent[place + bands, narrow // slots, narrow % slots]
            kept = sent[place + bands, wide // slots, wide % slots]
            sent[place + bands, wide // slots, wide % slots] = jnp.where(far, swap(value), kept)
        exchange(place + bands, False)

    def inward(place):
        columns = [got[place, :, x].reshape(points, points) for x in range(slots)]
        both = left(tables_l[1], jnp.concatenate(columns, 1))
        found = []
        for x in range(slots):
            part = both[:, x * points : (x + 1) * points]
            found.append(part[:half] - turn(part[half:]))
        return found

    grams = {}

    def measure(p):
        for q in range(p + 1):
            u = vectors[p // bands, p % bands].reshape(slots * half, points)
            v = vectors[q // bands, q % bands].reshape(slots * half, points)
            grams[q, p] = jnp.sum(u * v, 0, keepdims=True)

    tables[0].wait()
    for b in range(bands):
        distribute(b)
    for b in range(bands):
        gather(b)
        if b == 0:
            @pl.when(me == home)
            def _():
                fixed(0).wait_recv()
                fixed(1).wait_recv()
                for c in range(bands):
                    fixed_got[0, c] = fixed_got[0, c] + fixed_got[1, c]

        @pl.when(me == home)
        def _():
            clean = jnp.where(tile_row == 0, alone, 1.0)
            tile = raw[plan.home_part, b, plan.home_slot, 0:8, :]
            raw[plan.home_part, b, plan.home_slot, 0:8, :] = tile * clean + fixed_got[0, b]

        merge(b)
        vectors[0, b] = jnp.where(mask[...] > 0.0, raw[0, b], 0.0)
        outward(lambda x: vectors[0, b, x], b)

    late[0].wait()
    late[3].wait()
    tables[1].wait()
    tables[2].wait()
    size = (iters + 1) * bands
    for b in range(bands):
        measure(b)
    for t in range(iters):
        for b in range(bands):
            received(2 * t * bands + b, True)
            spectrum(t * bands + b, 2 * t * bands + b)
        for b in range(bands):
            place = (2 * t + 1) * bands + b
            received(place, False)
            found = inward(place)
            for x in range(slots):
                value = kinetic[x] * vectors[t, b, x] + found[x] * (1.0 / points**3)
                vectors[t + 1, b, x] = jnp.where(mask[x] > 0.0, value, 0.0)
            last = (t + 1) * bands + b == size - 1
            if last:
                measure(size - 1)
                tile = jnp.zeros((1, points), F32)
                keys = sorted(grams)
                for k, key in enumerate(keys):
                    tile = jnp.where(lanes == k, jnp.sum(grams[key], 1, keepdims=True), tile)
                gram_tile[...] = tile

                def gram_copy(target):
                    return remote(gram_tile, gram_got.at[me], gram_sem.at[0], gram_sem.at[1], at(target))

                @pl.loop(1, n)
                def _(i):
                    gram_copy(lax.rem(me + i, n)).start()

                pltpu.make_async_copy(gram_tile, gram_got.at[me], gram_sem.at[1]).start()
            outward(lambda x: vectors[t + 1, b, x], (2 * t + 2) * bands + b)
            if not last:
                measure((t + 1) * bands + b)

    drained(gram_got, gram_sem.at[1])
    sums = jnp.sum(gram_got[...], 0)
    gram = {}
    for k, (p, q) in enumerate(keys):
        gram[p, q] = gram[q, p] = sums[:, k : k + 1]

    def product(u, v):
        total = None
        for p, a in enumerate(u):
            inner = None
            for q, c in enumerate(v):
                if a is not None and c is not None:
                    term = c * gram[p, q]
                    inner = term if inner is None else inner + term
            if inner is not None:
                total = a * inner if total is None else total + a * inner
        return total

    def combine(terms):
        result = []
        for p in range(size):
            value = None
            for scale, u in terms:
                if u[p] is not None:
                    value = scale * u[p] if value is None else value + scale * u[p]
            result.append(value)
        return result

    one = jnp.ones((1, 1), F32)
    current = [[one if p == b else None for p in range(size)] for b in range(bands)]
    for t in range(iters):
        moved = []
        for b in range(bands):
            pushed = [None] * bands + current[b][: size - bands]
            factor = 1.0 + step_size * (product(current[b], pushed) / (product(current[b], current[b]) + epsilon))
            moved.append(combine([(factor, current[b]), (-step_size, pushed)]))
        following = []
        for b in range(bands):
            rotated = combine([(rotations[t, b, c], moved[c]) for c in range(bands)])
            scale = lax.rsqrt(jnp.maximum(product(rotated, rotated), 0.0) + epsilon)
            following.append([None if value is None else scale * value for value in rotated])
        current = following

    for b in range(bands):
        for x in range(slots):
            fresh[b, x] = sum(current[b][p] * vectors[p // bands, p % bands, x] for p in range(size))

    place = 2 * iters * bands
    for b in range(bands - 1):
        received(place + b, True)

        def keep(y, wave):
            space_of[iters * bands + b, y] = wave

        space(place + b, keep)

    for y in range(planes):
        for b in range(bands):
            known = [space_of[p, y] for p in range(size - 1)]
            mixed = [sum(current[b][p] * known[p] for p in range(size - 1)) for b in range(bands)]
        for b in range(bands):
            space_of[b, y] = mixed[b]

    def density_copy(i, y):
        target = lax.rem(band + i, peers)
        return remote(
            parts.at[band, y], parts.at[band, y], dens_sem.at[0, i - 1, y], dens_sem.at[1, i - 1, y], at(me, target)
        )

    received(place + bands - 1, True)

    def density(y, wave):
        total = None
        for b in range(bands):
            value = space_of[b, y] + current[b][size - 1] * wave
            square = value * value
            square = square[:, :points] + square[:, points:]
            total = square if total is None else total + square
        parts[band, y] = total * (2.0 / (bands * peers))
        for i in range(1, peers):
            @pl.when(lax.rem(lax.rem(band + i, peers), sub) == lax.div(y, share))
            def _():
                density_copy(i, y).start()

    turns = [lax.rem(seat + 1 + m // share, sub) * share + m % share for m in range(planes)]
    space(place + bands - 1, density, turns)

    late[2].wait()
    late[1].wait()
    late[4].wait()
    late[5].wait()
    tables[3].wait()
    tables[4].wait()
    for i in range(1, peers):
        for y in range(planes):
            @pl.when(lax.rem(lax.rem(band + i, peers), sub) == y // share)
            def _():
                density_copy(i, y).wait_send()

            @pl.when(seat == y // share)
            def _():
                density_copy(i, y).wait_recv()

    first_plane = seat * share
    whole = []
    for k in range(share):
        total = core[first_plane + k]
        for other in range(peers):
            total = total + parts[other, first_plane + k]
        whole.append(total)
    varying = [value - level_shift for value in whole]

    pieces = 2 if share % 2 == 0 else 1
    piece = block // pieces
    width = share // pieces

    def field_exchange(stage, part, source, target):
        k = stage * pieces + part

        def copy(other, seat_of):
            return remote(
                source.at[pl.ds((other * sub + seat_of) * block + part * piece, piece)],
                target.at[pl.ds(rank * block + part * piece, piece)],
                field_sem.at[0, k],
                field_sem.at[1, k],
                at(other, team + seat_of),
            )

        @pl.loop(1, n)
        def _(i):
            for seat_of in range(sub):
                copy(lax.rem(me + i, n), seat_of).start()

        for i in range(1, sub):
            copy(me, lax.rem(seat + i, sub)).start()

        own = pl.ds(rank * block + part * piece, piece)
        pltpu.make_async_copy(source.at[own], target.at[own], field_sem.at[1, k]).start()

    def field_drained(stage, part, ref):
        drained(ref.at[pl.ds(0, count * piece)], field_sem.at[1, stage * pieces + part])

    level = left(tables_l[8], jnp.concatenate(varying, 1))
    level = jnp.concatenate([level[:, k * points : (k + 1) * points] for k in range(share)], 0)
    level = right(level, tables_r[:, :points])
    for k in range(share):
        staged[pl.ds(k, points, stride=share), :] = level[k * points : (k + 1) * points]
    for part in range(pieces):
        field_exchange(0, part, staged, arrived)

    def returning(b, d, remote_only=False):
        found = []
        for i, planes_of in enumerate(plan.owned[d]):
            for part, plane in enumerate(planes_of):
                if plane is None:
                    continue
                h, x = plane // planes, plane % planes
                if h != d:
                    found.append(remote(
                        fresh.at[b, i], returned.at[b, x], last_send.at[b, i, part], last_recv.at[b, x], at(h)
                    ))
                elif not remote_only:
                    found.append(pltpu.make_async_copy(fresh.at[b, i], returned.at[b, x], last_recv.at[b, x]))
        return found

    def back(target, sem):
        return remote(fixed_new, fixed_back, back_sem.at[sem], back_sem.at[2], at(target))

    for d in range(n):
        @pl.when(me == d)
        def _():
            for b in range(bands):
                for copy in returning(b, d):
                    copy.start()

    @pl.when(me == home)
    def _():
        for b in range(bands):
            tile = fresh[b, plan.home_slot, 0:8, :]
            fixed_new[b] = swap(tile) if plan.home_part else tile
        back(0, 0).start()
        back(zone, 1).start()

    columns = jnp.concatenate(varying, 1)
    change_x = left(tables_l[7], columns)
    change_z = right(jnp.concatenate(varying, 0), tables_r[:, points:])
    for k in range(share):
        cx = change_x[:, k * points : (k + 1) * points]
        cz = change_z[k * points : (k + 1) * points]
        change[k] = cx * cx + cz * cz
    gy_all = frequency(lax.broadcasted_iota(jnp.int32, (points, points), 0))
    gz_all = frequency(lax.broadcasted_iota(jnp.int32, (points, points), 1))
    flat_all = gy_all * gy_all + gz_all * gz_all
    for i in range(share):
        gx = frequency(rank * share + i)
        squared = flat_all + gx * gx
        coulomb[:, i * points : (i + 1) * points] = jnp.where(
            squared > 0, (coulomb_scale / points) / jnp.maximum(squared, 1).astype(F32), 0.0
        )

    def column(ref, i):
        return jnp.concatenate([ref[pl.ds(i * share + k, count, stride=block), :] for k in range(share)], 0)

    def plane_of(ref, k):
        return jnp.concatenate([ref[pl.ds(i * share + k, count, stride=block), :] for i in range(share)], 0)

    def scattered(ref, part, value):
        for j in range(width):
            for k in range(share):
                ref[pl.ds((part * width + j) * share + k, count, stride=block), :] = value[
                    k * count : (k + 1) * count, j * points : (j + 1) * points
                ]

    columns = []
    for part in range(pieces):
        field_drained(0, part, arrived)
        columns.append(jnp.concatenate([column(arrived, part * width + j) for j in range(width)], 1))
        scattered(slope_sent, part, left(tables_l[5], columns[part]))
        field_exchange(1, part, slope_sent, slope_got)
    for part in range(pieces):
        weight = coulomb[:, part * width * points : (part + 1) * width * points]
        scattered(wave_sent, part, left(tables_l[4], weight * full_dot(table_plain[0], columns[part])))
        field_exchange(2, part, wave_sent, wave_got)

    def to_cells(ref):
        value = left(tables_l[6], jnp.concatenate([plane_of(ref, k) for k in range(share)], 1))
        value = jnp.concatenate([value[:, k * points : (k + 1) * points] for k in range(share)], 0)
        return right(value, tables_r[:, :points])

    @pl.when(holder)
    def _():
        for x in range(planes):
            narrow = [p // planes for p in sorted(plan.narrow) if p % planes == x]
            gx = frequency(me * planes + x)
            inside = 16 * (flat + gx * gx) <= points * points
            for b in range(bands):
                drained(returned.at[b, x], last_recv.at[b, x])
                value = returned[b, x]
                if narrow:
                    value = jnp.where(one_of(narrow), swap(value), value)
                value = jnp.where(inside, value, 0.0)
                swapped = pltpu.roll(value, half, 1)
                real = jnp.where(lanes < reach, value, jnp.where(lanes >= points - reach, swapped, 0.0))
                imag = jnp.where(lanes < reach, swapped, jnp.where(lanes >= points - reach, value, 0.0))
                for p, found in enumerate((real, imag)):
                    low_here[b, p, x, 0:reach] = found[:reach]
                    low_here[b, p, x, reach : reach + 8] = jnp.zeros((8, points), F32)
                    high_here[b, p, x] = found[reach:]

    @pl.when(jnp.logical_not(holder))
    def _():
        low_here[...] = jnp.zeros_like(low_here)
        high_here[...] = jnp.zeros_like(high_here)

    @pl.when(me == 0)
    def _():
        back(0, 0).wait_recv()
        for b in range(bands):
            for p in range(2):
                z_point = lane_to(fixed_back[b], 2 + half * p, reach)
                low_here[b, p, 0, 0:8] = low_here[b, p, 0, 0:8] + z_point
                low_here[b, p, 0, reach : reach + 8] = lane_to(fixed_back[b], 3 + half * p, 0)

    @pl.when(me == zone)
    def _():
        back(0, 0).wait_recv()
        for b in range(bands):
            for p in range(2):
                low_here[b, p, 0, 0:8] = lane_to(fixed_back[b], 1 + half * p, 0)

    leaving = [
        pltpu.make_async_copy(low_here, low_out, out_sem.at[0]),
        pltpu.make_async_copy(high_here, high_out, out_sem.at[1]),
    ]
    for copy in leaving:
        copy.start()

    for part in range(pieces):
        field_drained(1, part, slope_got)
    change_y = to_cells(slope_got) * (1.0 / (points * points))
    for k in range(share):
        cy = change_y[k * points : (k + 1) * points]
        gradient = jnp.sqrt(change[k] + cy * cy)
        dens = core[first_plane + k]
        for other in range(peers):
            dens = dens + parts[other, first_plane + k]
        root = jnp.exp(jnp.log(dens) * (1.0 / 3.0))
        root = root - (root * root * root - dens) / (3.0 * root * root)
        reduced = gradient / (reduced_scale * dens * root)
        bounded = reduced / (1.0 + reduced)

        for first_row in range(0, points, points // 2):
            r = root[first_row : first_row + points // 2]
            q = bounded[first_row : first_row + points // 2]

            def unit(h, total):
                return total + mlp_out[h] * jnp.tanh(mlp_in[0, h] * r + mlp_in[1, h] * q + mlp_in[2, h])

            enhance = lax.fori_loop(0, hidden, unit, jnp.ones_like(r), unroll=8)
            rows = pl.ds(first_row, points // 2)
            network[k, rows] = external[first_plane + k, rows] - exchange_scale * r * enhance

    for part in range(pieces):
        field_drained(2, part, wave_got)
    hartree = to_cells(wave_got)

    def shared(i, seat_of, k):
        return remote(
            network.at[k], out.at[seat_of * share + k],
            share_sem.at[0, i - 1, k], share_sem.at[1, i - 1, k], at(me, team + lax.rem(seat + i, sub)),
        )

    for k in range(share):
        network[k] = network[k] + hartree[k * points : (k + 1) * points]
        for i in range(1, sub):
            shared(i, seat, k).start()
        leaving.append(pltpu.make_async_copy(network.at[k], out.at[first_plane + k], out_sem.at[2 + k]))
        leaving[-1].start()

    for h, entries in plan.sends.items():
        @pl.when(me == h)
        def _():
            for b in range(bands):
                for entry in entries:
                    if entry[1] != h:
                        first(b, h, entry).wait_send()

    for d in range(n):
        @pl.when(me == d)
        def _():
            for b in range(bands):
                for copy in returning(b, d, True):
                    copy.wait_send()

    @pl.when(me == 0)
    def _():
        fixed(0).wait_send()

    @pl.when(me == zone)
    def _():
        fixed(1).wait_send()

    @pl.when(me == home)
    def _():
        back(0, 0).wait_send()
        back(zone, 1).wait_send()

    for k in range((2 * iters + 1) * bands):
        all_sent(k, k // bands % 2 == 0)
    drained(gram_got.at[pl.ds(0, n - 1)], gram_sem.at[0])
    for stage, ref in enumerate((staged, slope_sent, wave_sent)):
        for part in range(pieces):
            drained(ref.at[pl.ds(0, (count - 1) * piece)], field_sem.at[0, stage * pieces + part])
    for i in range(1, sub):
        for k in range(share):
            shared(i, seat, k).wait_send()
            shared(i, lax.rem(seat + sub - i, sub), k).wait_recv()
    for copy in leaving:
        copy.wait()


def spread(bands, low, high, field, new, out, low_here, high_here, field_here, zeros, in_sem, out_sem):
    edge, width = low.shape[3], zeros.shape[2]
    arrivals = []
    for b in range(bands):
        arrivals.append(pltpu.make_async_copy(low.at[b], low_here.at[b], in_sem.at[2 * b]))
        arrivals.append(pltpu.make_async_copy(high.at[b], high_here.at[b], in_sem.at[2 * b + 1]))
    arrivals.append(pltpu.make_async_copy(field, field_here, in_sem.at[2 * bands]))
    for copy in arrivals:
        copy.start()
    zeros[...] = jnp.zeros_like(zeros)
    leaving = []
    for b in range(bands):
        leaving.append(pltpu.make_async_copy(zeros, new.at[b, :, :, pl.ds(edge, width)], out_sem.at[3 * b]))
        leaving[-1].start()
    for k, copy in enumerate(arrivals):
        copy.wait()
        b = k // 2
        if b == bands:
            place, source = out, field_here
        elif k % 2 == 0:
            place, source = new.at[b, :, :, pl.ds(0, edge)], low_here.at[b]
        else:
            place, source = new.at[b, :, :, pl.ds(edge + width, high.shape[3])], high_here.at[b]
        leaving.append(pltpu.make_async_copy(source, place, out_sem.at[3 * b + 1 + k % 2 if b < bands else 3 * bands]))
        leaving[-1].start()
    for copy in leaving:
        copy.wait()


def body(coefficients, potential, external, core_density, rotations, mlp_in, mlp_out):
    n, peers = lax.axis_size("grid"), lax.axis_size("band")
    bands, _, planes, points, _ = coefficients.shape
    iters = rotations.shape[0]
    half = points // 2
    slots = half // n
    sub = math.gcd(peers, planes)
    share = planes // sub
    count = n * sub
    rows = count * share * share
    stages = (2 * iters + 1) * bands
    size = (iters + 1) * bands
    lefts, rights, z_out, z_in, plain = transform_tables(n, points, count, share)
    tables = (lefts, rights, z_out, z_in, plain)
    any_space = pl.BlockSpec(memory_space=pl.ANY)
    dma = pltpu.SemaphoreType.DMA

    def store(*shape):
        return pltpu.VMEM(shape, F32)

    low, high, new_potential = pl.pallas_call(
        functools.partial(kernel, n, peers, bands, points, iters, mlp_out.shape[0]),
        out_shape=(
            jax.ShapeDtypeStruct((bands, 2, planes, half // 2 + 8, points), F32),
            jax.ShapeDtypeStruct((bands, 2, planes, half // 2, points), F32),
            jax.ShapeDtypeStruct((planes, points, points), F32),
        ),
        in_specs=[any_space] * (7 + len(tables)),
        out_specs=(any_space, any_space, any_space),
        scratch_shapes=[
            store(bands, 2, planes, half // 2 + 8, points),
            store(bands, 2, planes, half // 2, points),
            pltpu.SMEM(rotations.shape, F32),
            pltpu.SMEM(mlp_in.shape, F32),
            pltpu.SMEM(mlp_out.shape, F32),
        ] + [pltpu.VMEM(t.shape, t.dtype) for t in tables] + [
            store(bands, 2, planes, half + 8, points),
            store(planes, points, points),
            store(planes, points, points),
            store(planes, points, points),
            store(2, bands, slots, half, points),
            store(bands, planes, half, points),
            store(iters + 1, bands, slots, half, points),
            store(slots, half, points),
            store(slots, half, points),
            store(stages, n, slots, planes, points),
            store(stages, n, slots, planes, points),
            store(half * planes, points),
            store(half * planes, points),
            store(16 * planes, points),
            store(16 * planes, points),
            store(size, planes, points, 2 * points),
            store(bands, 8, points),
            store(2, bands, 8, points),
            store(1, points),
            store(n, 1, points),
            store(bands, slots, half, points),
            store(bands, planes, half, points),
            store(bands, 8, points),
            store(bands, 8, points),
            store(peers, planes, points, points),
            store(points, share * points),
            store(rows, points),
            store(rows, points),
            store(rows, points),
            store(rows, points),
            store(rows, points),
            store(rows, points),
            store(share, points, points),
            store(share, points, points),
            dma((4 * bands + 6 + len(tables),)),
            dma((bands, planes)),
            dma((2, bands, slots)),
            dma((3,)),
            dma((2, stages)),
            dma((2, stages)),
            dma((2,)),
            dma((bands, slots, 2)),
            dma((bands, planes)),
            dma((3,)),
            dma((2, max(peers - 1, 1), planes)),
            dma((2, 6)),
            dma((2 + share,)),
            dma((2, max(sub - 1, 1), share)),
        ],
        compiler_params=pltpu.CompilerParams(
            collective_id=0, has_side_effects=True, vmem_limit_bytes=60 * 2**20
        ),
    )(coefficients, potential, external, core_density, rotations, mlp_in, mlp_out, *tables)

    return pl.pallas_call(
        functools.partial(spread, bands),
        out_shape=(
            jax.ShapeDtypeStruct((bands, 2, planes, points, points), F32),
            jax.ShapeDtypeStruct((planes, points, points), F32),
        ),
        in_specs=[any_space] * 3,
        out_specs=(any_space, any_space),
        scratch_shapes=[
            pltpu.VMEM(low.shape, F32),
            pltpu.VMEM(high.shape, F32),
            pltpu.VMEM(new_potential.shape, F32),
            store(2, planes, points - half - 8, points),
            dma((2 * bands + 1,)),
            dma((3 * bands + 1,)),
        ],
        compiler_params=pltpu.CompilerParams(vmem_limit_bytes=60 * 2**20),
    )(low, high, new_potential)


def solution(mesh):
    in_specs = (
        P("band", None, "grid", None, None),
        P("grid", None, None),
        P("grid", None, None),
        P("grid", None, None),
        P(None, "band", None),
        P(),
        P(),
    )
    out_specs = (P("band", None, "grid", None, None), P("grid", None, None))
    return jax.shard_map(body, mesh=mesh, in_specs=in_specs, out_specs=out_specs, check_vma=False)
```

```python
import functools
import math

import jax
import jax.numpy as jnp
import numpy as np
from jax import lax
from jax.experimental import pallas as pl
from jax.experimental.pallas import tpu as pltpu
from jax.sharding import PartitionSpec as P

MESH = pl.DeviceIdType.MESH
F32 = jnp.float32
BF16 = jnp.bfloat16
HIGHEST = lax.Precision.HIGHEST

step_size = 0.2
epsilon = 1e-06
spacing = 0.58
kinetic_scale = 0.5 * (2.0 * math.pi / spacing) ** 2
coulomb_scale = spacing * spacing / math.pi
gradient_scale = 2.0 * math.pi / spacing
reduced_scale = 2.0 * (3.0 * math.pi * math.pi) ** (1.0 / 3.0)
exchange_scale = (3.0 / math.pi) ** (1.0 / 3.0)
level_shift = 2.275


def halves(table):
    table = np.asarray(table, np.float32)
    high = table.astype(BF16)
    low = (table - high.astype(np.float32)).astype(BF16)
    return high, low


def table_for_left(table):
    high, low = halves(table)
    return np.concatenate([high, high, low], 1)


def table_for_right(table):
    high, low = halves(table)
    return np.concatenate([high, high, low], 0)


def split(value):
    high = value.astype(BF16)
    return high, (value - high.astype(F32)).astype(BF16)


def dot(a, b):
    return jnp.dot(a, b, preferred_element_type=F32)


def left(table, value):
    high, low = split(value)
    return dot(table, jnp.concatenate([high, low, high], 0))


def right(value, table):
    high, low = split(value)
    return dot(jnp.concatenate([high, low, high], 1), table)


def full_dot(a, b):
    return jnp.dot(a, b, preferred_element_type=F32, precision=HIGHEST)


class Plan:
    def __init__(self, n, points):
        planes, slots, reach, zone = points // n, points // 2 // n, points // 4, n // 4
        self.points, self.reach, self.planes, self.slots = points, reach, planes, slots
        kept = list(range(reach)) + list(range(points - reach, points))
        edge = points - reach
        holders = list(range(zone)) + list(range(n - zone, n))
        pairs = self.pairs(kept, edge) if slots > 1 else {}
        owned = self.shared_rows(n, pairs, kept, holders) if len(pairs) == n // 2 else None
        if owned is None:
            owned = [None] * n
            for h in holders:
                other = h + zone if h < zone else h - zone
                owned[h] = [(h * planes + i, None) for i in range(slots)]
                owned[other] = [(h * planes + slots + i, None) for i in range(slots)]
        self.owned = owned
        self.base = min(len(rows) for rows in owned)
        self.extra = [d for d in range(n) if len(owned[d]) > self.base]
        if len(self.extra) == n:
            self.base, self.extra = slots, []
        spare = [d * slots + i for d in range(n) for i in range(len(owned[d]), slots)]
        self.mixed, self.order, self.sends = [], [0] * (n * slots), {h: [] for h in holders}
        self.narrow = set()
        for d in range(n):
            for i, (wide, narrow) in enumerate(owned[d]):
                place = d * slots + i
                self.order[place] = wide
                self.sends[wide // planes].append((wide % planes, d, i, 0))
                if narrow is not None:
                    self.narrow.add(narrow)
                    self.sends[narrow // planes].append((narrow % planes, d, i, 1))
                    self.mixed.append((place, spare[len(self.mixed)], wide))
                    self.order[self.mixed[-1][1]] = narrow
                if edge in (wide, narrow):
                    self.home, self.home_slot, self.home_part = d, i, 0 if edge == wide else 1
        self.edge, self.zero = self.order.index(edge), self.order.index(0)

    def freq(self, plane):
        return plane if 2 * plane < self.points else plane - self.points

    def width(self, plane):
        return math.isqrt(self.reach**2 - self.freq(plane) ** 2)

    def pairs(self, kept, edge):
        found, used = {}, {edge}
        for side in (1, -1):
            group = [p for p in kept if (self.freq(p) >= 0) == (side > 0) and p != edge]
            for narrow in sorted(group, key=self.width):
                if narrow in used or 2 * self.width(narrow) >= self.reach - 1:
                    continue
                limit = self.reach - 1 - self.width(narrow)
                fits = [p for p in group if p not in used and p != narrow and self.width(p) <= limit]
                fits = [p for p in fits if self.width(p) > self.width(narrow)]
                if fits:
                    wide = max(fits, key=lambda p: (self.width(p), abs(self.freq(p))))
                    found[wide] = narrow
                    used |= {wide, narrow}
        for wide in sorted(kept, reverse=True):
            mirror = (self.points - wide) % self.points
            if wide not in used and mirror not in used and wide > mirror and mirror in kept:
                if 2 * self.width(wide) < self.reach:
                    found[wide] = mirror
                    used |= {wide, mirror}
        close = [p for p in kept if p not in used and p // self.planes == edge // self.planes]
        close = [p for p in close if self.width(p) <= self.reach - 4]
        if close:
            found[max(close, key=self.width)] = edge
        return found

    def shared_rows(self, n, pairs, kept, holders):
        zone, slots, planes = n // 4, self.slots, self.planes
        taken = set(pairs.values())
        owned = [[] for _ in range(n)]
        for group in (holders[:zone], holders[zone:]):
            waiting = []
            others = []
            for h in group:
                other = h + zone if h < zone else h - zone
                others.append(other)
                rows = [(p, pairs.get(p)) for p in range(h * planes, (h + 1) * planes) if p not in taken]
                rows.sort(key=lambda row: row[1] is None)
                owned[h] = rows[:slots]
                owned[other] = rows[slots : 2 * slots - 1]
                waiting += rows[2 * slots - 1 :]
                if len(owned[h]) < slots:
                    return None
            for other in others:
                while len(owned[other]) < slots - 1 and waiting:
                    owned[other].append(waiting.pop(0))
            if waiting or any(len(owned[other]) != slots - 1 for other in others):
                return None
        return owned


def cell_order(count, share):
    return np.array([o * share + k for k in range(share) for o in range(count)])


def transform_tables(n, points, count, share):
    half = points // 2
    keep = np.arange(half)
    keep = np.where(keep < half // 2, keep, keep - half)
    cell = np.arange(points)

    def waves(freq):
        angle = 2.0 * np.pi * ((freq[:, None] * cell[None, :]) % points) / points
        return np.cos(angle), np.sin(angle)

    cos, sin = waves(keep)
    plane = np.array(Plan(n, points).order)
    cos_x, sin_x = waves(np.where(2 * plane < points, plane, plane - points))
    freq = np.where(2 * cell < points, cell, cell - points)
    slope = gradient_scale * np.where(2 * freq == -points, 0, freq) / points
    cos_all, sin_all = waves(cell)
    derivative = ((cos_all + 1j * sin_all) * slope[None, :] * 1j) @ (cos_all - 1j * sin_all) / points
    derivative = derivative.real
    basis = cos_all + sin_all
    order = cell_order(count, share)
    lefts = np.stack([
        table_for_left(t) for t in (
            np.concatenate([cos.T, sin.T], 1),
            np.concatenate([cos, sin], 0),
            np.concatenate([cos_x.T, sin_x.T], 1),
            np.concatenate([cos_x, sin_x], 0),
            basis[order],
            derivative[order][:, order],
            basis[:, order],
            derivative,
            basis,
        )
    ])
    rights = np.concatenate([table_for_right(basis), table_for_right(derivative.T)], 1)
    z_out = table_for_right(np.block([[cos, sin], [-sin, cos]]))
    z_in = table_for_right(np.block([[cos.T, -sin.T], [sin.T, cos.T]]))
    plain = basis[:, order][None].astype(np.float32)
    return lefts, rights, z_out, z_in, plain


def kernel(
    n, peers, bands, points, iters, hidden,
    coefficients, potential_in, external_in, core_in, rotations_in, mlp_first_in, mlp_second_in,
    lefts_in, rights_in, z_out_in, z_in_in, plain_in,
    low_out, high_out, out,
    low_here, high_here, rotations, mlp_in, mlp_out,
    tables_l, tables_r, table_out, table_in, table_plain, given, potential, external, core, raw, forward, vectors, mask, kinetic,
    sent, got, level_r, level_i, edge_r, edge_i, space_of, fixed_out, fixed_got,
    gram_tile, gram_got, fresh, returned, fixed_new, fixed_back,
    parts, coulomb, staged, arrived, slope_sent, slope_got, wave_sent, wave_got, change, network,
    load_sem, first_send, first_recv, fixed_sem, send_sem, recv_sem, gram_sem, last_send, last_recv, back_sem, dens_sem, field_sem, out_sem,
    share_sem,
):
    me = lax.axis_index("grid")
    band = lax.axis_index("band")
    half = points // 2
    reach = half // 2
    slots = half // n
    planes = points // n
    zone = n // 4
    plan = Plan(n, points)
    base_rows, extra = plan.base, plan.extra
    home, edge = plan.home, plan.edge
    edge_tile, edge_row = edge // 8 * 8, edge % 8
    zero = plan.zero * planes
    sub = math.gcd(peers, planes)
    share = planes // sub
    count = n * sub
    block = share * share
    seat = lax.rem(band, sub)
    team = band - seat
    rank = me * sub + seat
    holder = jnp.logical_or(me < zone, me >= n - zone)

    def one_of(devices):
        found = me == -1
        for d in devices:
            found = jnp.logical_or(found, me == d)
        return found

    def pick(values):
        found = jnp.int32(values[0])
        for d in range(1, n):
            if values[d] != values[0]:
                found = jnp.where(me == d, values[d], found)
        return found

    def at(grid, other=None):
        return {"band": band if other is None else other, "grid": grid}

    def remote(source, target, send, recv, device):
        return pltpu.make_async_remote_copy(
            src_ref=source, dst_ref=target, send_sem=send, recv_sem=recv, device_id=device, device_id_type=MESH
        )

    def drained(ref, sem):
        pltpu.make_async_copy(ref, ref, sem).wait()

    barrier = pltpu.get_barrier_semaphore()

    @pl.loop(1, n)
    def _(i):
        for k in range(sub):
            pl.semaphore_signal(barrier, inc=1, device_id=at(lax.rem(me + i, n), team + k), device_id_type=MESH)

    for k in range(1, sub):
        pl.semaphore_signal(barrier, inc=1, device_id=at(me, team + lax.rem(seat + k, sub)), device_id_type=MESH)

    for i in range(1, peers):
        other = lax.rem(band + i, peers)

        @pl.when(other - lax.rem(other, sub) != team)
        def _():
            pl.semaphore_signal(barrier, inc=1, device_id=at(me, other), device_id_type=MESH)

    loads = []
    for b in range(bands):
        for p in range(2):
            k = 2 * (2 * b + p)
            loads.append(pltpu.make_async_copy(
                coefficients.at[b, p, :, pl.ds(0, reach + 8)], given.at[b, p, :, pl.ds(0, reach + 8)], load_sem.at[k]
            ))
            loads.append(pltpu.make_async_copy(
                coefficients.at[b, p, :, pl.ds(points - reach, reach)],
                given.at[b, p, :, pl.ds(reach + 8, reach)],
                load_sem.at[k + 1],
            ))
    base = 4 * bands
    tables = [
        pltpu.make_async_copy(source, target, load_sem.at[base + 3 + k])
        for k, (source, target) in enumerate((
            (lefts_in, tables_l), (z_out_in, table_out), (z_in_in, table_in), (rights_in, tables_r), (plain_in, table_plain)
        ))
    ]
    late = [
        pltpu.make_async_copy(potential_in, potential, load_sem.at[base]),
        pltpu.make_async_copy(external_in, external, load_sem.at[base + 1]),
        pltpu.make_async_copy(core_in, core, load_sem.at[base + 2]),
        pltpu.make_async_copy(rotations_in, rotations, load_sem.at[base + 3 + len(tables)]),
        pltpu.make_async_copy(mlp_first_in, mlp_in, load_sem.at[base + 4 + len(tables)]),
        pltpu.make_async_copy(mlp_second_in, mlp_out, load_sem.at[base + 5 + len(tables)]),
    ]
    needed = jnp.logical_or(holder, me == zone)

    @pl.when(needed)
    def _():
        for copy in loads:
            copy.start()

    for copy in tables + late:
        copy.start()

    lanes = lax.broadcasted_iota(jnp.int32, (1, points), 1)
    tile_lane = lax.broadcasted_iota(jnp.int32, (8, points), 1)
    tile_row = lax.broadcasted_iota(jnp.int32, (8, points), 0)
    sign = jnp.where(lanes < half, -1.0, 1.0).astype(F32)
    alone = jnp.where(lax.rem(lanes, half) == 0, 1.0, 0.0).astype(F32)

    def quarter_turn(k):
        k = lax.rem(k, 4)
        c = jnp.where(k == 0, 1.0, jnp.where(k == 2, -1.0, 0.0)).astype(F32)
        s = jnp.where(k == 1, 1.0, jnp.where(k == 3, -1.0, 0.0)).astype(F32)
        return c, s

    z_c, z_s = quarter_turn(lanes)
    y_c, y_s = quarter_turn(me * planes + lax.broadcasted_iota(jnp.int32, (planes, 1), 0))

    def turn(value):
        return pltpu.roll(value, half, 1) * sign

    def frequency(place):
        return jnp.where(2 * place < points, place, place - points)

    row = lax.broadcasted_iota(jnp.int32, (half, points), 0)
    gy = jnp.where(row < reach, row, row - half)
    lane = lax.rem(lanes, half)
    lane_far = lax.rem(lane + reach, half)

    def centred(value):
        return jnp.where(value < reach, value, value - half)

    def swap(value):
        return jnp.where(lane < reach, pltpu.roll(value, points - reach, 1), pltpu.roll(value, reach, 1))

    gz, gz_far = centred(lane), centred(lane_far)
    flat, flat_far = gy * gy + gz * gz, gy * gy + gz_far * gz_far
    outer = []
    for x in range(slots):
        rows = [plan.owned[d][x] if x < len(plan.owned[d]) else (None, None) for d in range(n)]
        gx = pick([points if wide is None else plan.freq(wide) for wide, _ in rows])
        gx_far = pick([points if narrow is None else plan.freq(narrow) for _, narrow in rows])
        outer.append(gx * gx + gz * gz > reach * reach)
        squared = jnp.where(outer[x], flat_far + gx_far * gx_far, flat + gx * gx)
        if x == plan.home_slot:
            spot = jnp.logical_and(row == 0, me == home)
            where = jnp.logical_and(outer[x], lane_far < 4) if plan.home_part else lane < 4
            squared = jnp.where(jnp.logical_and(spot, where), reach * reach, squared)
        mask[x] = jnp.where(16 * squared <= points * points, 1.0, 0.0).astype(F32)
        kinetic[x] = kinetic_scale * squared.astype(F32) / (points * points)
    edge_r[...] = jnp.zeros_like(edge_r)
    edge_i[...] = jnp.zeros_like(edge_i)

    @pl.when(needed)
    def _():
        for copy in loads:
            copy.wait()

    def packed(b, x):
        found = []
        for p in range(2):
            found.append(jnp.concatenate([given[b, p, x, 0:reach], given[b, p, x, reach + 8 : half + 8]], 0))
        real, imag = found
        low = jnp.where(lanes < reach, real, pltpu.roll(real, half, 1))
        high = jnp.where(lanes < half + reach, pltpu.roll(imag, half, 1), imag)
        return jnp.where(lanes < half, low, high)

    @pl.when(holder)
    def _():
        for b in range(bands):
            for x in range(planes):
                forward[b, x] = packed(b, x)

    if extra:
        @pl.when(jnp.logical_not(one_of(extra)))
        def _():
            for b in range(bands):
                raw[0, b, base_rows] = jnp.zeros((half, points), F32)

    def lane_to(value, start, target):
        moved = pltpu.roll(value, (target - start) % points, 1)
        return jnp.where(jnp.logical_and(tile_lane == target, tile_row == 0), moved, 0.0)

    @pl.when(me == 0)
    def _():
        for b in range(bands):
            total = None
            for p in range(2):
                z_point = lane_to(given[b, p, 0, 0:8], reach, 2 + half * p)
                y_point = lane_to(given[b, p, 0, reach : reach + 8], 0, 3 + half * p)
                total = z_point + y_point if total is None else total + z_point + y_point
            fixed_out[b] = total

    @pl.when(me == zone)
    def _():
        for b in range(bands):
            fixed_out[b] = lane_to(given[b, 0, 0, 0:8], 0, 1) + lane_to(given[b, 1, 0, 0:8], 0, 1 + half)

    pl.semaphore_wait(barrier, count - 1 + peers - sub)

    def first(b, h, entry):
        x, d, i, part = entry
        target, sem = raw.at[part, b, i], first_recv.at[part, b, i]
        if d == h:
            return pltpu.make_async_copy(forward.at[b, x], target, sem)
        return remote(forward.at[b, x], target, first_send.at[b, x], sem, at(d))

    def distribute(b):
        for h, entries in plan.sends.items():
            @pl.when(me == h)
            def _():
                for entry in sorted(entries, key=lambda e: e[1] == h):
                    first(b, h, entry).start()

    def gather(b):
        for x in range(slots):
            for part in range(2):
                devices = [
                    d for d in range(n) if x < len(plan.owned[d]) and plan.owned[d][x][part] is not None
                ]
                if len(devices) == n:
                    drained(raw.at[part, b, x], first_recv.at[part, b, x])
                elif devices:
                    @pl.when(one_of(devices))
                    def _():
                        drained(raw.at[part, b, x], first_recv.at[part, b, x])

    def merge(b):
        for x in range(slots):
            devices = [d for d in range(n) if x < len(plan.owned[d]) and plan.owned[d][x][1] is not None]
            if devices:
                @pl.when(one_of(devices))
                def _():
                    raw[0, b, x] = jnp.where(outer[x], swap(raw[1, b, x]), raw[0, b, x])

    def fixed(place):
        return remote(fixed_out, fixed_got.at[place], fixed_sem.at[0], fixed_sem.at[1 + place], at(home))

    @pl.when(me == 0)
    def _():
        fixed(0).start()

    @pl.when(me == zone)
    def _():
        fixed(1).start()

    def part_copy(place, target, full):
        rows = pl.ds(0, slots if full else base_rows)
        return remote(
            sent.at[place, target, rows], got.at[place, me, rows], send_sem.at[place], recv_sem.at[place], at(target)
        )

    def own_copy(place, full):
        rows = pl.ds(0, slots if full else base_rows)
        return pltpu.make_async_copy(sent.at[place, me, rows], got.at[place, me, rows], recv_sem.at[place])

    def is_extra(device):
        return jnp.logical_or(device < zone, device >= n - zone)

    if extra:
        assert extra == list(range(zone)) + list(range(n - zone, n))

    def either(device, act):
        if not extra:
            act(False)
            return

        @pl.when(is_extra(device))
        def _():
            act(True)

        @pl.when(jnp.logical_not(is_extra(device)))
        def _():
            act(False)

    def exchange(place, to_cells):
        @pl.loop(1, n)
        def _(i):
            target = lax.rem(me + i, n)
            either(me if to_cells else target, lambda full: part_copy(place, target, full).start())

        either(me, lambda full: own_copy(place, full).start())

    total_rows = base_rows * n + len(extra)

    def chunks(count, sem):
        drained(level_r.at[pl.ds(0, count * planes)], sem)

    def received(place, to_cells):
        if to_cells:
            chunks(total_rows, recv_sem.at[place])
        else:
            either(me, lambda full: chunks(n * (base_rows + full), recv_sem.at[place]))

    def all_sent(place, to_cells):
        if to_cells:
            either(me, lambda full: chunks((n - 1) * (base_rows + full), send_sem.at[place]))
        else:
            either(me, lambda full: chunks(total_rows - base_rows - full, send_sem.at[place]))

    def outward(value_of, place):
        stacked = []
        for x in range(slots):
            value = value_of(x)
            stacked.append(jnp.concatenate([value, turn(value)], 0))
        full = left(tables_l[0], jnp.concatenate(stacked, 1))
        for x in range(slots):
            sent[place, :, x] = full[:, x * points : (x + 1) * points].reshape(n, planes, points)
        exchange(place, True)

    def space(place, action, order=range(planes)):
        for wide, narrow, plane in plan.mixed:
            value = got[place, wide // slots, wide % slots]
            far = gz * gz + plan.freq(plane) ** 2 > reach * reach
            got[place, narrow // slots, narrow % slots] = swap(jnp.where(far, value, 0.0))
            got[place, wide // slots, wide % slots] = jnp.where(far, 0.0, value)
        levels = right(got[place].reshape(half * planes, points), table_out[...])
        level_r[...] = levels[:, :points]
        level_i[...] = levels[:, points:]
        special = got[place, edge // slots, edge % slots]

        def lane_of(k):
            return jnp.broadcast_to(special[:, k : k + 1], (planes, points))

        minus_r, plus_r, z_r, y_r = [lane_of(k) for k in range(4)]
        minus_i, plus_i, z_i, y_i = [lane_of(half + k) for k in range(4)]
        level_r[edge * planes : (edge + 1) * planes, :] = minus_r + plus_r
        level_i[edge * planes : (edge + 1) * planes, :] = minus_i + plus_i
        level_r[zero : zero + planes, :] += z_r * z_c - z_i * z_s + y_r * y_c - y_i * y_s
        level_i[zero : zero + planes, :] += z_r * z_s + z_i * z_c + y_r * y_s + y_i * y_c
        edge_r[pl.ds(edge_row, planes, stride=8), :] = 2.0 * plus_r
        edge_i[pl.ds(edge_row, planes, stride=8), :] = 2.0 * plus_i

        def without(value, y, extra):
            tile = value[edge_tile : edge_tile + 8] - extra[pl.ds(pl.multiple_of(y * 8, 8), 8), :]
            return jnp.concatenate([value[:edge_tile], tile, value[edge_tile + 8 :]], 0)

        for y in order:
            real = level_r[pl.ds(y, half, stride=planes), :]
            imag = level_i[pl.ds(y, half, stride=planes), :]
            stacked = jnp.concatenate(
                [
                    jnp.concatenate([real, imag], 1),
                    jnp.concatenate([-without(imag, y, edge_i), without(real, y, edge_r)], 1),
                ],
                0,
            )
            action(y, left(tables_l[2], stacked))

    def spectrum(index, place):
        def action(y, wave):
            space_of[index, y] = wave
            field = potential[y]
            product = wave * jnp.concatenate([field, field], 1)
            both = left(tables_l[3], product)
            cos_r, cos_i = both[:half, :points], both[:half, points:]
            sin_r, sin_i = both[half:, :points], both[half:, points:]
            level_r[pl.ds(y, half, stride=planes), :] = cos_r + sin_i
            level_i[pl.ds(y, half, stride=planes), :] = cos_i - sin_r
            edge_r[8 * (planes + y) : 8 * (planes + y) + 8, :] = cos_r[edge_tile : edge_tile + 8] - sin_i[edge_tile : edge_tile + 8]
            edge_i[8 * (planes + y) : 8 * (planes + y) + 8, :] = cos_i[edge_tile : edge_tile + 8] + sin_r[edge_tile : edge_tile + 8]

        space(place, action)
        both = jnp.concatenate([level_r[...], level_i[...]], 1)
        sent[place + bands] = right(both, table_in[...]).reshape(n, slots, planes, points)

        def total(value):
            return jnp.sum(value, 1, keepdims=True)

        plus_r = edge_r[pl.ds(8 * planes + edge_row, planes, stride=8), :]
        plus_i = edge_i[pl.ds(8 * planes + edge_row, planes, stride=8), :]
        zero_r, zero_i = level_r[zero : zero + planes, :], level_i[zero : zero + planes, :]
        line_r, line_i = total(zero_r), total(zero_i)
        found = [
            total(plus_r), total(zero_r * z_c + zero_i * z_s), line_r * y_c + line_i * y_s,
            total(plus_i), total(zero_i * z_c - zero_r * z_s), line_i * y_c - line_r * y_s,
        ]
        special = sent[place + bands, edge // slots, edge % slots] * alone
        for k, value in enumerate(found):
            special = jnp.where(lanes == (k + 1 if k < 3 else half + k - 2), value, special)
        sent[place + bands, edge // slots, edge % slots] = special
        for wide, narrow, plane in plan.mixed:
            far = gz * gz + plan.freq(plane) ** 2 > reach * reach
            value = sent[place + bands, narrow // slots, narrow % slots]
            kept = sent[place + bands, wide // slots, wide % slots]
            sent[place + bands, wide // slots, wide % slots] = jnp.where(far, swap(value), kept)
        exchange(place + bands, False)

    def inward(place):
        columns = [got[place, :, x].reshape(points, points) for x in range(slots)]
        both = left(tables_l[1], jnp.concatenate(columns, 1))
        found = []
        for x in range(slots):
            part = both[:, x * points : (x + 1) * points]
            found.append(part[:half] - turn(part[half:]))
        return found

    grams = {}

    def measure(p):
        for q in range(p + 1):
            u = vectors[p // bands, p % bands].reshape(slots * half, points)
            v = vectors[q // bands, q % bands].reshape(slots * half, points)
            grams[q, p] = jnp.sum(u * v, 0, keepdims=True)

    tables[0].wait()
    for b in range(bands):
        distribute(b)
    for b in range(bands):
        gather(b)
        if b == 0:
            @pl.when(me == home)
            def _():
                fixed(0).wait_recv()
                fixed(1).wait_recv()
                for c in range(bands):
                    fixed_got[0, c] = fixed_got[0, c] + fixed_got[1, c]

        @pl.when(me == home)
        def _():
            clean = jnp.where(tile_row == 0, alone, 1.0)
            tile = raw[plan.home_part, b, plan.home_slot, 0:8, :]
            raw[plan.home_part, b, plan.home_slot, 0:8, :] = tile * clean + fixed_got[0, b]

        merge(b)
        vectors[0, b] = jnp.where(mask[...] > 0.0, raw[0, b], 0.0)
        outward(lambda x: vectors[0, b, x], b)

    late[0].wait()
    late[3].wait()
    tables[1].wait()
    tables[2].wait()
    size = (iters + 1) * bands
    for b in range(bands):
        measure(b)
    for t in range(iters):
        for b in range(bands):
            received(2 * t * bands + b, True)
            spectrum(t * bands + b, 2 * t * bands + b)
        for b in range(bands):
            place = (2 * t + 1) * bands + b
            received(place, False)
            found = inward(place)
            for x in range(slots):
                value = kinetic[x] * vectors[t, b, x] + found[x] * (1.0 / points**3)
                vectors[t + 1, b, x] = jnp.where(mask[x] > 0.0, value, 0.0)
            last = (t + 1) * bands + b == size - 1
            if last:
                measure(size - 1)
                tile = jnp.zeros((1, points), F32)
                keys = sorted(grams)
                for k, key in enumerate(keys):
                    tile = jnp.where(lanes == k, jnp.sum(grams[key], 1, keepdims=True), tile)
                gram_tile[...] = tile

                def gram_copy(target):
                    return remote(gram_tile, gram_got.at[me], gram_sem.at[0], gram_sem.at[1], at(target))

                @pl.loop(1, n)
                def _(i):
                    gram_copy(lax.rem(me + i, n)).start()

                pltpu.make_async_copy(gram_tile, gram_got.at[me], gram_sem.at[1]).start()
            outward(lambda x: vectors[t + 1, b, x], (2 * t + 2) * bands + b)
            if not last:
                measure((t + 1) * bands + b)

    drained(gram_got, gram_sem.at[1])
    sums = jnp.sum(gram_got[...], 0)
    gram = {}
    for k, (p, q) in enumerate(keys):
        gram[p, q] = gram[q, p] = sums[:, k : k + 1]

    def product(u, v):
        total = None
        for p, a in enumerate(u):
            inner = None
            for q, c in enumerate(v):
                if a is not None and c is not None:
                    term = c * gram[p, q]
                    inner = term if inner is None else inner + term
            if inner is not None:
                total = a * inner if total is None else total + a * inner
        return total

    def combine(terms):
        result = []
        for p in range(size):
            value = None
            for scale, u in terms:
                if u[p] is not None:
                    value = scale * u[p] if value is None else value + scale * u[p]
            result.append(value)
        return result

    one = jnp.ones((1, 1), F32)
    current = [[one if p == b else None for p in range(size)] for b in range(bands)]
    for t in range(iters):
        moved = []
        for b in range(bands):
            pushed = [None] * bands + current[b][: size - bands]
            factor = 1.0 + step_size * (product(current[b], pushed) / (product(current[b], current[b]) + epsilon))
            moved.append(combine([(factor, current[b]), (-step_size, pushed)]))
        following = []
        for b in range(bands):
            rotated = combine([(rotations[t, b, c], moved[c]) for c in range(bands)])
            scale = lax.rsqrt(jnp.maximum(product(rotated, rotated), 0.0) + epsilon)
            following.append([None if value is None else scale * value for value in rotated])
        current = following

    for b in range(bands):
        for x in range(slots):
            fresh[b, x] = sum(current[b][p] * vectors[p // bands, p % bands, x] for p in range(size))

    place = 2 * iters * bands
    for b in range(bands - 1):
        received(place + b, True)

        def keep(y, wave):
            space_of[iters * bands + b, y] = wave

        space(place + b, keep)

    for y in range(planes):
        for b in range(bands):
            known = [space_of[p, y] for p in range(size - 1)]
            mixed = [sum(current[b][p] * known[p] for p in range(size - 1)) for b in range(bands)]
        for b in range(bands):
            space_of[b, y] = mixed[b]

    def density_copy(i, y):
        target = lax.rem(band + i, peers)
        return remote(
            parts.at[band, y], parts.at[band, y], dens_sem.at[0, i - 1, y], dens_sem.at[1, i - 1, y], at(me, target)
        )

    received(place + bands - 1, True)

    def density(y, wave):
        total = None
        for b in range(bands):
            value = space_of[b, y] + current[b][size - 1] * wave
            square = value * value
            square = square[:, :points] + square[:, points:]
            total = square if total is None else total + square
        parts[band, y] = total * (2.0 / (bands * peers))
        for i in range(1, peers):
            @pl.when(lax.rem(lax.rem(band + i, peers), sub) == lax.div(y, share))
            def _():
                density_copy(i, y).start()

    turns = [lax.rem(seat + 1 + m // share, sub) * share + m % share for m in range(planes)]
    space(place + bands - 1, density, turns)

    late[2].wait()
    late[1].wait()
    late[4].wait()
    late[5].wait()
    tables[3].wait()
    tables[4].wait()
    for i in range(1, peers):
        for y in range(planes):
            @pl.when(lax.rem(lax.rem(band + i, peers), sub) == y // share)
            def _():
                density_copy(i, y).wait_send()

            @pl.when(seat == y // share)
            def _():
                density_copy(i, y).wait_recv()

    first_plane = seat * share
    whole = []
    for k in range(share):
        total = core[first_plane + k]
        for other in range(peers):
            total = total + parts[other, first_plane + k]
        whole.append(total)
    varying = [value - level_shift for value in whole]

    pieces = 2 if share % 2 == 0 else 1
    piece = block // pieces
    width = share // pieces

    def field_exchange(stage, part, source, target):
        k = stage * pieces + part

        def copy(other, seat_of):
            return remote(
                source.at[pl.ds((other * sub + seat_of) * block + part * piece, piece)],
                target.at[pl.ds(rank * block + part * piece, piece)],
                field_sem.at[0, k],
                field_sem.at[1, k],
                at(other, team + seat_of),
            )

        @pl.loop(1, n)
        def _(i):
            for seat_of in range(sub):
                copy(lax.rem(me + i, n), seat_of).start()

        for i in range(1, sub):
            copy(me, lax.rem(seat + i, sub)).start()

        own = pl.ds(rank * block + part * piece, piece)
        pltpu.make_async_copy(source.at[own], target.at[own], field_sem.at[1, k]).start()

    def field_drained(stage, part, ref):
        drained(ref.at[pl.ds(0, count * piece)], field_sem.at[1, stage * pieces + part])

    level = left(tables_l[8], jnp.concatenate(varying, 1))
    level = jnp.concatenate([level[:, k * points : (k + 1) * points] for k in range(share)], 0)
    level = right(level, tables_r[:, :points])
    for k in range(share):
        staged[pl.ds(k, points, stride=share), :] = level[k * points : (k + 1) * points]
    for part in range(pieces):
        field_exchange(0, part, staged, arrived)

    def returning(b, d, remote_only=False):
        found = []
        for i, planes_of in enumerate(plan.owned[d]):
            for part, plane in enumerate(planes_of):
                if plane is None:
                    continue
                h, x = plane // planes, plane % planes
                if h != d:
                    found.append(remote(
                        fresh.at[b, i], returned.at[b, x], last_send.at[b, i, part], last_recv.at[b, x], at(h)
                    ))
                elif not remote_only:
                    found.append(pltpu.make_async_copy(fresh.at[b, i], returned.at[b, x], last_recv.at[b, x]))
        return found

    def back(target, sem):
        return remote(fixed_new, fixed_back, back_sem.at[sem], back_sem.at[2], at(target))

    for d in range(n):
        @pl.when(me == d)
        def _():
            for b in range(bands):
                for copy in returning(b, d):
                    copy.start()

    @pl.when(me == home)
    def _():
        for b in range(bands):
            tile = fresh[b, plan.home_slot, 0:8, :]
            fixed_new[b] = swap(tile) if plan.home_part else tile
        back(0, 0).start()
        back(zone, 1).start()

    columns = jnp.concatenate(varying, 1)
    change_x = left(tables_l[7], columns)
    change_z = right(jnp.concatenate(varying, 0), tables_r[:, points:])
    for k in range(share):
        cx = change_x[:, k * points : (k + 1) * points]
        cz = change_z[k * points : (k + 1) * points]
        change[k] = cx * cx + cz * cz
    gy_all = frequency(lax.broadcasted_iota(jnp.int32, (points, points), 0))
    gz_all = frequency(lax.broadcasted_iota(jnp.int32, (points, points), 1))
    flat_all = gy_all * gy_all + gz_all * gz_all
    for i in range(share):
        gx = frequency(rank * share + i)
        squared = flat_all + gx * gx
        coulomb[:, i * points : (i + 1) * points] = jnp.where(
            squared > 0, (coulomb_scale / points) / jnp.maximum(squared, 1).astype(F32), 0.0
        )

    def column(ref, i):
        return jnp.concatenate([ref[pl.ds(i * share + k, count, stride=block), :] for k in range(share)], 0)

    def plane_of(ref, k):
        return jnp.concatenate([ref[pl.ds(i * share + k, count, stride=block), :] for i in range(share)], 0)

    def scattered(ref, part, value):
        for j in range(width):
            for k in range(share):
                ref[pl.ds((part * width + j) * share + k, count, stride=block), :] = value[
                    k * count : (k + 1) * count, j * points : (j + 1) * points
                ]

    columns = []
    for part in range(pieces):
        field_drained(0, part, arrived)
        columns.append(jnp.concatenate([column(arrived, part * width + j) for j in range(width)], 1))
        scattered(slope_sent, part, left(tables_l[5], columns[part]))
        field_exchange(1, part, slope_sent, slope_got)
    for part in range(pieces):
        weight = coulomb[:, part * width * points : (part + 1) * width * points]
        scattered(wave_sent, part, left(tables_l[4], weight * full_dot(table_plain[0], columns[part])))
        field_exchange(2, part, wave_sent, wave_got)

    def to_cells(ref):
        value = left(tables_l[6], jnp.concatenate([plane_of(ref, k) for k in range(share)], 1))
        value = jnp.concatenate([value[:, k * points : (k + 1) * points] for k in range(share)], 0)
        return right(value, tables_r[:, :points])

    @pl.when(holder)
    def _():
        for x in range(planes):
            narrow = [p // planes for p in sorted(plan.narrow) if p % planes == x]
            gx = frequency(me * planes + x)
            inside = 16 * (flat + gx * gx) <= points * points
            for b in range(bands):
                drained(returned.at[b, x], last_recv.at[b, x])
                value = returned[b, x]
                if narrow:
                    value = jnp.where(one_of(narrow), swap(value), value)
                value = jnp.where(inside, value, 0.0)
                swapped = pltpu.roll(value, half, 1)
                real = jnp.where(lanes < reach, value, jnp.where(lanes >= points - reach, swapped, 0.0))
                imag = jnp.where(lanes < reach, swapped, jnp.where(lanes >= points - reach, value, 0.0))
                for p, found in enumerate((real, imag)):
                    low_here[b, p, x, 0:reach] = found[:reach]
                    low_here[b, p, x, reach : reach + 8] = jnp.zeros((8, points), F32)
                    high_here[b, p, x] = found[reach:]

    @pl.when(jnp.logical_not(holder))
    def _():
        low_here[...] = jnp.zeros_like(low_here)
        high_here[...] = jnp.zeros_like(high_here)

    @pl.when(me == 0)
    def _():
        back(0, 0).wait_recv()
        for b in range(bands):
            for p in range(2):
                z_point = lane_to(fixed_back[b], 2 + half * p, reach)
                low_here[b, p, 0, 0:8] = low_here[b, p, 0, 0:8] + z_point
                low_here[b, p, 0, reach : reach + 8] = lane_to(fixed_back[b], 3 + half * p, 0)

    @pl.when(me == zone)
    def _():
        back(0, 0).wait_recv()
        for b in range(bands):
            for p in range(2):
                low_here[b, p, 0, 0:8] = lane_to(fixed_back[b], 1 + half * p, 0)

    leaving = [
        pltpu.make_async_copy(low_here, low_out, out_sem.at[0]),
        pltpu.make_async_copy(high_here, high_out, out_sem.at[1]),
    ]
    for copy in leaving:
        copy.start()

    for part in range(pieces):
        field_drained(1, part, slope_got)
    change_y = to_cells(slope_got) * (1.0 / (points * points))
    for k in range(share):
        cy = change_y[k * points : (k + 1) * points]
        gradient = jnp.sqrt(change[k] + cy * cy)
        dens = core[first_plane + k]
        for other in range(peers):
            dens = dens + parts[other, first_plane + k]
        root = jnp.exp(jnp.log(dens) * (1.0 / 3.0))
        root = root - (root * root * root - dens) / (3.0 * root * root)
        reduced = gradient / (reduced_scale * dens * root)
        bounded = reduced / (1.0 + reduced)

        for first_row in range(0, points, points // 2):
            r = root[first_row : first_row + points // 2]
            q = bounded[first_row : first_row + points // 2]

            def unit(h, total):
                return total + mlp_out[h] * jnp.tanh(mlp_in[0, h] * r + mlp_in[1, h] * q + mlp_in[2, h])

            enhance = lax.fori_loop(0, hidden, unit, jnp.ones_like(r), unroll=8)
            rows = pl.ds(first_row, points // 2)
            network[k, rows] = external[first_plane + k, rows] - exchange_scale * r * enhance

    for part in range(pieces):
        field_drained(2, part, wave_got)
    hartree = to_cells(wave_got)

    def shared(i, seat_of, k):
        return remote(
            network.at[k], out.at[seat_of * share + k],
            share_sem.at[0, i - 1, k], share_sem.at[1, i - 1, k], at(me, team + lax.rem(seat + i, sub)),
        )

    for k in range(share):
        network[k] = network[k] + hartree[k * points : (k + 1) * points]
        for i in range(1, sub):
            shared(i, seat, k).start()
        leaving.append(pltpu.make_async_copy(network.at[k], out.at[first_plane + k], out_sem.at[2 + k]))
        leaving[-1].start()

    for h, entries in plan.sends.items():
        @pl.when(me == h)
        def _():
            for b in range(bands):
                for entry in entries:
                    if entry[1] != h:
                        first(b, h, entry).wait_send()

    for d in range(n):
        @pl.when(me == d)
        def _():
            for b in range(bands):
                for copy in returning(b, d, True):
                    copy.wait_send()

    @pl.when(me == 0)
    def _():
        fixed(0).wait_send()

    @pl.when(me == zone)
    def _():
        fixed(1).wait_send()

    @pl.when(me == home)
    def _():
        back(0, 0).wait_send()
        back(zone, 1).wait_send()

    for k in range((2 * iters + 1) * bands):
        all_sent(k, k // bands % 2 == 0)
    drained(gram_got.at[pl.ds(0, n - 1)], gram_sem.at[0])
    for stage, ref in enumerate((staged, slope_sent, wave_sent)):
        for part in range(pieces):
            drained(ref.at[pl.ds(0, (count - 1) * piece)], field_sem.at[0, stage * pieces + part])
    for i in range(1, sub):
        for k in range(share):
            shared(i, seat, k).wait_send()
            shared(i, lax.rem(seat + sub - i, sub), k).wait_recv()
    for copy in leaving:
        copy.wait()


def spread(bands, low, high, field, new, out, low_here, high_here, field_here, zeros, in_sem, out_sem):
    edge, width = low.shape[3], zeros.shape[2]
    arrivals = []
    for b in range(bands):
        arrivals.append(pltpu.make_async_copy(low.at[b], low_here.at[b], in_sem.at[2 * b]))
        arrivals.append(pltpu.make_async_copy(high.at[b], high_here.at[b], in_sem.at[2 * b + 1]))
    arrivals.append(pltpu.make_async_copy(field, field_here, in_sem.at[2 * bands]))
    for copy in arrivals:
        copy.start()
    zeros[...] = jnp.zeros_like(zeros)
    leaving = []
    for b in range(bands):
        leaving.append(pltpu.make_async_copy(zeros, new.at[b, :, :, pl.ds(edge, width)], out_sem.at[3 * b]))
        leaving[-1].start()
    for k, copy in enumerate(arrivals):
        copy.wait()
        b = k // 2
        if b == bands:
            place, source = out, field_here
        elif k % 2 == 0:
            place, source = new.at[b, :, :, pl.ds(0, edge)], low_here.at[b]
        else:
            place, source = new.at[b, :, :, pl.ds(edge + width, high.shape[3])], high_here.at[b]
        leaving.append(pltpu.make_async_copy(source, place, out_sem.at[3 * b + 1 + k % 2 if b < bands else 3 * bands]))
        leaving[-1].start()
    for copy in leaving:
        copy.wait()


def body(coefficients, potential, external, core_density, rotations, mlp_in, mlp_out):
    n, peers = lax.axis_size("grid"), lax.axis_size("band")
    bands, _, planes, points, _ = coefficients.shape
    iters = rotations.shape[0]
    half = points // 2
    slots = half // n
    sub = math.gcd(peers, planes)
    share = planes // sub
    count = n * sub
    rows = count * share * share
    stages = (2 * iters + 1) * bands
    size = (iters + 1) * bands
    lefts, rights, z_out, z_in, plain = transform_tables(n, points, count, share)
    tables = (lefts, rights, z_out, z_in, plain)
    any_space = pl.BlockSpec(memory_space=pl.ANY)
    dma = pltpu.SemaphoreType.DMA

    def store(*shape):
        return pltpu.VMEM(shape, F32)

    low, high, new_potential = pl.pallas_call(
        functools.partial(kernel, n, peers, bands, points, iters, mlp_out.shape[0]),
        out_shape=(
            jax.ShapeDtypeStruct((bands, 2, planes, half // 2 + 8, points), F32),
            jax.ShapeDtypeStruct((bands, 2, planes, half // 2, points), F32),
            jax.ShapeDtypeStruct((planes, points, points), F32),
        ),
        in_specs=[any_space] * (7 + len(tables)),
        out_specs=(any_space, any_space, any_space),
        scratch_shapes=[
            store(bands, 2, planes, half // 2 + 8, points),
            store(bands, 2, planes, half // 2, points),
            pltpu.SMEM(rotations.shape, F32),
            pltpu.SMEM(mlp_in.shape, F32),
            pltpu.SMEM(mlp_out.shape, F32),
        ] + [pltpu.VMEM(t.shape, t.dtype) for t in tables] + [
            store(bands, 2, planes, half + 8, points),
            store(planes, points, points),
            store(planes, points, points),
            store(planes, points, points),
            store(2, bands, slots, half, points),
            store(bands, planes, half, points),
            store(iters + 1, bands, slots, half, points),
            store(slots, half, points),
            store(slots, half, points),
            store(stages, n, slots, planes, points),
            store(stages, n, slots, planes, points),
            store(half * planes, points),
            store(half * planes, points),
            store(16 * planes, points),
            store(16 * planes, points),
            store(size, planes, points, 2 * points),
            store(bands, 8, points),
            store(2, bands, 8, points),
            store(1, points),
            store(n, 1, points),
            store(bands, slots, half, points),
            store(bands, planes, half, points),
            store(bands, 8, points),
            store(bands, 8, points),
            store(peers, planes, points, points),
            store(points, share * points),
            store(rows, points),
            store(rows, points),
            store(rows, points),
            store(rows, points),
            store(rows, points),
            store(rows, points),
            store(share, points, points),
            store(share, points, points),
            dma((4 * bands + 6 + len(tables),)),
            dma((bands, planes)),
            dma((2, bands, slots)),
            dma((3,)),
            dma((stages,)),
            dma((stages,)),
            dma((2,)),
            dma((bands, slots, 2)),
            dma((bands, planes)),
            dma((3,)),
            dma((2, max(peers - 1, 1), planes)),
            dma((2, 6)),
            dma((2 + share,)),
            dma((2, max(sub - 1, 1), share)),
        ],
        compiler_params=pltpu.CompilerParams(
            collective_id=0, has_side_effects=True, vmem_limit_bytes=60 * 2**20
        ),
    )(coefficients, potential, external, core_density, rotations, mlp_in, mlp_out, *tables)

    return pl.pallas_call(
        functools.partial(spread, bands),
        out_shape=(
            jax.ShapeDtypeStruct((bands, 2, planes, points, points), F32),
            jax.ShapeDtypeStruct((planes, points, points), F32),
        ),
        in_specs=[any_space] * 3,
        out_specs=(any_space, any_space),
        scratch_shapes=[
            pltpu.VMEM(low.shape, F32),
            pltpu.VMEM(high.shape, F32),
            pltpu.VMEM(new_potential.shape, F32),
            store(2, planes, points - half - 8, points),
            dma((2 * bands + 1,)),
            dma((3 * bands + 1,)),
        ],
        compiler_params=pltpu.CompilerParams(vmem_limit_bytes=60 * 2**20),
    )(low, high, new_potential)


def solution(mesh):
    in_specs = (
        P("band", None, "grid", None, None),
        P("grid", None, None),
        P("grid", None, None),
        P("grid", None, None),
        P(None, "band", None),
        P(),
        P(),
    )
    out_specs = (P("band", None, "grid", None, None), P("grid", None, None))
    return jax.shard_map(body, mesh=mesh, in_specs=in_specs, out_specs=out_specs, check_vma=False)
```
